32 devices in a mesh: dp: 8 (over z, y), ctx: 4 (over x, core).
Axes of the slice: x: 2, y: 2, z: 4, core: 2. Of those that a mesh axis runs over, the one named last changes fastest.
Arguments:
- projected: bfloat16 [8, 512, 3, 4096], P('dp', 'ctx'), may hold values from -6 to 6
- short_taps: float32 [3, 3, 4096], P(None, None, 'ctx'), may hold values from -3 to 3
- long_filter: bfloat16 [512, 4096], P('dp', 'ctx'), may hold values from -1.1 to 1.1
- skip_gain: float32 [4096], P('ctx'), may hold values from -4 to 4
Outputs:
- mixed: bfloat16 [8, 512, 4096], P('dp', 'ctx')
The draws below stay inside these ranges and needn't reach their ends.
All inputs are finite; a program needn't handle non-finite values.
Results may differ from the reference program's by a relative error of at most 0.012.
Values may be sent and summed in bfloat16 or wider, within the bound.
A program may use at most 64 MiB of HBM per device.

```python
import math
import jax
import jax.numpy as jnp
from jax import lax

D = 4096
KSHORT = 3
SEQ_LEN = 512
SEQS = 8


def draw_long_filter(key, part):
    rate_key, tap_key = jax.random.split(jax.random.fold_in(key, 11))
    rate_low = 0.25 / SEQ_LEN
    rate_high = 1.0 / 30.0
    log_rate = jax.random.uniform(rate_key, (D,), jnp.float32, math.log(rate_low), math.log(rate_high))
    decay_rates = jnp.exp(log_rate)
    positions = jnp.arange(SEQ_LEN, dtype=jnp.float32)[:, None]
    envelope = jnp.exp(-decay_rates[None, :] * positions)
    scale_norm = jnp.sqrt(jnp.expm1(-2.0 * decay_rates) / jnp.expm1(-2.0 * decay_rates * SEQ_LEN))
    tap_noise = jnp.clip(jax.random.normal(tap_key, (SEQ_LEN, D), jnp.float32), -4.0, 4.0)
    return (tap_noise * envelope * scale_norm[None, :]).astype(jnp.bfloat16)


def shard_levels(stream_key, dims, pieces, least, high):
    factor_of = 1.0
    for dim, shards_of in pieces:
        draws = jax.random.uniform(jax.random.fold_in(jax.random.fold_in(stream_key, 6), dim), (shards_of,), jnp.float32, least / len(pieces), high / len(pieces))
        factor_of = factor_of * jnp.repeat(jnp.exp(draws), dims[dim] // shards_of).reshape((-1,) + (1,) * (len(dims) - 1 - dim))
    return factor_of


def gaussian(own_key, shape, spread, limit, pieces=(), kind=jnp.bfloat16):
    gain = shard_levels(own_key, shape, pieces, -0.22, 0.18) if pieces else 1.0
    array = jax.random.normal(own_key, shape, jnp.float32) * spread * gain
    return jnp.minimum(jnp.maximum(array, -limit), limit).astype(kind)


def setup_inputs(seed: int = 0) -> dict:
    keys = jax.random.split(jax.random.key(seed), 5)
    projected = gaussian(keys[0], (SEQS, SEQ_LEN, 3, D), 1.0, 6.0, ((0, 8), (1, 4)))
    short_taps = gaussian(keys[1], (KSHORT, 3, D), 0.6, 3.0, ((2, 4),), jnp.float32)
    long_filter = draw_long_filter(jax.random.fold_in(keys[4], 71), 0)
    skip_gain = gaussian(keys[3], (D,), 1.0, 4.0, ((0, 4),), jnp.float32)
    return {"projected": projected, "short_taps": short_taps, "long_filter": long_filter, "skip_gain": skip_gain}


def reference(projected, short_taps, long_filter, skip_gain):
    kernel_float = long_filter.astype(jnp.float32)
    fft_size = 2 * SEQ_LEN
    kernel_freq = jnp.fft.rfft(kernel_float, n=fft_size, axis=0)

    def per_sequence(sequence):
        widened = sequence.astype(jnp.float32)
        padded = jnp.pad(widened, ((KSHORT - 1, 0), (0, 0), (0, 0)))
        short_conv = jnp.zeros(widened.shape, jnp.float32)
        for tap_index in range(KSHORT):
            offset = KSHORT - 1 - tap_index
            short_conv = short_conv + short_taps[tap_index] * padded[offset:offset + SEQ_LEN]
        queries = short_conv[:, 0].astype(jnp.bfloat16)
        gated_rows = (short_conv[:, 1] * short_conv[:, 2]).astype(jnp.bfloat16)
        gated_float = gated_rows.astype(jnp.float32)
        spectrum = jnp.fft.rfft(gated_float, n=fft_size, axis=0) * kernel_freq
        long_part = jnp.fft.irfft(spectrum, n=fft_size, axis=0)[:SEQ_LEN]
        response = (long_part + skip_gain * gated_float).astype(jnp.bfloat16)
        return (queries.astype(jnp.float32) * response.astype(jnp.float32)).astype(jnp.bfloat16)

    return lax.map(per_sequence, projected)
```

```python
import functools
import math

import jax
import jax.numpy as jnp
import numpy as np
from jax import lax
from jax.experimental import pallas as pl
from jax.experimental.pallas import tpu as pltpu
from jax.sharding import PartitionSpec as P

RADIX = 64


HIGH = lax.Precision.HIGHEST


def causal_short(extended, taps, kernel_size):
    row_count = extended.shape[0] - (kernel_size - 1)
    widened = extended.astype(jnp.float32)
    summed = jnp.zeros((row_count,) + widened.shape[1:], jnp.float32)
    for tap_index in range(kernel_size):
        offset = kernel_size - 1 - tap_index
        summed = summed + taps[tap_index] * widened[offset : offset + row_count]
    return (summed[:, 0].astype(jnp.bfloat16), (summed[:, 1] * summed[:, 2]).astype(jnp.bfloat16))


def dft_tables(length, radix_size):
    outer_size = 2 * length // radix_size
    total_size = outer_size * radix_size
    outer_range = jnp.arange(outer_size, dtype=jnp.int32)
    inner_range = jnp.arange(radix_size, dtype=jnp.int32)
    angle_one = (
        2.0
        * math.pi
        / outer_size
        * (outer_range[:, None] * outer_range[None, :] % outer_size).astype(jnp.float32)
    )
    angle_twist = (
        2.0
        * math.pi
        / total_size
        * (outer_range[:, None] * inner_range[None, :] % total_size).astype(jnp.float32)
    )
    angle_two = (
        2.0
        * math.pi
        / radix_size
        * (inner_range[:, None] * inner_range[None, :] % radix_size).astype(jnp.float32)
    )
    twist_cos = jnp.cos(angle_twist)[:, :, None]
    twist_sin = jnp.sin(angle_twist)[:, :, None]
    return (
        jnp.cos(angle_one),
        jnp.sin(angle_one),
        twist_cos,
        twist_sin,
        jnp.cos(angle_two),
        jnp.sin(angle_two),
    )


def forward_dft(signal, tables, radix_size):
    cos_one, sin_one, twist_cos, twist_sin, cos_two, sin_two = tables
    outer_size = cos_one.shape[0]
    half_size = outer_size // 2
    block_width = signal.shape[1]
    shaped = signal.reshape(half_size, radix_size * block_width)
    first_re = jnp.dot(cos_one[:, :half_size], shaped, precision=HIGH).reshape(
        outer_size, radix_size, block_width
    )
    first_im = -jnp.dot(sin_one[:, :half_size], shaped, precision=HIGH).reshape(
        outer_size, radix_size, block_width
    )
    second_re = first_re * twist_cos + first_im * twist_sin
    second_im = first_im * twist_cos - first_re * twist_sin
    spec_re = jnp.einsum("amc,mb->abc", second_re, cos_two, precision=HIGH) + jnp.einsum(
        "amc,mb->abc", second_im, sin_two, precision=HIGH
    )
    spec_im = jnp.einsum("amc,mb->abc", second_im, cos_two, precision=HIGH) - jnp.einsum(
        "amc,mb->abc", second_re, sin_two, precision=HIGH
    )
    return (spec_re, spec_im)


def inverse_dft(spec_re, spec_im, tables, radix_size):
    cos_one, sin_one, twist_cos, twist_sin, cos_two, sin_two = tables
    outer_size = cos_one.shape[0]
    half_size = outer_size // 2
    block_width = spec_re.shape[2]
    back_re = jnp.einsum("abc,mb->amc", spec_re, cos_two, precision=HIGH) - jnp.einsum(
        "abc,mb->amc", spec_im, sin_two, precision=HIGH
    )
    back_im = jnp.einsum("abc,mb->amc", spec_re, sin_two, precision=HIGH) + jnp.einsum(
        "abc,mb->amc", spec_im, cos_two, precision=HIGH
    )
    turned_re = (back_re * twist_cos - back_im * twist_sin).reshape(
        outer_size, radix_size * block_width
    )
    turned_im = (back_re * twist_sin + back_im * twist_cos).reshape(
        outer_size, radix_size * block_width
    )
    result = jnp.dot(cos_one[:half_size], turned_re, precision=HIGH) - jnp.dot(
        sin_one[:half_size], turned_im, precision=HIGH
    )
    return result.reshape(half_size * radix_size, block_width) / (outer_size * radix_size)


def long_convolve_blocked(gated_slab, filter_slab):
    length, channels = gated_slab.shape
    block_width = min(128, channels)
    tables = dft_tables(length, RADIX)

    def one_block(block_index, output):
        offset = block_index * block_width
        signal = lax.dynamic_slice_in_dim(gated_slab, offset, block_width, 1).astype(jnp.float32)
        kernel_block = lax.dynamic_slice_in_dim(filter_slab, offset, block_width, 1).astype(
            jnp.float32
        )
        sig_re, sig_im = forward_dft(signal, tables, RADIX)
        ker_re, ker_im = forward_dft(kernel_block, tables, RADIX)
        prod_re = sig_re * ker_re - sig_im * ker_im
        prod_im = sig_re * ker_im + sig_im * ker_re
        result = inverse_dft(prod_re, prod_im, tables, RADIX)
        return lax.dynamic_update_slice_in_dim(output, result, offset, 1)

    return lax.fori_loop(
        0, channels // block_width, one_block, jnp.zeros((length, channels), jnp.float32)
    )


def long_convolve(gated_slab, filter_slab):
    length = gated_slab.shape[0]
    if length > 1024:
        return long_convolve_blocked(gated_slab, filter_slab)
    forward, backward = quarter_tables(length)
    sig = jnp.dot(forward, gated_slab, preferred_element_type=jnp.float32)
    ker = jnp.dot(forward, filter_slab, preferred_element_type=jnp.float32)
    sig_cos, sig_sin, ker_cos, ker_sin = sig[:length], sig[length:], ker[:length], ker[length:]
    prod = jnp.concatenate(
        [sig_cos * ker_cos - sig_sin * ker_sin, sig_cos * ker_sin + sig_sin * ker_cos]
    ).astype(jnp.bfloat16)
    return jnp.dot(backward, prod, preferred_element_type=jnp.float32)


def quarter_tables(length):
    steps = (4 * np.arange(length)[:, None] + 1) * np.arange(length)[None, :] % (4 * length)
    angles = steps * (2.0 * math.pi / (4 * length))
    table = np.concatenate([np.cos(angles), np.sin(angles)])
    return (jnp.asarray(table, jnp.bfloat16), jnp.asarray(table.T / length, jnp.bfloat16))


def make_response(gated_slab, filter_slab, skip_gain):
    long_part = long_convolve(gated_slab, filter_slab)
    return (long_part + skip_gain * gated_slab.astype(jnp.float32)).astype(jnp.bfloat16)


def combine_rows(query_part, response_part):
    return (query_part.astype(jnp.float32) * response_part.astype(jnp.float32)).astype(jnp.bfloat16)


def on_device_large(projected, short_taps, long_filter, skip_gain):
    kernel_size = short_taps.shape[0]
    ctx_size = lax.axis_size("ctx")
    rows = projected[0]
    filter_slab = lax.all_gather(long_filter, "dp", axis=0, tiled=True)
    all_taps = lax.all_gather(short_taps, "ctx", axis=2, tiled=True)
    halo = lax.ppermute(
        rows[-(kernel_size - 1) :], "ctx", [(i, i + 1) for i in range(ctx_size - 1)]
    )
    queries, gated = causal_short(jnp.concatenate([halo, rows]), all_taps, kernel_size)
    gated_slab = lax.all_to_all(gated, "ctx", split_axis=1, concat_axis=0, tiled=True)
    response_slab = make_response(gated_slab, filter_slab, skip_gain)
    response = lax.all_to_all(response_slab, "ctx", split_axis=0, concat_axis=1, tiled=True)
    return combine_rows(queries, response)[None]


CHUNK = 256
MESH = pl.DeviceIdType.MESH


def ctx_offsets(ctx_size):
    pairs = [(a, b) for a in range(1, ctx_size // 2) for b in range(2)]
    return pairs + [(0, 1)]


def ctx_peer(me, offset, ctx_size, sign):
    half = ctx_size // 2
    chip = lax.rem(me // 2 + (half + sign * offset[0]) % half, half)
    core = lax.rem(lax.rem(me, 2) + offset[1], 2)
    return chip * 2 + core


def mixer_kernel(
    ctx_size,
    dp_size,
    x_hbm,
    taps_hbm,
    filter_hbm,
    skip_hbm,
    forward_hbm,
    backward_hbm,
    out_ref,
    x_ref,
    tail_ref,
    skip_ref,
    forward_ref,
    backward_ref,
    taps_all,
    halo_out,
    halo_in,
    gated_out,
    gated_slab,
    filter_slab,
    spectrum,
    prod_ref,
    response_slab,
    response_in,
    queries,
    local_sem,
    taps_send,
    taps_recv,
    halo_send,
    halo_recv,
    zfil_send,
    zfil_recv,
    yfil_send,
    yfil_recv,
    gated_send,
    gated_recv,
    resp_send,
    resp_recv,
    filter_sem,
    ready_sem,
):
    kernel_size = taps_hbm.shape[0]
    channels = taps_hbm.shape[2]
    rows = x_ref.shape[1]
    length = rows * ctx_size
    chunks = channels // CHUNK
    fil_rows = filter_hbm.shape[0]
    zsize = dp_size // 2
    turns = range(1, zsize)
    me = lax.axis_index("ctx")
    dp = lax.axis_index("dp")
    zpos, ypos = dp // 2, lax.rem(dp, 2)
    offsets = ctx_offsets(ctx_size)
    peers = range(len(offsets))
    dests = [ctx_peer(me, o, ctx_size, 1) for o in offsets]
    sources = [ctx_peer(me, o, ctx_size, -1) for o in offsets]
    ypeer = zpos * 2 + (1 - ypos)

    def signal(semaphore, **where):
        pl.semaphore_signal(semaphore, inc=1, device_id=where, device_id_type=MESH)

    barrier = pltpu.get_barrier_semaphore()
    for dest in dests:
        signal(barrier, ctx=dest)
    for turn in turns:

        @pl.when(zpos + turn < zsize)
        def _(turn=turn):
            signal(barrier, dp=dp + 2 * turn)

    @pl.when(ypos == 0)
    def _():
        signal(barrier, dp=dp + 1)

    def local_copy(source, target, index):
        copy = pltpu.make_async_copy(source, target, local_sem.at[index])
        copy.start()
        return copy

    own_taps_copy = local_copy(taps_hbm, taps_all.at[me], 0)
    tail_rows = tail_ref.shape[1]
    tail_copy = local_copy(x_hbm.at[:, pl.ds(rows - tail_rows, tail_rows), :], tail_ref, 1)
    x_copies = [local_copy(x_hbm.at[stream], x_ref.at[stream], 2 + stream) for stream in (1, 2, 0)]

    def filter_block(block, chunk):
        return filter_slab.at[
            chunk, pl.ds(pl.multiple_of(block * fil_rows, fil_rows), fil_rows), :
        ]

    def own_filter_copy(chunk):
        columns = pl.ds(pl.multiple_of(chunk * CHUNK, CHUNK), CHUNK)
        return pltpu.make_async_copy(
            filter_hbm.at[:, columns], filter_block(dp, chunk), filter_sem.at[chunk]
        )

    for chunk in range(chunks):
        own_filter_copy(chunk).start()
    table_copies = [
        local_copy(skip_hbm, skip_ref, 5),
        local_copy(forward_hbm, forward_ref, 6),
        local_copy(backward_hbm, backward_ref, 7),
    ]

    own_taps_copy.wait()
    pl.semaphore_wait(barrier, len(dests) + zpos + ypos)

    def taps_copy(i, slot):
        return pltpu.make_async_remote_copy(
            src_ref=taps_all.at[slot],
            dst_ref=taps_all.at[slot],
            send_sem=taps_send.at[i],
            recv_sem=taps_recv.at[i],
            device_id={"ctx": dests[i] if offsets[i][1] == 0 else dests[-1]},
            device_id_type=MESH,
        )

    direct = [i for i, offset in enumerate(offsets) if offset[1] == 0 or offset[0] == 0]
    relayed = [i for i in peers if i not in direct]
    for i in direct:
        taps_copy(i, me).start()

    halo_copy = pltpu.make_async_remote_copy(
        src_ref=halo_out,
        dst_ref=halo_in,
        send_sem=halo_send,
        recv_sem=halo_recv,
        device_id={"ctx": lax.rem(me + 1, ctx_size)},
        device_id_type=MESH,
    )
    tail_copy.wait()
    has_following, has_previous = me < ctx_size - 1, me > 0

    @pl.when(has_following)
    def _():
        halo_out[...] = tail_ref[:, tail_rows - (kernel_size - 1) :, :]
        halo_copy.start()

    for turn in turns:

        @pl.when(zpos >= turn)
        def _(turn=turn):
            signal(ready_sem.at[turn], dp=dp - 2 * turn)

    @pl.when(ypos == 1)
    def _():
        signal(ready_sem.at[0], dp=dp - 1)

    def zfil_copy(turn, chunk):
        target = lax.rem(zpos + turn, zsize)
        return pltpu.make_async_remote_copy(
            src_ref=filter_block(dp, chunk),
            dst_ref=filter_block(dp, chunk),
            send_sem=zfil_send.at[turn - 1, chunk],
            recv_sem=zfil_recv.at[turn - 1, chunk],
            device_id={"dp": target * 2 + ypos},
            device_id_type=MESH,
        )

    def yfil_copy(turn, chunk):
        origin = lax.rem(zpos + zsize - turn, zsize)
        block = origin * 2 + ypos
        return pltpu.make_async_remote_copy(
            src_ref=filter_block(block, chunk),
            dst_ref=filter_block(block, chunk),
            send_sem=yfil_send.at[turn, chunk],
            recv_sem=yfil_recv.at[turn, chunk],
            device_id={"dp": ypeer},
            device_id_type=MESH,
        )

    def relay_filter(chunk):
        for turn in turns:
            zfil_copy(turn, chunk).wait_recv()
            yfil_copy(turn, chunk).start()

    for chunk in range(chunks):
        own_filter_copy(chunk).wait()
    for chunk in range(chunks):
        for turn in turns:

            @pl.when(zpos + turn >= zsize)
            def _(turn=turn, chunk=chunk):
                zfil_copy(turn, chunk).start()

    for i in direct:
        taps_copy(i, sources[i]).wait_recv()
    for i in relayed:
        taps_copy(i, sources[i - 1]).start()
    for copy in x_copies:
        copy.wait()

    @pl.when(has_previous)
    def _():
        halo_copy.wait_recv()

    def short_filter(stream, owner, chunk):
        columns = pl.ds(pl.multiple_of(owner * channels + chunk * CHUNK, CHUNK), CHUNK)
        taps_columns = pl.ds(pl.multiple_of(chunk * CHUNK, CHUNK), CHUNK)
        values = x_ref[stream, :, columns].astype(jnp.float32)
        edge = halo_in[stream, :, columns].astype(jnp.float32)
        edge = jnp.where(has_previous, edge, jnp.zeros_like(edge))
        row_index = lax.broadcasted_iota(jnp.int32, (8, CHUNK), 0)
        total = taps_all[owner, 0, stream : stream + 1, taps_columns] * values
        for tap in range(1, kernel_size):
            moved = pltpu.roll(values, tap, 0)
            top = moved[:8]
            for row in range(tap):
                at = kernel_size - 1 + row - tap
                top = jnp.where(row_index == row, edge[at : at + 1], top)
            moved = jnp.concatenate([top, moved[8:]], axis=0)
            total = total + taps_all[owner, tap, stream : stream + 1, taps_columns] * moved
        return total

    def gated_rows(owner, chunk):
        return (short_filter(1, owner, chunk) * short_filter(2, owner, chunk)).astype(jnp.bfloat16)

    def position_rows(owner):
        return pl.ds(pl.multiple_of(owner * rows, rows), rows)

    def gated_copy(i, chunk, owner):
        return pltpu.make_async_remote_copy(
            src_ref=gated_out.at[i, chunk],
            dst_ref=gated_slab.at[chunk, position_rows(owner), :],
            send_sem=gated_send.at[i, chunk],
            recv_sem=gated_recv.at[i, chunk],
            device_id={"ctx": dests[i]},
            device_id_type=MESH,
        )

    def response_copy(i, chunk):
        return pltpu.make_async_remote_copy(
            src_ref=response_slab.at[chunk, position_rows(dests[i]), :],
            dst_ref=response_in.at[i, chunk],
            send_sem=resp_send.at[i, chunk],
            recv_sem=resp_recv.at[i, chunk],
            device_id={"ctx": dests[i]},
            device_id_type=MESH,
        )

    def push_gated(i, chunk):
        gated_out[i, chunk] = gated_rows(dests[i], chunk)
        gated_copy(i, chunk, me).start()

    def push_chunk(chunk, carry):
        for i in peers:
            push_gated(i, chunk)
        gated_slab[chunk, position_rows(me), :] = gated_rows(me, chunk)
        return carry

    for i in peers:
        if i in relayed:
            taps_copy(i, sources[i]).wait_recv()
        push_gated(i, 0)
    gated_slab[0, position_rows(me), :] = gated_rows(me, 0)

    @pl.when(ypos == 0)
    def _():
        pl.semaphore_wait(ready_sem.at[0], 1)

    for chunk in range(chunks):
        yfil_copy(0, chunk).start()
    early = min(2, chunks)
    lax.fori_loop(1, early, push_chunk, 0)
    for turn in turns:

        @pl.when(zpos + turn < zsize)
        def _(turn=turn):
            pl.semaphore_wait(ready_sem.at[turn], 1)

    for chunk in range(chunks):
        for turn in turns:

            @pl.when(zpos + turn < zsize)
            def _(turn=turn, chunk=chunk):
                zfil_copy(turn, chunk).start()

    lax.fori_loop(early, chunks, push_chunk, 0)

    def fill_queries(chunk, carry):
        def one_owner(owner, inner):
            queries[owner, chunk] = short_filter(0, owner, chunk).astype(jnp.bfloat16)
            return inner

        return lax.fori_loop(0, ctx_size, one_owner, carry)

    lax.fori_loop(0, chunks, fill_queries, 0)
    for chunk in range(early):
        relay_filter(chunk)
    for copy in table_copies:
        copy.wait()

    def mix_into(owner, chunk, response):
        columns = pl.ds(pl.multiple_of(owner * channels + chunk * CHUNK, CHUNK), CHUNK)
        mixed = queries[owner, chunk].astype(jnp.float32) * response.astype(jnp.float32)
        out_ref[:, columns] = mixed.astype(jnp.bfloat16)

    def convolve(chunk, carry):
        columns = pl.ds(pl.multiple_of(chunk * CHUNK, CHUNK), CHUNK)
        for i in peers:
            gated_copy(i, chunk, sources[i]).wait_recv()
        gated = gated_slab[chunk]
        spectrum[...] = jnp.dot(forward_ref[...], gated, preferred_element_type=jnp.float32)
        for turn in range(zsize):
            yfil_copy(turn, chunk).wait_recv()
        taps = filter_slab[chunk]
        ker_cos = jnp.dot(forward_ref[:length], taps, preferred_element_type=jnp.float32)
        ker_sin = jnp.dot(forward_ref[length:], taps, preferred_element_type=jnp.float32)
        sig_cos, sig_sin = spectrum[:length], spectrum[length:]
        prod_ref[:length] = (sig_cos * ker_cos - sig_sin * ker_sin).astype(jnp.bfloat16)
        prod_ref[length:] = (sig_cos * ker_sin + sig_sin * ker_cos).astype(jnp.bfloat16)
        long_part = jnp.dot(backward_ref[...], prod_ref[...], preferred_element_type=jnp.float32)
        direct_part = skip_ref[:, columns] * gated.astype(jnp.float32)
        response_slab[chunk] = (long_part + direct_part).astype(jnp.bfloat16)
        for i in peers:
            response_copy(i, chunk).start()

        @pl.when(chunk + early < chunks)
        def _():
            relay_filter(chunk + early)

        mix_into(me, chunk, response_slab[chunk, position_rows(me), :])
        return carry

    lax.fori_loop(0, chunks, convolve, 0)

    def finish(chunk, carry):
        for i in peers:
            response_copy(i, chunk).wait_recv()
            mix_into(sources[i], chunk, response_in[i, chunk])
        return carry

    lax.fori_loop(0, chunks, finish, 0)

    def drain(chunk, carry):
        for i in peers:
            gated_copy(i, chunk, me).wait_send()
            response_copy(i, chunk).wait_send()
        for turn in turns:
            zfil_copy(turn, chunk).wait_send()
        for turn in range(zsize):
            yfil_copy(turn, chunk).wait_send()
        return carry

    lax.fori_loop(0, chunks, drain, 0)
    for i in peers:
        taps_copy(i, me).wait_send()

    @pl.when(has_following)
    def _():
        halo_copy.wait_send()


def write_kernel(mixed_ref, out_hbm, sem):
    copy = pltpu.make_async_copy(mixed_ref, out_hbm, sem)
    copy.start()
    copy.wait()


def write_out(mixed):
    return pl.pallas_call(
        write_kernel,
        out_shape=jax.ShapeDtypeStruct(mixed.shape, mixed.dtype),
        in_specs=[pl.BlockSpec(memory_space=pltpu.VMEM)],
        out_specs=pl.BlockSpec(memory_space=pltpu.HBM),
        scratch_shapes=[pltpu.SemaphoreType.DMA],
    )(pltpu.with_memory_space_constraint(mixed, pltpu.VMEM))


def on_device(projected, short_taps, long_filter, skip_gain):
    ctx_size, dp_size = lax.axis_size("ctx"), lax.axis_size("dp")
    kernel_size, streams, channels = short_taps.shape
    rows, width = projected.shape[1], projected.shape[3]
    length = rows * ctx_size
    regular = ctx_size % 2 == 0 and dp_size % 2 == 0 and dp_size >= 6 and channels % CHUNK == 0
    if length > 1024 or not regular:
        return on_device_large(projected, short_taps, long_filter, skip_gain)
    forward, backward = quarter_tables(length)
    chunks = channels // CHUNK
    peers = ctx_size - 1
    zsize = dp_size // 2
    hbm_spec = pl.BlockSpec(memory_space=pltpu.HBM)
    dma = pltpu.SemaphoreType.DMA
    operands = (
        projected[0].transpose(1, 0, 2),
        short_taps,
        long_filter,
        skip_gain[None],
        forward,
        backward,
    )
    mixed = pl.pallas_call(
        functools.partial(mixer_kernel, ctx_size, dp_size),
        out_shape=pltpu.VMEM((rows, width), jnp.bfloat16),
        in_specs=[hbm_spec] * len(operands),
        out_specs=pl.BlockSpec(memory_space=pltpu.VMEM),
        scratch_shapes=[
            pltpu.VMEM((streams, rows, width), jnp.bfloat16),
            pltpu.VMEM((streams, 16, width), jnp.bfloat16),
            pltpu.VMEM((1, channels), jnp.float32),
            pltpu.VMEM(forward.shape, jnp.bfloat16),
            pltpu.VMEM(backward.shape, jnp.bfloat16),
            pltpu.VMEM((ctx_size, kernel_size, streams, channels), jnp.float32),
            pltpu.VMEM((streams, kernel_size - 1, width), jnp.bfloat16),
            pltpu.VMEM((streams, kernel_size - 1, width), jnp.bfloat16),
            pltpu.VMEM((peers, chunks, rows, CHUNK), jnp.bfloat16),
            pltpu.VMEM((chunks, length, CHUNK), jnp.bfloat16),
            pltpu.VMEM((chunks, length, CHUNK), jnp.bfloat16),
            pltpu.VMEM((2 * length, CHUNK), jnp.float32),
            pltpu.VMEM((2 * length, CHUNK), jnp.bfloat16),
            pltpu.VMEM((chunks, length, CHUNK), jnp.bfloat16),
            pltpu.VMEM((peers, chunks, rows, CHUNK), jnp.bfloat16),
            pltpu.VMEM((ctx_size, chunks, rows, CHUNK), jnp.bfloat16),
            dma((8,)),
            dma((peers,)),
            dma((peers,)),
            dma,
            dma,
            dma((zsize - 1, chunks)),
            dma((zsize - 1, chunks)),
            dma((zsize, chunks)),
            dma((zsize, chunks)),
            dma((peers, chunks)),
            dma((peers, chunks)),
            dma((peers, chunks)),
            dma((peers, chunks)),
            dma((chunks,)),
            pltpu.SemaphoreType.REGULAR((zsize,)),
        ],
        compiler_params=pltpu.CompilerParams(
            collective_id=0, has_side_effects=True, vmem_limit_bytes=40 * 2**20
        ),
    )(*(pltpu.with_memory_space_constraint(array, pltpu.HBM) for array in operands))
    return write_out(mixed)[None]


def solution(mesh):
    return jax.shard_map(
        on_device,
        mesh=mesh,
        in_specs=(P("dp", "ctx", None, None), P(None, None, "ctx"), P("dp", "ctx"), P("ctx")),
        out_specs=P("dp", "ctx", None),
        check_vma=False,
    )
```

```python
import functools
import math

import jax
import jax.numpy as jnp
import numpy as np
from jax import lax
from jax.experimental import pallas as pl
from jax.experimental.pallas import tpu as pltpu
from jax.sharding import PartitionSpec as P

RADIX = 64


HIGH = lax.Precision.HIGHEST


def causal_short(extended, taps, kernel_size):
    row_count = extended.shape[0] - (kernel_size - 1)
    widened = extended.astype(jnp.float32)
    summed = jnp.zeros((row_count,) + widened.shape[1:], jnp.float32)
    for tap_index in range(kernel_size):
        offset = kernel_size - 1 - tap_index
        summed = summed + taps[tap_index] * widened[offset : offset + row_count]
    return (summed[:, 0].astype(jnp.bfloat16), (summed[:, 1] * summed[:, 2]).astype(jnp.bfloat16))


def dft_tables(length, radix_size):
    outer_size = 2 * length // radix_size
    total_size = outer_size * radix_size
    outer_range = jnp.arange(outer_size, dtype=jnp.int32)
    inner_range = jnp.arange(radix_size, dtype=jnp.int32)
    angle_one = (
        2.0
        * math.pi
        / outer_size
        * (outer_range[:, None] * outer_range[None, :] % outer_size).astype(jnp.float32)
    )
    angle_twist = (
        2.0
        * math.pi
        / total_size
        * (outer_range[:, None] * inner_range[None, :] % total_size).astype(jnp.float32)
    )
    angle_two = (
        2.0
        * math.pi
        / radix_size
        * (inner_range[:, None] * inner_range[None, :] % radix_size).astype(jnp.float32)
    )
    twist_cos = jnp.cos(angle_twist)[:, :, None]
    twist_sin = jnp.sin(angle_twist)[:, :, None]
    return (
        jnp.cos(angle_one),
        jnp.sin(angle_one),
        twist_cos,
        twist_sin,
        jnp.cos(angle_two),
        jnp.sin(angle_two),
    )


def forward_dft(signal, tables, radix_size):
    cos_one, sin_one, twist_cos, twist_sin, cos_two, sin_two = tables
    outer_size = cos_one.shape[0]
    half_size = outer_size // 2
    block_width = signal.shape[1]
    shaped = signal.reshape(half_size, radix_size * block_width)
    first_re = jnp.dot(cos_one[:, :half_size], shaped, precision=HIGH).reshape(
        outer_size, radix_size, block_width
    )
    first_im = -jnp.dot(sin_one[:, :half_size], shaped, precision=HIGH).reshape(
        outer_size, radix_size, block_width
    )
    second_re = first_re * twist_cos + first_im * twist_sin
    second_im = first_im * twist_cos - first_re * twist_sin
    spec_re = jnp.einsum("amc,mb->abc", second_re, cos_two, precision=HIGH) + jnp.einsum(
        "amc,mb->abc", second_im, sin_two, precision=HIGH
    )
    spec_im = jnp.einsum("amc,mb->abc", second_im, cos_two, precision=HIGH) - jnp.einsum(
        "amc,mb->abc", second_re, sin_two, precision=HIGH
    )
    return (spec_re, spec_im)


def inverse_dft(spec_re, spec_im, tables, radix_size):
    cos_one, sin_one, twist_cos, twist_sin, cos_two, sin_two = tables
    outer_size = cos_one.shape[0]
    half_size = outer_size // 2
    block_width = spec_re.shape[2]
    back_re = jnp.einsum("abc,mb->amc", spec_re, cos_two, precision=HIGH) - jnp.einsum(
        "abc,mb->amc", spec_im, sin_two, precision=HIGH
    )
    back_im = jnp.einsum("abc,mb->amc", spec_re, sin_two, precision=HIGH) + jnp.einsum(
        "abc,mb->amc", spec_im, cos_two, precision=HIGH
    )
    turned_re = (back_re * twist_cos - back_im * twist_sin).reshape(
        outer_size, radix_size * block_width
    )
    turned_im = (back_re * twist_sin + back_im * twist_cos).reshape(
        outer_size, radix_size * block_width
    )
    result = jnp.dot(cos_one[:half_size], turned_re, precision=HIGH) - jnp.dot(
        sin_one[:half_size], turned_im, precision=HIGH
    )
    return result.reshape(half_size * radix_size, block_width) / (outer_size * radix_size)


def long_convolve_blocked(gated_slab, filter_slab):
    length, channels = gated_slab.shape
    block_width = min(128, channels)
    tables = dft_tables(length, RADIX)

    def one_block(block_index, output):
        offset = block_index * block_width
        signal = lax.dynamic_slice_in_dim(gated_slab, offset, block_width, 1).astype(jnp.float32)
        kernel_block = lax.dynamic_slice_in_dim(filter_slab, offset, block_width, 1).astype(
            jnp.float32
        )
        sig_re, sig_im = forward_dft(signal, tables, RADIX)
        ker_re, ker_im = forward_dft(kernel_block, tables, RADIX)
        prod_re = sig_re * ker_re - sig_im * ker_im
        prod_im = sig_re * ker_im + sig_im * ker_re
        result = inverse_dft(prod_re, prod_im, tables, RADIX)
        return lax.dynamic_update_slice_in_dim(output, result, offset, 1)

    return lax.fori_loop(
        0, channels // block_width, one_block, jnp.zeros((length, channels), jnp.float32)
    )


def long_convolve(gated_slab, filter_slab):
    length = gated_slab.shape[0]
    if length > 1024:
        return long_convolve_blocked(gated_slab, filter_slab)
    forward, backward = quarter_tables(length)
    sig = jnp.dot(forward, gated_slab, preferred_element_type=jnp.float32)
    ker = jnp.dot(forward, filter_slab, preferred_element_type=jnp.float32)
    sig_cos, sig_sin, ker_cos, ker_sin = sig[:length], sig[length:], ker[:length], ker[length:]
    prod = jnp.concatenate(
        [sig_cos * ker_cos - sig_sin * ker_sin, sig_cos * ker_sin + sig_sin * ker_cos]
    ).astype(jnp.bfloat16)
    return jnp.dot(backward, prod, preferred_element_type=jnp.float32)


def quarter_tables(length):
    steps = (4 * np.arange(length)[:, None] + 1) * np.arange(length)[None, :] % (4 * length)
    angles = steps * (2.0 * math.pi / (4 * length))
    table = np.concatenate([np.cos(angles), np.sin(angles)])
    return (jnp.asarray(table, jnp.bfloat16), jnp.asarray(table.T / length, jnp.bfloat16))


def make_response(gated_slab, filter_slab, skip_gain):
    long_part = long_convolve(gated_slab, filter_slab)
    return (long_part + skip_gain * gated_slab.astype(jnp.float32)).astype(jnp.bfloat16)


def combine_rows(query_part, response_part):
    return (query_part.astype(jnp.float32) * response_part.astype(jnp.float32)).astype(jnp.bfloat16)


def on_device_large(projected, short_taps, long_filter, skip_gain):
    kernel_size = short_taps.shape[0]
    ctx_size = lax.axis_size("ctx")
    rows = projected[0]
    filter_slab = lax.all_gather(long_filter, "dp", axis=0, tiled=True)
    all_taps = lax.all_gather(short_taps, "ctx", axis=2, tiled=True)
    halo = lax.ppermute(
        rows[-(kernel_size - 1) :], "ctx", [(i, i + 1) for i in range(ctx_size - 1)]
    )
    queries, gated = causal_short(jnp.concatenate([halo, rows]), all_taps, kernel_size)
    gated_slab = lax.all_to_all(gated, "ctx", split_axis=1, concat_axis=0, tiled=True)
    response_slab = make_response(gated_slab, filter_slab, skip_gain)
    response = lax.all_to_all(response_slab, "ctx", split_axis=0, concat_axis=1, tiled=True)
    return combine_rows(queries, response)[None]


CHUNK = 256
MESH = pl.DeviceIdType.MESH
ACROSS, DIAGONAL, SIBLING = 0, 1, 2
CROSS = (ACROSS, DIAGONAL)


def ctx_offsets(ctx_size):
    pairs = [(a, b) for a in range(1, ctx_size // 2) for b in range(2)]
    return pairs + [(0, 1)]


def ctx_peer(me, offset, ctx_size, sign):
    half = ctx_size // 2
    chip = lax.rem(me // 2 + (half + sign * offset[0]) % half, half)
    core = lax.rem(lax.rem(me, 2) + offset[1], 2)
    return chip * 2 + core


def mixer_kernel(
    ctx_size,
    dp_size,
    x_hbm,
    taps_hbm,
    filter_hbm,
    skip_hbm,
    forward_hbm,
    backward_hbm,
    out_ref,
    x_ref,
    tail_ref,
    skip_ref,
    forward_ref,
    backward_ref,
    taps_all,
    halo_out,
    halo_in,
    gated_out,
    gated_slab,
    filter_slab,
    spectrum,
    prod_ref,
    response_slab,
    response_in,
    queries,
    local_sem,
    taps_send,
    taps_recv,
    halo_send,
    halo_recv,
    zfil_send,
    zfil_recv,
    yfil_send,
    yfil_recv,
    gated_send,
    gated_recv,
    resp_send,
    resp_recv,
    filter_sem,
    ready_sem,
    shared_send,
    shared_recv,
):
    kernel_size = taps_hbm.shape[0]
    channels = taps_hbm.shape[2]
    rows = x_ref.shape[1]
    length = rows * ctx_size
    chunks = channels // CHUNK
    fil_rows = filter_hbm.shape[0]
    zsize = dp_size // 2
    turns = list(range(1, zsize))
    me = lax.axis_index("ctx")
    dp = lax.axis_index("dp")
    zpos, ypos = dp // 2, lax.rem(dp, 2)
    chip, core = me // 2, lax.rem(me, 2)
    first = 1 - chip
    offsets = ctx_offsets(ctx_size)
    dests = [ctx_peer(me, o, ctx_size, 1) for o in offsets]
    sources = [ctx_peer(me, o, ctx_size, -1) for o in offsets]
    ypeer = zpos * 2 + (1 - ypos)

    def signal(semaphore, **where):
        pl.semaphore_signal(semaphore, inc=1, device_id=where, device_id_type=MESH)

    barrier = pltpu.get_barrier_semaphore()
    for dest in dests:
        signal(barrier, ctx=dest)
    for turn in turns:

        @pl.when(zpos + turn < zsize)
        def _(turn=turn):
            signal(barrier, dp=dp + 2 * turn)

    @pl.when(ypos == 0)
    def _():
        signal(barrier, dp=dp + 1)

    def local_copy(source, target, index):
        copy = pltpu.make_async_copy(source, target, local_sem.at[index])
        copy.start()
        return copy

    own_taps_copy = local_copy(taps_hbm, taps_all.at[me], 0)
    tail_rows = tail_ref.shape[1]
    tail_copy = local_copy(x_hbm.at[:, pl.ds(rows - tail_rows, tail_rows), :], tail_ref, 1)
    gate_copies = [local_copy(x_hbm.at[stream], x_ref.at[stream], 2 + stream) for stream in (1, 2)]

    shared = chunks
    slots = [first + k for k in range(chunks)]

    def filter_block(block, slot):
        return filter_slab.at[slot, pl.ds(pl.multiple_of(block * fil_rows, fil_rows), fil_rows), :]

    def own_filter_copy(chunk):
        slot = shared * first if chunk == 0 else chunk
        return pltpu.make_async_copy(
            filter_hbm.at[:, pl.ds(chunk * CHUNK, CHUNK)],
            filter_block(dp, slot),
            filter_sem.at[chunk],
        )

    for chunk in range(chunks):
        own_filter_copy(chunk).start()
    skip_copy = local_copy(skip_hbm, skip_ref.at[:, pl.ds(0, channels)], 5)
    shared_skip = skip_ref.at[:, pl.ds(channels, CHUNK)]
    shared_skip_copy = pltpu.make_async_copy(
        skip_hbm.at[:, pl.ds(0, CHUNK)], shared_skip, local_sem.at[8]
    )

    @pl.when(chip == 0)
    def _():
        shared_skip_copy.start()

    late_copies = [
        local_copy(x_hbm.at[0], x_ref.at[0], 2),
        local_copy(forward_hbm, forward_ref, 6),
        local_copy(backward_hbm, backward_ref, 7),
        skip_copy,
    ]

    own_taps_copy.wait()
    pl.semaphore_wait(barrier, len(dests) + zpos + ypos)

    def taps_copy(i, slot):
        return pltpu.make_async_remote_copy(
            src_ref=taps_all.at[slot],
            dst_ref=taps_all.at[slot],
            send_sem=taps_send.at[i],
            recv_sem=taps_recv.at[i],
            device_id={"ctx": dests[ACROSS] if i == ACROSS else dests[SIBLING]},
            device_id_type=MESH,
        )

    for i in (ACROSS, SIBLING):
        taps_copy(i, me).start()

    halo_copy = pltpu.make_async_remote_copy(
        src_ref=halo_out,
        dst_ref=halo_in,
        send_sem=halo_send,
        recv_sem=halo_recv,
        device_id={"ctx": lax.rem(me + 1, ctx_size)},
        device_id_type=MESH,
    )
    tail_copy.wait()
    has_following, has_previous = me < ctx_size - 1, me > 0

    @pl.when(has_following)
    def _():
        halo_out[...] = tail_ref[:, tail_rows - (kernel_size - 1) :, :]
        halo_copy.start()

    for turn in turns:

        @pl.when(zpos >= turn)
        def _(turn=turn):
            signal(ready_sem.at[turn], dp=dp - 2 * turn)

    @pl.when(ypos == 1)
    def _():
        signal(ready_sem.at[0], dp=dp - 1)

    def zfil_copy(turn, slot):
        target = lax.rem(zpos + turn, zsize)
        return pltpu.make_async_remote_copy(
            src_ref=filter_block(dp, slot),
            dst_ref=filter_block(dp, slot),
            send_sem=zfil_send.at[turn - 1, slot],
            recv_sem=zfil_recv.at[turn - 1, slot],
            device_id={"dp": target * 2 + ypos},
            device_id_type=MESH,
        )

    def yfil_copy(turn, slot):
        origin = lax.rem(zpos + zsize - turn, zsize)
        block = origin * 2 + ypos
        return pltpu.make_async_remote_copy(
            src_ref=filter_block(block, slot),
            dst_ref=filter_block(block, slot),
            send_sem=yfil_send.at[turn, slot],
            recv_sem=yfil_recv.at[turn, slot],
            device_id={"dp": ypeer},
            device_id_type=MESH,
        )

    def shared_filter_copy():
        return pltpu.make_async_remote_copy(
            src_ref=filter_block(dp, shared),
            dst_ref=filter_block(dp, shared),
            send_sem=shared_send.at[0],
            recv_sem=shared_recv.at[0],
            device_id={"ctx": dests[ACROSS]},
            device_id_type=MESH,
        )

    def shared_skip_send():
        return pltpu.make_async_remote_copy(
            src_ref=shared_skip,
            dst_ref=shared_skip,
            send_sem=shared_send.at[1],
            recv_sem=shared_recv.at[1],
            device_id={"ctx": dests[ACROSS]},
            device_id_type=MESH,
        )

    def relay_filter(slot):
        for turn in turns:
            zfil_copy(turn, slot).wait_recv()
            yfil_copy(turn, slot).start()

    def send_up(turn, slot):
        @pl.when(zpos + turn < zsize)
        def _():
            zfil_copy(turn, slot).start()

    def send_down(turn, slot):
        @pl.when(zpos + turn >= zsize)
        def _():
            zfil_copy(turn, slot).start()

    def wait_up(turn):
        @pl.when(zpos + turn < zsize)
        def _():
            pl.semaphore_wait(ready_sem.at[turn], 1)

    for chunk in range(chunks):
        own_filter_copy(chunk).wait()
    for slot in slots:
        for turn in turns:
            send_down(turn, slot)

    def short_filter(stream, owner, chunk):
        columns = pl.ds(pl.multiple_of(owner * channels + chunk * CHUNK, CHUNK), CHUNK)
        taps_columns = pl.ds(pl.multiple_of(chunk * CHUNK, CHUNK), CHUNK)
        values = x_ref[stream, :, columns].astype(jnp.float32)
        edge = halo_in[stream, :, columns].astype(jnp.float32)
        edge = jnp.where(has_previous, edge, jnp.zeros_like(edge))
        row_index = lax.broadcasted_iota(jnp.int32, (8, CHUNK), 0)
        total = taps_all[owner, 0, stream : stream + 1, taps_columns] * values
        for tap in range(1, kernel_size):
            moved = pltpu.roll(values, tap, 0)
            top = moved[:8]
            for row in range(tap):
                at = kernel_size - 1 + row - tap
                top = jnp.where(row_index == row, edge[at : at + 1], top)
            moved = jnp.concatenate([top, moved[8:]], axis=0)
            total = total + taps_all[owner, tap, stream : stream + 1, taps_columns] * moved
        return total

    def gated_rows(owner, chunk):
        return (short_filter(1, owner, chunk) * short_filter(2, owner, chunk)).astype(jnp.bfloat16)

    def position_rows(owner):
        return pl.ds(pl.multiple_of(owner * rows, rows), rows)

    def gated_copy(i, slot, owner, source=None):
        return pltpu.make_async_remote_copy(
            src_ref=gated_out.at[i, slot] if source is None else source,
            dst_ref=gated_slab.at[slot, position_rows(owner), :],
            send_sem=gated_send.at[i, slot],
            recv_sem=gated_recv.at[i, slot],
            device_id={"ctx": dests[i]},
            device_id_type=MESH,
        )

    def response_copy(i, slot):
        return pltpu.make_async_remote_copy(
            src_ref=response_slab.at[slot, position_rows(dests[i]), :],
            dst_ref=response_in.at[i, slot],
            send_sem=resp_send.at[i, slot],
            recv_sem=resp_recv.at[i, slot],
            device_id={"ctx": dests[i]},
            device_id_type=MESH,
        )

    def push_gated(i, chunk):
        gated_out[i, chunk] = gated_rows(dests[i], chunk)
        gated_copy(i, chunk, me).start()

    def push_near(chunk):
        push_gated(SIBLING, chunk)
        gated_slab[chunk, position_rows(me), :] = gated_rows(me, chunk)

    def shared_own():
        gated_slab[shared, position_rows(me), :] = gated_rows(core, 0)

    def shared_other():
        gated_out[SIBLING, shared] = gated_rows(1 - core, 0)
        gated_copy(SIBLING, shared, me).start()

    taps_copy(SIBLING, sources[SIBLING]).wait_recv()
    for copy in gate_copies:
        copy.wait()

    @pl.when(jnp.logical_and(chip == 0, has_previous))
    def _():
        halo_copy.wait_recv()

    @pl.when(chip == 0)
    def _():
        shared_own()
        gated_copy(ACROSS, shared, me, gated_slab.at[shared, position_rows(me), :]).start()
        shared_other()
        gated_copy(DIAGONAL, shared, me, gated_out.at[SIBLING, shared]).start()
        shared_filter_copy().start()
        shared_skip_copy.wait()
        shared_skip_send().start()
        half = length // 2
        gated_slab[shared, half:] = jnp.zeros((length - half, CHUNK), jnp.bfloat16)

    taps_copy(ACROSS, sources[ACROSS]).wait_recv()
    taps_copy(DIAGONAL, sources[ACROSS]).start()

    @pl.when(chip == 1)
    def _():
        halo_copy.wait_recv()

    push_gated(ACROSS, chip)
    taps_copy(DIAGONAL, sources[DIAGONAL]).wait_recv()
    push_gated(DIAGONAL, chip)

    @pl.when(ypos == 0)
    def _():
        pl.semaphore_wait(ready_sem.at[0], 1)

    for slot in slots:
        yfil_copy(0, slot).start()
    for turn in turns[:-1]:
        wait_up(turn)
    for slot in slots[:2]:
        for turn in turns[:-1]:
            send_up(turn, slot)
    push_near(first)
    wait_up(turns[-1])
    for slot in slots[:2]:
        send_up(turns[-1], slot)
    for slot in slots[2:]:
        for turn in turns:
            send_up(turn, slot)

    def push_chunk(step, carry):
        @pl.when(chip + step < chunks)
        def _():
            push_gated(ACROSS, chip + step)
            push_gated(DIAGONAL, chip + step)

        @pl.when(first + step < chunks)
        def _():
            push_near(first + step)

        return carry

    lax.fori_loop(1, chunks, push_chunk, 0)

    @pl.when(chip == 1)
    def _():
        shared_own()
        shared_other()

    for copy in late_copies:
        copy.wait()

    def fill_queries(chunk, carry):
        def one_owner(owner, inner):
            queries[owner, chunk] = short_filter(0, owner, chunk).astype(jnp.bfloat16)
            return inner

        return lax.fori_loop(0, ctx_size, one_owner, carry)

    relay_filter(first)
    lax.fori_loop(0, chunks // 2, fill_queries, 0)
    relay_filter(first + 1)

    @pl.when(chip == 1)
    def _():
        shared_filter_copy().wait_recv()
        shared_skip_send().wait_recv()
        yfil_copy(0, shared).start()
        for turn in turns:
            zfil_copy(turn, shared).start()

    lax.fori_loop(chunks // 2, chunks, fill_queries, 0)

    def mix_into(owner, chunk, response):
        columns = pl.ds(pl.multiple_of(owner * channels + chunk * CHUNK, CHUNK), CHUNK)
        mixed = queries[owner, chunk].astype(jnp.float32) * response.astype(jnp.float32)
        out_ref[:, columns] = mixed.astype(jnp.bfloat16)

    def convolve(slot, carry):
        columns = pl.ds(pl.multiple_of(slot * CHUNK, CHUNK), CHUNK)

        @pl.when(jnp.logical_or(slot < shared, chip == 1))
        def _():
            for i in CROSS:
                gated_copy(i, slot, sources[i]).wait_recv()

        gated_copy(SIBLING, slot, sources[SIBLING]).wait_recv()
        gated = gated_slab[slot]
        spectrum[...] = jnp.dot(forward_ref[...], gated, preferred_element_type=jnp.float32)
        for turn in range(zsize):
            yfil_copy(turn, slot).wait_recv()
        taps = filter_slab[slot]
        ker_cos = jnp.dot(forward_ref[:length], taps, preferred_element_type=jnp.float32)
        ker_sin = jnp.dot(forward_ref[length:], taps, preferred_element_type=jnp.float32)
        sig_cos, sig_sin = spectrum[:length], spectrum[length:]
        prod_ref[:length] = (sig_cos * ker_cos - sig_sin * ker_sin).astype(jnp.bfloat16)
        prod_ref[length:] = (sig_cos * ker_sin + sig_sin * ker_cos).astype(jnp.bfloat16)
        long_part = jnp.dot(backward_ref[...], prod_ref[...], preferred_element_type=jnp.float32)
        direct_part = skip_ref[:, columns] * gated.astype(jnp.float32)
        response_slab[slot] = (long_part + direct_part).astype(jnp.bfloat16)

        @pl.when(slot < shared)
        def _():
            for i in CROSS:
                response_copy(i, slot).start()

        response_copy(SIBLING, slot).start()

        @pl.when(slot + 2 <= shared)
        def _():
            relay_filter(slot + 2)

        response = response_slab[slot, position_rows(me), :]

        @pl.when(slot < shared)
        def _():
            mix_into(me, slot, response)

        @pl.when(slot == shared)
        def _():
            mix_into(core, 0, response)

        return carry

    lax.fori_loop(first, shared + 1, convolve, 0)

    def finish_near(chunk, carry):
        response_copy(SIBLING, chunk).wait_recv()
        mix_into(sources[SIBLING], chunk, response_in[SIBLING, chunk])
        return carry

    def finish_cross(chunk, carry):
        for i in CROSS:
            response_copy(i, chunk).wait_recv()
            mix_into(sources[i], chunk, response_in[i, chunk])
        return carry

    lax.fori_loop(first, chunks, finish_near, 0)
    response_copy(SIBLING, shared).wait_recv()
    mix_into(1 - core, 0, response_in[SIBLING, shared])
    lax.fori_loop(chip, chunks, finish_cross, 0)

    def drain_gated(chunk, carry):
        for i in CROSS:
            gated_copy(i, chunk, me).wait_send()
        return carry

    def drain_response(slot, carry):
        for i in CROSS:
            response_copy(i, slot).wait_send()
        return carry

    def drain_near(slot, carry):
        gated_copy(SIBLING, slot, me).wait_send()
        response_copy(SIBLING, slot).wait_send()
        for turn in turns:
            zfil_copy(turn, slot).wait_send()
        for turn in range(zsize):
            yfil_copy(turn, slot).wait_send()
        return carry

    lax.fori_loop(chip, chunks, drain_gated, 0)
    lax.fori_loop(first, chunks, drain_response, 0)
    lax.fori_loop(first, shared + 1, drain_near, 0)

    @pl.when(chip == 0)
    def _():
        gated_copy(ACROSS, shared, me, gated_slab.at[shared, position_rows(me), :]).wait_send()
        gated_copy(DIAGONAL, shared, me, gated_out.at[SIBLING, shared]).wait_send()
        shared_filter_copy().wait_send()
        shared_skip_send().wait_send()

    for i in (ACROSS, SIBLING, DIAGONAL):
        taps_copy(i, me).wait_send()

    @pl.when(has_following)
    def _():
        halo_copy.wait_send()


def write_kernel(mixed_ref, out_hbm, sem):
    copy = pltpu.make_async_copy(mixed_ref, out_hbm, sem)
    copy.start()
    copy.wait()


def write_out(mixed):
    return pl.pallas_call(
        write_kernel,
        out_shape=jax.ShapeDtypeStruct(mixed.shape, mixed.dtype),
        in_specs=[pl.BlockSpec(memory_space=pltpu.VMEM)],
        out_specs=pl.BlockSpec(memory_space=pltpu.HBM),
        scratch_shapes=[pltpu.SemaphoreType.DMA],
    )(pltpu.with_memory_space_constraint(mixed, pltpu.VMEM))


def on_device(projected, short_taps, long_filter, skip_gain):
    ctx_size, dp_size = lax.axis_size("ctx"), lax.axis_size("dp")
    kernel_size, streams, channels = short_taps.shape
    rows, width = projected.shape[1], projected.shape[3]
    length = rows * ctx_size
    regular = ctx_size == 4 and dp_size % 2 == 0 and dp_size >= 6
    regular = regular and channels % CHUNK == 0 and channels >= 2 * CHUNK
    if length > 1024 or not regular:
        return on_device_large(projected, short_taps, long_filter, skip_gain)
    forward, backward = quarter_tables(length)
    chunks = channels // CHUNK
    slots = chunks + 1
    peers = ctx_size - 1
    zsize = dp_size // 2
    hbm_spec = pl.BlockSpec(memory_space=pltpu.HBM)
    dma = pltpu.SemaphoreType.DMA
    operands = (
        projected[0].transpose(1, 0, 2),
        short_taps,
        long_filter,
        skip_gain[None],
        forward,
        backward,
    )
    mixed = pl.pallas_call(
        functools.partial(mixer_kernel, ctx_size, dp_size),
        out_shape=pltpu.VMEM((rows, width), jnp.bfloat16),
        in_specs=[hbm_spec] * len(operands),
        out_specs=pl.BlockSpec(memory_space=pltpu.VMEM),
        scratch_shapes=[
            pltpu.VMEM((streams, rows, width), jnp.bfloat16),
            pltpu.VMEM((streams, 16, width), jnp.bfloat16),
            pltpu.VMEM((1, channels + CHUNK), jnp.float32),
            pltpu.VMEM(forward.shape, jnp.bfloat16),
            pltpu.VMEM(backward.shape, jnp.bfloat16),
            pltpu.VMEM((ctx_size, kernel_size, streams, channels), jnp.float32),
            pltpu.VMEM((streams, kernel_size - 1, width), jnp.bfloat16),
            pltpu.VMEM((streams, kernel_size - 1, width), jnp.bfloat16),
            pltpu.VMEM((peers, slots, rows, CHUNK), jnp.bfloat16),
            pltpu.VMEM((slots, length, CHUNK), jnp.bfloat16),
            pltpu.VMEM((slots, length, CHUNK), jnp.bfloat16),
            pltpu.VMEM((2 * length, CHUNK), jnp.float32),
            pltpu.VMEM((2 * length, CHUNK), jnp.bfloat16),
            pltpu.VMEM((slots, length, CHUNK), jnp.bfloat16),
            pltpu.VMEM((peers, slots, rows, CHUNK), jnp.bfloat16),
            pltpu.VMEM((ctx_size, chunks, rows, CHUNK), jnp.bfloat16),
            dma((9,)),
            dma((peers,)),
            dma((peers,)),
            dma,
            dma,
            dma((zsize - 1, slots)),
            dma((zsize - 1, slots)),
            dma((zsize, slots)),
            dma((zsize, slots)),
            dma((peers, slots)),
            dma((peers, slots)),
            dma((peers, slots)),
            dma((peers, slots)),
            dma((chunks,)),
            pltpu.SemaphoreType.REGULAR((zsize,)),
            dma((2,)),
            dma((2,)),
        ],
        compiler_params=pltpu.CompilerParams(
            collective_id=0, has_side_effects=True, vmem_limit_bytes=40 * 2**20
        ),
    )(*(pltpu.with_memory_space_constraint(array, pltpu.HBM) for array in operands))
    return write_out(mixed)[None]


def solution(mesh):
    return jax.shard_map(
        on_device,
        mesh=mesh,
        in_specs=(P("dp", "ctx", None, None), P(None, None, "ctx"), P("dp", "ctx"), P("ctx")),
        out_specs=P("dp", "ctx", None),
        check_vma=False,
    )
```

```python
import functools
import math

import jax
import jax.numpy as jnp
import numpy as np
from jax import lax
from jax.experimental import pallas as pl
from jax.experimental.pallas import tpu as pltpu
from jax.sharding import PartitionSpec as P

RADIX = 64


HIGH = lax.Precision.HIGHEST


def causal_short(extended, taps, kernel_size):
    row_count = extended.shape[0] - (kernel_size - 1)
    widened = extended.astype(jnp.float32)
    summed = jnp.zeros((row_count,) + widened.shape[1:], jnp.float32)
    for tap_index in range(kernel_size):
        offset = kernel_size - 1 - tap_index
        summed = summed + taps[tap_index] * widened[offset : offset + row_count]
    return (summed[:, 0].astype(jnp.bfloat16), (summed[:, 1] * summed[:, 2]).astype(jnp.bfloat16))


def dft_tables(length, radix_size):
    outer_size = 2 * length // radix_size
    total_size = outer_size * radix_size
    outer_range = jnp.arange(outer_size, dtype=jnp.int32)
    inner_range = jnp.arange(radix_size, dtype=jnp.int32)
    angle_one = (
        2.0
        * math.pi
        / outer_size
        * (outer_range[:, None] * outer_range[None, :] % outer_size).astype(jnp.float32)
    )
    angle_twist = (
        2.0
        * math.pi
        / total_size
        * (outer_range[:, None] * inner_range[None, :] % total_size).astype(jnp.float32)
    )
    angle_two = (
        2.0
        * math.pi
        / radix_size
        * (inner_range[:, None] * inner_range[None, :] % radix_size).astype(jnp.float32)
    )
    twist_cos = jnp.cos(angle_twist)[:, :, None]
    twist_sin = jnp.sin(angle_twist)[:, :, None]
    return (
        jnp.cos(angle_one),
        jnp.sin(angle_one),
        twist_cos,
        twist_sin,
        jnp.cos(angle_two),
        jnp.sin(angle_two),
    )


def forward_dft(signal, tables, radix_size):
    cos_one, sin_one, twist_cos, twist_sin, cos_two, sin_two = tables
    outer_size = cos_one.shape[0]
    half_size = outer_size // 2
    block_width = signal.shape[1]
    shaped = signal.reshape(half_size, radix_size * block_width)
    first_re = jnp.dot(cos_one[:, :half_size], shaped, precision=HIGH).reshape(
        outer_size, radix_size, block_width
    )
    first_im = -jnp.dot(sin_one[:, :half_size], shaped, precision=HIGH).reshape(
        outer_size, radix_size, block_width
    )
    second_re = first_re * twist_cos + first_im * twist_sin
    second_im = first_im * twist_cos - first_re * twist_sin
    spec_re = jnp.einsum("amc,mb->abc", second_re, cos_two, precision=HIGH) + jnp.einsum(
        "amc,mb->abc", second_im, sin_two, precision=HIGH
    )
    spec_im = jnp.einsum("amc,mb->abc", second_im, cos_two, precision=HIGH) - jnp.einsum(
        "amc,mb->abc", second_re, sin_two, precision=HIGH
    )
    return (spec_re, spec_im)


def inverse_dft(spec_re, spec_im, tables, radix_size):
    cos_one, sin_one, twist_cos, twist_sin, cos_two, sin_two = tables
    outer_size = cos_one.shape[0]
    half_size = outer_size // 2
    block_width = spec_re.shape[2]
    back_re = jnp.einsum("abc,mb->amc", spec_re, cos_two, precision=HIGH) - jnp.einsum(
        "abc,mb->amc", spec_im, sin_two, precision=HIGH
    )
    back_im = jnp.einsum("abc,mb->amc", spec_re, sin_two, precision=HIGH) + jnp.einsum(
        "abc,mb->amc", spec_im, cos_two, precision=HIGH
    )
    turned_re = (back_re * twist_cos - back_im * twist_sin).reshape(
        outer_size, radix_size * block_width
    )
    turned_im = (back_re * twist_sin + back_im * twist_cos).reshape(
        outer_size, radix_size * block_width
    )
    result = jnp.dot(cos_one[:half_size], turned_re, precision=HIGH) - jnp.dot(
        sin_one[:half_size], turned_im, precision=HIGH
    )
    return result.reshape(half_size * radix_size, block_width) / (outer_size * radix_size)


def long_convolve_blocked(gated_slab, filter_slab):
    length, channels = gated_slab.shape
    block_width = min(128, channels)
    tables = dft_tables(length, RADIX)

    def one_block(block_index, output):
        offset = block_index * block_width
        signal = lax.dynamic_slice_in_dim(gated_slab, offset, block_width, 1).astype(jnp.float32)
        kernel_block = lax.dynamic_slice_in_dim(filter_slab, offset, block_width, 1).astype(
            jnp.float32
        )
        sig_re, sig_im = forward_dft(signal, tables, RADIX)
        ker_re, ker_im = forward_dft(kernel_block, tables, RADIX)
        prod_re = sig_re * ker_re - sig_im * ker_im
        prod_im = sig_re * ker_im + sig_im * ker_re
        result = inverse_dft(prod_re, prod_im, tables, RADIX)
        return lax.dynamic_update_slice_in_dim(output, result, offset, 1)

    return lax.fori_loop(
        0, channels // block_width, one_block, jnp.zeros((length, channels), jnp.float32)
    )


def long_convolve(gated_slab, filter_slab):
    length = gated_slab.shape[0]
    if length > 1024:
        return long_convolve_blocked(gated_slab, filter_slab)
    forward, backward = quarter_tables(length)
    sig = jnp.dot(forward, gated_slab, preferred_element_type=jnp.float32)
    ker = jnp.dot(forward, filter_slab, preferred_element_type=jnp.float32)
    sig_cos, sig_sin, ker_cos, ker_sin = sig[:length], sig[length:], ker[:length], ker[length:]
    prod = jnp.concatenate(
        [sig_cos * ker_cos - sig_sin * ker_sin, sig_cos * ker_sin + sig_sin * ker_cos]
    ).astype(jnp.bfloat16)
    return jnp.dot(backward, prod, preferred_element_type=jnp.float32)


def quarter_tables(length):
    steps = (4 * np.arange(length)[:, None] + 1) * np.arange(length)[None, :] % (4 * length)
    angles = steps * (2.0 * math.pi / (4 * length))
    table = np.concatenate([np.cos(angles), np.sin(angles)])
    return (jnp.asarray(table, jnp.bfloat16), jnp.asarray(table.T / length, jnp.bfloat16))


def make_response(gated_slab, filter_slab, skip_gain):
    long_part = long_convolve(gated_slab, filter_slab)
    return (long_part + skip_gain * gated_slab.astype(jnp.float32)).astype(jnp.bfloat16)


def combine_rows(query_part, response_part):
    return (query_part.astype(jnp.float32) * response_part.astype(jnp.float32)).astype(jnp.bfloat16)


def on_device_large(projected, short_taps, long_filter, skip_gain):
    kernel_size = short_taps.shape[0]
    ctx_size = lax.axis_size("ctx")
    rows = projected[0]
    filter_slab = lax.all_gather(long_filter, "dp", axis=0, tiled=True)
    all_taps = lax.all_gather(short_taps, "ctx", axis=2, tiled=True)
    halo = lax.ppermute(
        rows[-(kernel_size - 1) :], "ctx", [(i, i + 1) for i in range(ctx_size - 1)]
    )
    queries, gated = causal_short(jnp.concatenate([halo, rows]), all_taps, kernel_size)
    gated_slab = lax.all_to_all(gated, "ctx", split_axis=1, concat_axis=0, tiled=True)
    response_slab = make_response(gated_slab, filter_slab, skip_gain)
    response = lax.all_to_all(response_slab, "ctx", split_axis=0, concat_axis=1, tiled=True)
    return combine_rows(queries, response)[None]


CHUNK = 256
MESH = pl.DeviceIdType.MESH
ACROSS, DIAGONAL, SIBLING = 0, 1, 2
CROSS = (ACROSS, DIAGONAL)
TOP = 16


def ctx_offsets(ctx_size):
    pairs = [(a, b) for a in range(1, ctx_size // 2) for b in range(2)]
    return pairs + [(0, 1)]


def ctx_peer(me, offset, ctx_size, sign):
    half = ctx_size // 2
    chip = lax.rem(me // 2 + (half + sign * offset[0]) % half, half)
    core = lax.rem(lax.rem(me, 2) + offset[1], 2)
    return chip * 2 + core


def mixer_kernel(
    ctx_size,
    dp_size,
    x_hbm,
    taps_hbm,
    filter_hbm,
    skip_hbm,
    forward_hbm,
    backward_hbm,
    out_ref,
    x_ref,
    tail_ref,
    skip_ref,
    forward_ref,
    backward_ref,
    taps_all,
    halo_out,
    halo_in,
    gated_out,
    gated_slab,
    filter_slab,
    spectrum,
    prod_ref,
    response_slab,
    response_in,
    queries,
    local_sem,
    taps_send,
    taps_recv,
    halo_send,
    halo_recv,
    zfil_send,
    zfil_recv,
    yfil_send,
    yfil_recv,
    gated_send,
    gated_recv,
    resp_send,
    resp_recv,
    filter_sem,
    ready_sem,
    shared_send,
    shared_recv,
):
    kernel_size = taps_hbm.shape[0]
    channels = taps_hbm.shape[2]
    rows = x_ref.shape[1]
    length = rows * ctx_size
    chunks = channels // CHUNK
    fil_rows = filter_hbm.shape[0]
    zsize = dp_size // 2
    turns = list(range(1, zsize))
    me = lax.axis_index("ctx")
    dp = lax.axis_index("dp")
    zpos, ypos = dp // 2, lax.rem(dp, 2)
    chip, core = me // 2, lax.rem(me, 2)
    first = 1 - chip
    offsets = ctx_offsets(ctx_size)
    dests = [ctx_peer(me, o, ctx_size, 1) for o in offsets]
    sources = [ctx_peer(me, o, ctx_size, -1) for o in offsets]
    ypeer = zpos * 2 + (1 - ypos)

    def signal(semaphore, **where):
        pl.semaphore_signal(semaphore, inc=1, device_id=where, device_id_type=MESH)

    barrier = pltpu.get_barrier_semaphore()
    for dest in dests:
        signal(barrier, ctx=dest)
    signal(barrier, dp=ypeer)
    for turn in turns:

        @pl.when(zpos + turn < zsize)
        def _(turn=turn):
            signal(barrier, dp=dp + 2 * turn)

    @pl.when(zpos > 0)
    def _():
        signal(barrier, dp=dp - 2)

    above = (zpos < zsize - 1).astype(jnp.int32)
    greeted = len(dests) + 1 + above + zpos

    def local_copy(source, target, index):
        copy = pltpu.make_async_copy(source, target, local_sem.at[index])
        copy.start()
        return copy

    own_taps_copy = local_copy(taps_hbm, taps_all.at[me], 0)
    tail_rows = tail_ref.shape[1]
    tail_copy = local_copy(x_hbm.at[:, pl.ds(rows - tail_rows, tail_rows), :], tail_ref, 1)
    gate_copies = [local_copy(x_hbm.at[stream], x_ref.at[stream], 2 + stream) for stream in (1, 2)]

    shared = chunks
    slots = [first + k for k in range(chunks)]

    def filter_block(block, slot):
        return filter_slab.at[slot, pl.ds(pl.multiple_of(block * fil_rows, fil_rows), fil_rows), :]

    def own_filter_copy(chunk):
        slot = shared * first if chunk == 0 else chunk
        return pltpu.make_async_copy(
            filter_hbm.at[:, pl.ds(chunk * CHUNK, CHUNK)],
            filter_block(dp, slot),
            filter_sem.at[chunk],
        )

    for chunk in range(chunks):
        own_filter_copy(chunk).start()
    skip_copy = local_copy(skip_hbm, skip_ref.at[:, pl.ds(0, channels)], 5)
    shared_skip = skip_ref.at[:, pl.ds(channels, CHUNK)]
    shared_skip_copy = pltpu.make_async_copy(
        skip_hbm.at[:, pl.ds(0, CHUNK)], shared_skip, local_sem.at[8]
    )

    @pl.when(chip == 0)
    def _():
        shared_skip_copy.start()

    late_copies = [
        local_copy(x_hbm.at[0], x_ref.at[0], 2),
        local_copy(forward_hbm, forward_ref, 6),
        local_copy(backward_hbm, backward_ref, 7),
        skip_copy,
    ]

    halo_copy = pltpu.make_async_remote_copy(
        src_ref=halo_out,
        dst_ref=halo_in,
        send_sem=halo_send,
        recv_sem=halo_recv,
        device_id={"ctx": lax.rem(me + 1, ctx_size)},
        device_id_type=MESH,
    )
    has_following, has_previous = me < ctx_size - 1, me > 0
    tail_copy.wait()

    @pl.when(has_following)
    def _():
        halo_out[...] = tail_ref[:, tail_rows - (kernel_size - 1) :, :]

    own_taps_copy.wait()
    def short_filter(stream, owner, chunk, count, edged=True):
        columns = pl.ds(pl.multiple_of(owner * channels + chunk * CHUNK, CHUNK), CHUNK)
        taps_columns = pl.ds(pl.multiple_of(chunk * CHUNK, CHUNK), CHUNK)
        values = x_ref[stream, :count, columns].astype(jnp.float32)
        if edged:
            edge = halo_in[stream, :, columns].astype(jnp.float32)
            edge = jnp.where(has_previous, edge, jnp.zeros_like(edge))
            row_index = lax.broadcasted_iota(jnp.int32, (8, CHUNK), 0)
        total = taps_all[owner, 0, stream : stream + 1, taps_columns] * values
        for tap in range(1, kernel_size):
            moved = pltpu.roll(values, tap, 0)
            if edged:
                top = moved[:8]
                for row in range(tap):
                    at = kernel_size - 1 + row - tap
                    top = jnp.where(row_index == row, edge[at : at + 1], top)
                moved = jnp.concatenate([top, moved[8:]], axis=0)
            total = total + taps_all[owner, tap, stream : stream + 1, taps_columns] * moved
        return total

    def gated_rows(owner, chunk, count=rows, edged=True):
        keys, values = (short_filter(stream, owner, chunk, count, edged) for stream in (1, 2))
        return (keys * values).astype(jnp.bfloat16)

    def position_rows(owner):
        return pl.ds(pl.multiple_of(owner * rows, rows), rows)

    body_rows = pl.ds(pl.multiple_of(me * rows + TOP, TOP), rows - TOP)
    top_rows = pl.ds(pl.multiple_of(me * rows, rows), TOP)

    @pl.when(chip == 0)
    def _():
        for copy in gate_copies:
            copy.wait()
        gated_slab[shared, body_rows, :] = gated_rows(core, 0, edged=False)[TOP:]

    def shared_part_copy(part, part_rows):
        return pltpu.make_async_remote_copy(
            src_ref=gated_slab.at[shared, part_rows, :],
            dst_ref=gated_slab.at[shared, part_rows, :],
            send_sem=shared_send.at[part],
            recv_sem=shared_recv.at[part],
            device_id={"ctx": dests[ACROSS]},
            device_id_type=MESH,
        )

    def shared_body_copy():
        return shared_part_copy(2, body_rows)

    def shared_top_copy():
        return shared_part_copy(3, top_rows)

    pl.semaphore_wait(barrier, greeted)

    @pl.when(has_following)
    def _():
        halo_copy.start()

    def taps_copy(i, slot):
        return pltpu.make_async_remote_copy(
            src_ref=taps_all.at[slot],
            dst_ref=taps_all.at[slot],
            send_sem=taps_send.at[i],
            recv_sem=taps_recv.at[i],
            device_id={"ctx": dests[ACROSS] if i == ACROSS else dests[SIBLING]},
            device_id_type=MESH,
        )

    for i in (ACROSS, SIBLING):
        taps_copy(i, me).start()

    @pl.when(chip == 0)
    def _():
        shared_body_copy().start()

    for turn in turns[1:]:

        @pl.when(zpos >= turn)
        def _(turn=turn):
            signal(ready_sem.at[turn], dp=dp - 2 * turn)

    def zfil_copy(turn, slot):
        target = lax.rem(zpos + turn, zsize)
        return pltpu.make_async_remote_copy(
            src_ref=filter_block(dp, slot),
            dst_ref=filter_block(dp, slot),
            send_sem=zfil_send.at[turn - 1, slot],
            recv_sem=zfil_recv.at[turn - 1, slot],
            device_id={"dp": target * 2 + ypos},
            device_id_type=MESH,
        )

    def yfil_copy(turn, slot):
        origin = lax.rem(zpos + zsize - turn, zsize)
        block = origin * 2 + ypos
        return pltpu.make_async_remote_copy(
            src_ref=filter_block(block, slot),
            dst_ref=filter_block(block, slot),
            send_sem=yfil_send.at[turn, slot],
            recv_sem=yfil_recv.at[turn, slot],
            device_id={"dp": ypeer},
            device_id_type=MESH,
        )

    def shared_filter_copy():
        return pltpu.make_async_remote_copy(
            src_ref=filter_block(dp, shared),
            dst_ref=filter_block(dp, shared),
            send_sem=shared_send.at[0],
            recv_sem=shared_recv.at[0],
            device_id={"ctx": dests[ACROSS]},
            device_id_type=MESH,
        )

    def shared_skip_send():
        return pltpu.make_async_remote_copy(
            src_ref=shared_skip,
            dst_ref=shared_skip,
            send_sem=shared_send.at[1],
            recv_sem=shared_recv.at[1],
            device_id={"ctx": dests[ACROSS]},
            device_id_type=MESH,
        )

    def relay_filter(slot):
        for turn in turns:
            zfil_copy(turn, slot).wait_recv()
            yfil_copy(turn, slot).start()

    def send_up(turn, slot):
        @pl.when(zpos + turn < zsize)
        def _():
            zfil_copy(turn, slot).start()

    def send_down(turn, slot):
        @pl.when(zpos + turn >= zsize)
        def _():
            zfil_copy(turn, slot).start()

    def wait_up(turn):
        @pl.when(zpos + turn < zsize)
        def _():
            pl.semaphore_wait(ready_sem.at[turn], 1)

    for chunk in range(chunks):
        own_filter_copy(chunk).wait()
    for slot in slots:
        for turn in turns:
            send_down(turn, slot)
        yfil_copy(0, slot).start()
    for slot in slots[:2]:
        send_up(1, slot)

    def gated_copy(i, slot, owner, source=None):
        return pltpu.make_async_remote_copy(
            src_ref=gated_out.at[i, slot] if source is None else source,
            dst_ref=gated_slab.at[slot, position_rows(owner), :],
            send_sem=gated_send.at[i, slot],
            recv_sem=gated_recv.at[i, slot],
            device_id={"ctx": dests[i]},
            device_id_type=MESH,
        )

    def response_copy(i, slot):
        return pltpu.make_async_remote_copy(
            src_ref=response_slab.at[slot, position_rows(dests[i]), :],
            dst_ref=response_in.at[i, slot],
            send_sem=resp_send.at[i, slot],
            recv_sem=resp_recv.at[i, slot],
            device_id={"ctx": dests[i]},
            device_id_type=MESH,
        )

    def push_gated(i, chunk):
        gated_out[i, chunk] = gated_rows(dests[i], chunk)
        gated_copy(i, chunk, me).start()

    def push_near(chunk):
        push_gated(SIBLING, chunk)
        gated_slab[chunk, position_rows(me), :] = gated_rows(me, chunk)

    def shared_own():
        gated_slab[shared, position_rows(me), :] = gated_rows(core, 0)

    def shared_other():
        gated_out[SIBLING, shared] = gated_rows(1 - core, 0)
        gated_copy(SIBLING, shared, me).start()

    taps_copy(SIBLING, sources[SIBLING]).wait_recv()

    @pl.when(chip == 1)
    def _():
        for copy in gate_copies:
            copy.wait()

    @pl.when(jnp.logical_and(chip == 0, has_previous))
    def _():
        halo_copy.wait_recv()

    @pl.when(chip == 0)
    def _():
        gated_slab[shared, top_rows, :] = gated_rows(core, 0, TOP)
        shared_top_copy().start()
        shared_other()
        gated_copy(DIAGONAL, shared, me, gated_out.at[SIBLING, shared]).start()
        shared_filter_copy().start()
        shared_skip_copy.wait()
        shared_skip_send().start()
        half = length // 2
        gated_slab[shared, half:] = jnp.zeros((length - half, CHUNK), jnp.bfloat16)

    for turn in turns[1:]:
        wait_up(turn)
    for k, slot in enumerate(slots):
        for turn in reversed(turns):
            if turn > 1 or k > 1:
                send_up(turn, slot)

    taps_copy(ACROSS, sources[ACROSS]).wait_recv()
    taps_copy(DIAGONAL, sources[ACROSS]).start()

    @pl.when(chip == 1)
    def _():
        halo_copy.wait_recv()

    push_gated(ACROSS, chip)
    taps_copy(DIAGONAL, sources[DIAGONAL]).wait_recv()
    push_gated(DIAGONAL, chip)

    push_near(first)
    def push_chunk(step, carry):
        @pl.when(chip + step < chunks)
        def _():
            push_gated(ACROSS, chip + step)
            push_gated(DIAGONAL, chip + step)

        @pl.when(first + step < chunks)
        def _():
            push_near(first + step)

        return carry

    lax.fori_loop(1, 3, push_chunk, 0)
    relay_filter(first)
    lax.fori_loop(3, chunks, push_chunk, 0)

    @pl.when(chip == 1)
    def _():
        shared_own()
        shared_other()

    for copy in late_copies:
        copy.wait()

    def fill_queries(chunk, carry):
        def one_owner(owner, inner):
            queries[owner, chunk] = short_filter(0, owner, chunk, rows).astype(jnp.bfloat16)
            return inner

        return lax.fori_loop(0, ctx_size, one_owner, carry)

    @pl.when(chip == 1)
    def _():
        shared_filter_copy().wait_recv()
        shared_skip_send().wait_recv()
        yfil_copy(0, shared).start()
        for turn in turns:
            zfil_copy(turn, shared).start()

    lax.fori_loop(0, chunks, fill_queries, 0)
    relay_filter(first + 1)

    def mix_into(owner, chunk, response):
        columns = pl.ds(pl.multiple_of(owner * channels + chunk * CHUNK, CHUNK), CHUNK)
        mixed = queries[owner, chunk].astype(jnp.float32) * response.astype(jnp.float32)
        out_ref[:, columns] = mixed.astype(jnp.bfloat16)

    def convolve(slot, carry):
        columns = pl.ds(pl.multiple_of(slot * CHUNK, CHUNK), CHUNK)

        @pl.when(slot < shared)
        def _():
            gated_copy(ACROSS, slot, sources[ACROSS]).wait_recv()

        @pl.when(jnp.logical_and(slot == shared, chip == 1))
        def _():
            shared_body_copy().wait_recv()
            shared_top_copy().wait_recv()

        @pl.when(jnp.logical_or(slot < shared, chip == 1))
        def _():
            gated_copy(DIAGONAL, slot, sources[DIAGONAL]).wait_recv()

        gated_copy(SIBLING, slot, sources[SIBLING]).wait_recv()
        gated = gated_slab[slot]
        spectrum[...] = jnp.dot(forward_ref[...], gated, preferred_element_type=jnp.float32)
        for turn in range(zsize):
            yfil_copy(turn, slot).wait_recv()
        taps = filter_slab[slot]
        ker_cos = jnp.dot(forward_ref[:length], taps, preferred_element_type=jnp.float32)
        ker_sin = jnp.dot(forward_ref[length:], taps, preferred_element_type=jnp.float32)
        sig_cos, sig_sin = spectrum[:length], spectrum[length:]
        prod_ref[:length] = (sig_cos * ker_cos - sig_sin * ker_sin).astype(jnp.bfloat16)
        prod_ref[length:] = (sig_cos * ker_sin + sig_sin * ker_cos).astype(jnp.bfloat16)
        long_part = jnp.dot(backward_ref[...], prod_ref[...], preferred_element_type=jnp.float32)
        direct_part = skip_ref[:, columns] * gated.astype(jnp.float32)
        response_slab[slot] = (long_part + direct_part).astype(jnp.bfloat16)

        @pl.when(slot < shared)
        def _():
            for i in CROSS:
                response_copy(i, slot).start()

        response_copy(SIBLING, slot).start()

        @pl.when(slot + 2 <= shared)
        def _():
            relay_filter(slot + 2)

        response = response_slab[slot, position_rows(me), :]

        @pl.when(slot < shared)
        def _():
            mix_into(me, slot, response)

        @pl.when(slot == shared)
        def _():
            mix_into(core, 0, response)

        return carry

    lax.fori_loop(first, shared + 1, convolve, 0)

    def finish_near(chunk, carry):
        response_copy(SIBLING, chunk).wait_recv()
        mix_into(sources[SIBLING], chunk, response_in[SIBLING, chunk])
        return carry

    def finish_cross(chunk, carry):
        for i in CROSS:
            response_copy(i, chunk).wait_recv()
            mix_into(sources[i], chunk, response_in[i, chunk])
        return carry

    lax.fori_loop(first, chunks, finish_near, 0)
    response_copy(SIBLING, shared).wait_recv()
    mix_into(1 - core, 0, response_in[SIBLING, shared])
    lax.fori_loop(chip, chunks, finish_cross, 0)

    def drain_gated(chunk, carry):
        for i in CROSS:
            gated_copy(i, chunk, me).wait_send()
        return carry

    def drain_response(slot, carry):
        for i in CROSS:
            response_copy(i, slot).wait_send()
        return carry

    def drain_near(slot, carry):
        gated_copy(SIBLING, slot, me).wait_send()
        response_copy(SIBLING, slot).wait_send()
        for turn in turns:
            zfil_copy(turn, slot).wait_send()
        for turn in range(zsize):
            yfil_copy(turn, slot).wait_send()
        return carry

    lax.fori_loop(chip, chunks, drain_gated, 0)
    lax.fori_loop(first, chunks, drain_response, 0)
    lax.fori_loop(first, shared + 1, drain_near, 0)

    @pl.when(chip == 0)
    def _():
        shared_body_copy().wait_send()
        shared_top_copy().wait_send()
        gated_copy(DIAGONAL, shared, me, gated_out.at[SIBLING, shared]).wait_send()
        shared_filter_copy().wait_send()
        shared_skip_send().wait_send()

    for i in (ACROSS, SIBLING, DIAGONAL):
        taps_copy(i, me).wait_send()

    @pl.when(has_following)
    def _():
        halo_copy.wait_send()


def write_kernel(mixed_ref, out_hbm, sem):
    copy = pltpu.make_async_copy(mixed_ref, out_hbm, sem)
    copy.start()
    copy.wait()


def write_out(mixed):
    return pl.pallas_call(
        write_kernel,
        out_shape=jax.ShapeDtypeStruct(mixed.shape, mixed.dtype),
        in_specs=[pl.BlockSpec(memory_space=pltpu.VMEM)],
        out_specs=pl.BlockSpec(memory_space=pltpu.HBM),
        scratch_shapes=[pltpu.SemaphoreType.DMA],
    )(pltpu.with_memory_space_constraint(mixed, pltpu.VMEM))


def on_device(projected, short_taps, long_filter, skip_gain):
    ctx_size, dp_size = lax.axis_size("ctx"), lax.axis_size("dp")
    kernel_size, streams, channels = short_taps.shape
    rows, width = projected.shape[1], projected.shape[3]
    length = rows * ctx_size
    regular = ctx_size == 4 and dp_size % 2 == 0 and dp_size >= 6
    regular = regular and channels % CHUNK == 0 and channels >= 2 * CHUNK
    if length > 1024 or not regular:
        return on_device_large(projected, short_taps, long_filter, skip_gain)
    forward, backward = quarter_tables(length)
    chunks = channels // CHUNK
    slots = chunks + 1
    peers = ctx_size - 1
    zsize = dp_size // 2
    hbm_spec = pl.BlockSpec(memory_space=pltpu.HBM)
    dma = pltpu.SemaphoreType.DMA
    operands = (
        projected[0].transpose(1, 0, 2),
        short_taps,
        long_filter,
        skip_gain[None],
        forward,
        backward,
    )
    mixed = pl.pallas_call(
        functools.partial(mixer_kernel, ctx_size, dp_size),
        out_shape=pltpu.VMEM((rows, width), jnp.bfloat16),
        in_specs=[hbm_spec] * len(operands),
        out_specs=pl.BlockSpec(memory_space=pltpu.VMEM),
        scratch_shapes=[
            pltpu.VMEM((streams, rows, width), jnp.bfloat16),
            pltpu.VMEM((streams, 16, width), jnp.bfloat16),
            pltpu.VMEM((1, channels + CHUNK), jnp.float32),
            pltpu.VMEM(forward.shape, jnp.bfloat16),
            pltpu.VMEM(backward.shape, jnp.bfloat16),
            pltpu.VMEM((ctx_size, kernel_size, streams, channels), jnp.float32),
            pltpu.VMEM((streams, kernel_size - 1, width), jnp.bfloat16),
            pltpu.VMEM((streams, kernel_size - 1, width), jnp.bfloat16),
            pltpu.VMEM((peers, slots, rows, CHUNK), jnp.bfloat16),
            pltpu.VMEM((slots, length, CHUNK), jnp.bfloat16),
            pltpu.VMEM((slots, length, CHUNK), jnp.bfloat16),
            pltpu.VMEM((2 * length, CHUNK), jnp.float32),
            pltpu.VMEM((2 * length, CHUNK), jnp.bfloat16),
            pltpu.VMEM((slots, length, CHUNK), jnp.bfloat16),
            pltpu.VMEM((peers, slots, rows, CHUNK), jnp.bfloat16),
            pltpu.VMEM((ctx_size, chunks, rows, CHUNK), jnp.bfloat16),
            dma((9,)),
            dma((peers,)),
            dma((peers,)),
            dma,
            dma,
            dma((zsize - 1, slots)),
            dma((zsize - 1, slots)),
            dma((zsize, slots)),
            dma((zsize, slots)),
            dma((peers, slots)),
            dma((peers, slots)),
            dma((peers, slots)),
            dma((peers, slots)),
            dma((chunks,)),
            pltpu.SemaphoreType.REGULAR((zsize,)),
            dma((4,)),
            dma((4,)),
        ],
        compiler_params=pltpu.CompilerParams(
            collective_id=0, has_side_effects=True, vmem_limit_bytes=40 * 2**20
        ),
    )(*(pltpu.with_memory_space_constraint(array, pltpu.HBM) for array in operands))
    return write_out(mixed)[None]


def solution(mesh):
    return jax.shard_map(
        on_device,
        mesh=mesh,
        in_specs=(P("dp", "ctx", None, None), P(None, None, "ctx"), P("dp", "ctx"), P("ctx")),
        out_specs=P("dp", "ctx", None),
        check_vma=False,
    )
```

```python
import functools
import math

import jax
import jax.numpy as jnp
import numpy as np
from jax import lax
from jax.experimental import pallas as pl
from jax.experimental.pallas import tpu as pltpu
from jax.sharding import PartitionSpec as P

RADIX = 64


HIGH = lax.Precision.HIGHEST


def causal_short(extended, taps, kernel_size):
    row_count = extended.shape[0] - (kernel_size - 1)
    widened = extended.astype(jnp.float32)
    summed = jnp.zeros((row_count,) + widened.shape[1:], jnp.float32)
    for tap_index in range(kernel_size):
        offset = kernel_size - 1 - tap_index
        summed = summed + taps[tap_index] * widened[offset : offset + row_count]
    return (summed[:, 0].astype(jnp.bfloat16), (summed[:, 1] * summed[:, 2]).astype(jnp.bfloat16))


def dft_tables(length, radix_size):
    outer_size = 2 * length // radix_size
    total_size = outer_size * radix_size
    outer_range = jnp.arange(outer_size, dtype=jnp.int32)
    inner_range = jnp.arange(radix_size, dtype=jnp.int32)
    angle_one = (
        2.0
        * math.pi
        / outer_size
        * (outer_range[:, None] * outer_range[None, :] % outer_size).astype(jnp.float32)
    )
    angle_twist = (
        2.0
        * math.pi
        / total_size
        * (outer_range[:, None] * inner_range[None, :] % total_size).astype(jnp.float32)
    )
    angle_two = (
        2.0
        * math.pi
        / radix_size
        * (inner_range[:, None] * inner_range[None, :] % radix_size).astype(jnp.float32)
    )
    twist_cos = jnp.cos(angle_twist)[:, :, None]
    twist_sin = jnp.sin(angle_twist)[:, :, None]
    return (
        jnp.cos(angle_one),
        jnp.sin(angle_one),
        twist_cos,
        twist_sin,
        jnp.cos(angle_two),
        jnp.sin(angle_two),
    )


def forward_dft(signal, tables, radix_size):
    cos_one, sin_one, twist_cos, twist_sin, cos_two, sin_two = tables
    outer_size = cos_one.shape[0]
    half_size = outer_size // 2
    block_width = signal.shape[1]
    shaped = signal.reshape(half_size, radix_size * block_width)
    first_re = jnp.dot(cos_one[:, :half_size], shaped, precision=HIGH).reshape(
        outer_size, radix_size, block_width
    )
    first_im = -jnp.dot(sin_one[:, :half_size], shaped, precision=HIGH).reshape(
        outer_size, radix_size, block_width
    )
    second_re = first_re * twist_cos + first_im * twist_sin
    second_im = first_im * twist_cos - first_re * twist_sin
    spec_re = jnp.einsum("amc,mb->abc", second_re, cos_two, precision=HIGH) + jnp.einsum(
        "amc,mb->abc", second_im, sin_two, precision=HIGH
    )
    spec_im = jnp.einsum("amc,mb->abc", second_im, cos_two, precision=HIGH) - jnp.einsum(
        "amc,mb->abc", second_re, sin_two, precision=HIGH
    )
    return (spec_re, spec_im)


def inverse_dft(spec_re, spec_im, tables, radix_size):
    cos_one, sin_one, twist_cos, twist_sin, cos_two, sin_two = tables
    outer_size = cos_one.shape[0]
    half_size = outer_size // 2
    block_width = spec_re.shape[2]
    back_re = jnp.einsum("abc,mb->amc", spec_re, cos_two, precision=HIGH) - jnp.einsum(
        "abc,mb->amc", spec_im, sin_two, precision=HIGH
    )
    back_im = jnp.einsum("abc,mb->amc", spec_re, sin_two, precision=HIGH) + jnp.einsum(
        "abc,mb->amc", spec_im, cos_two, precision=HIGH
    )
    turned_re = (back_re * twist_cos - back_im * twist_sin).reshape(
        outer_size, radix_size * block_width
    )
    turned_im = (back_re * twist_sin + back_im * twist_cos).reshape(
        outer_size, radix_size * block_width
    )
    result = jnp.dot(cos_one[:half_size], turned_re, precision=HIGH) - jnp.dot(
        sin_one[:half_size], turned_im, precision=HIGH
    )
    return result.reshape(half_size * radix_size, block_width) / (outer_size * radix_size)


def long_convolve_blocked(gated_slab, filter_slab):
    length, channels = gated_slab.shape
    block_width = min(128, channels)
    tables = dft_tables(length, RADIX)

    def one_block(block_index, output):
        offset = block_index * block_width
        signal = lax.dynamic_slice_in_dim(gated_slab, offset, block_width, 1).astype(jnp.float32)
        kernel_block = lax.dynamic_slice_in_dim(filter_slab, offset, block_width, 1).astype(
            jnp.float32
        )
        sig_re, sig_im = forward_dft(signal, tables, RADIX)
        ker_re, ker_im = forward_dft(kernel_block, tables, RADIX)
        prod_re = sig_re * ker_re - sig_im * ker_im
        prod_im = sig_re * ker_im + sig_im * ker_re
        result = inverse_dft(prod_re, prod_im, tables, RADIX)
        return lax.dynamic_update_slice_in_dim(output, result, offset, 1)

    return lax.fori_loop(
        0, channels // block_width, one_block, jnp.zeros((length, channels), jnp.float32)
    )


def long_convolve(gated_slab, filter_slab):
    length = gated_slab.shape[0]
    if length > 1024:
        return long_convolve_blocked(gated_slab, filter_slab)
    forward, backward = quarter_tables(length)
    sig = jnp.dot(forward, gated_slab, preferred_element_type=jnp.float32)
    ker = jnp.dot(forward, filter_slab, preferred_element_type=jnp.float32)
    sig_cos, sig_sin, ker_cos, ker_sin = sig[:length], sig[length:], ker[:length], ker[length:]
    prod = jnp.concatenate(
        [sig_cos * ker_cos - sig_sin * ker_sin, sig_cos * ker_sin + sig_sin * ker_cos]
    ).astype(jnp.bfloat16)
    return jnp.dot(backward, prod, preferred_element_type=jnp.float32)


def quarter_tables(length):
    steps = (4 * np.arange(length)[:, None] + 1) * np.arange(length)[None, :] % (4 * length)
    angles = steps * (2.0 * math.pi / (4 * length))
    table = np.concatenate([np.cos(angles), np.sin(angles)])
    return (jnp.asarray(table, jnp.bfloat16), jnp.asarray(table.T / length, jnp.bfloat16))


def make_response(gated_slab, filter_slab, skip_gain):
    long_part = long_convolve(gated_slab, filter_slab)
    return (long_part + skip_gain * gated_slab.astype(jnp.float32)).astype(jnp.bfloat16)


def combine_rows(query_part, response_part):
    return (query_part.astype(jnp.float32) * response_part.astype(jnp.float32)).astype(jnp.bfloat16)


def on_device_large(projected, short_taps, long_filter, skip_gain):
    kernel_size = short_taps.shape[0]
    ctx_size = lax.axis_size("ctx")
    rows = projected[0]
    filter_slab = lax.all_gather(long_filter, "dp", axis=0, tiled=True)
    all_taps = lax.all_gather(short_taps, "ctx", axis=2, tiled=True)
    halo = lax.ppermute(
        rows[-(kernel_size - 1) :], "ctx", [(i, i + 1) for i in range(ctx_size - 1)]
    )
    queries, gated = causal_short(jnp.concatenate([halo, rows]), all_taps, kernel_size)
    gated_slab = lax.all_to_all(gated, "ctx", split_axis=1, concat_axis=0, tiled=True)
    response_slab = make_response(gated_slab, filter_slab, skip_gain)
    response = lax.all_to_all(response_slab, "ctx", split_axis=0, concat_axis=1, tiled=True)
    return combine_rows(queries, response)[None]


CHUNK = 256
MESH = pl.DeviceIdType.MESH
ACROSS, DIAGONAL, SIBLING = 0, 1, 2
CROSS = (ACROSS, DIAGONAL)
TOP = 16


def ctx_offsets(ctx_size):
    pairs = [(a, b) for a in range(1, ctx_size // 2) for b in range(2)]
    return pairs + [(0, 1)]


def ctx_peer(me, offset, ctx_size, sign):
    half = ctx_size // 2
    chip = lax.rem(me // 2 + (half + sign * offset[0]) % half, half)
    core = lax.rem(lax.rem(me, 2) + offset[1], 2)
    return chip * 2 + core


def mixer_kernel(
    ctx_size,
    dp_size,
    x_hbm,
    taps_hbm,
    filter_hbm,
    skip_hbm,
    forward_hbm,
    backward_hbm,
    out_ref,
    x_ref,
    shared_x,
    tail_ref,
    skip_ref,
    forward_ref,
    backward_ref,
    own_taps,
    gate_rows,
    query_rows,
    gate_taps,
    query_taps,
    halo_out,
    halo_in,
    gated_out,
    gated_slab,
    filter_slab,
    spectrum,
    prod_ref,
    response_slab,
    response_in,
    queries,
    local_sem,
    taps_send,
    taps_recv,
    halo_send,
    halo_recv,
    zfil_send,
    zfil_recv,
    yfil_send,
    yfil_recv,
    gated_send,
    gated_recv,
    resp_send,
    resp_recv,
    filter_sem,
    ready_sem,
    shared_send,
    shared_recv,
):
    kernel_size = taps_hbm.shape[0]
    channels = taps_hbm.shape[2]
    rows = x_ref.shape[1]
    length = rows * ctx_size
    chunks = channels // CHUNK
    fil_rows = filter_hbm.shape[0]
    zsize = dp_size // 2
    turns = list(range(1, zsize))
    me = lax.axis_index("ctx")
    dp = lax.axis_index("dp")
    zpos, ypos = dp // 2, lax.rem(dp, 2)
    chip, core = me // 2, lax.rem(me, 2)
    first = 1 - chip
    offsets = ctx_offsets(ctx_size)
    dests = [ctx_peer(me, o, ctx_size, 1) for o in offsets]
    sources = [ctx_peer(me, o, ctx_size, -1) for o in offsets]
    ypeer = zpos * 2 + (1 - ypos)

    def signal(semaphore, **where):
        pl.semaphore_signal(semaphore, inc=1, device_id=where, device_id_type=MESH)

    barrier = pltpu.get_barrier_semaphore()
    for dest in dests:
        signal(barrier, ctx=dest)
    signal(barrier, dp=ypeer)
    for turn in turns:

        @pl.when(zpos + turn < zsize)
        def _(turn=turn):
            signal(barrier, dp=dp + 2 * turn)

    @pl.when(zpos > 0)
    def _():
        signal(barrier, dp=dp - 2)

    above = (zpos < zsize - 1).astype(jnp.int32)
    greeted = len(dests) + 1 + above + zpos

    def local_copy(source, target, index):
        copy = pltpu.make_async_copy(source, target, local_sem.at[index])
        copy.start()
        return copy

    own_taps_copy = local_copy(taps_hbm, own_taps, 0)
    shared_copies = []
    for side in range(2):
        owner = lax.rem(core + side, 2)
        columns = pl.ds(pl.multiple_of(owner * channels, channels), CHUNK)
        for gate in range(2):
            shared_copies.append(
                local_copy(
                    x_hbm.at[1 + gate, :, columns], shared_x.at[side, gate], 9 + 2 * side + gate
                )
            )
    tail_rows = tail_ref.shape[1]
    tail_copy = local_copy(x_hbm.at[:, pl.ds(rows - tail_rows, tail_rows), :], tail_ref, 1)

    shared = chunks
    slots = [first + k for k in range(chunks)]

    def filter_block(block, slot):
        return filter_slab.at[slot, pl.ds(pl.multiple_of(block * fil_rows, fil_rows), fil_rows), :]

    def own_filter_copy(chunk):
        slot = shared * first if chunk == 0 else chunk
        return pltpu.make_async_copy(
            filter_hbm.at[:, pl.ds(chunk * CHUNK, CHUNK)],
            filter_block(dp, slot),
            filter_sem.at[chunk],
        )

    for chunk in range(chunks):
        own_filter_copy(chunk).start()
    gate_copies = [local_copy(x_hbm.at[stream], x_ref.at[stream], 2 + stream) for stream in (1, 2)]
    skip_copy = local_copy(skip_hbm, skip_ref.at[:, pl.ds(0, channels)], 5)
    shared_skip = skip_ref.at[:, pl.ds(channels, CHUNK)]
    shared_skip_copy = pltpu.make_async_copy(
        skip_hbm.at[:, pl.ds(0, CHUNK)], shared_skip, local_sem.at[8]
    )

    @pl.when(chip == 0)
    def _():
        shared_skip_copy.start()

    def enter():
        pl.semaphore_wait(barrier, greeted)
        for turn in turns[1:]:

            @pl.when(zpos >= turn)
            def _(turn=turn):
                signal(ready_sem.at[turn], dp=dp - 2 * turn)

    def zfil_copy(turn, slot):
        target = lax.rem(zpos + turn, zsize)
        return pltpu.make_async_remote_copy(
            src_ref=filter_block(dp, slot),
            dst_ref=filter_block(dp, slot),
            send_sem=zfil_send.at[turn - 1, slot],
            recv_sem=zfil_recv.at[turn - 1, slot],
            device_id={"dp": target * 2 + ypos},
            device_id_type=MESH,
        )

    def yfil_copy(turn, slot):
        origin = lax.rem(zpos + zsize - turn, zsize)
        block = origin * 2 + ypos
        return pltpu.make_async_remote_copy(
            src_ref=filter_block(block, slot),
            dst_ref=filter_block(block, slot),
            send_sem=yfil_send.at[turn, slot],
            recv_sem=yfil_recv.at[turn, slot],
            device_id={"dp": ypeer},
            device_id_type=MESH,
        )

    def shared_filter_copy():
        return pltpu.make_async_remote_copy(
            src_ref=filter_block(dp, shared),
            dst_ref=filter_block(dp, shared),
            send_sem=shared_send.at[0],
            recv_sem=shared_recv.at[0],
            device_id={"ctx": dests[ACROSS]},
            device_id_type=MESH,
        )

    def shared_skip_send():
        return pltpu.make_async_remote_copy(
            src_ref=shared_skip,
            dst_ref=shared_skip,
            send_sem=shared_send.at[1],
            recv_sem=shared_recv.at[1],
            device_id={"ctx": dests[ACROSS]},
            device_id_type=MESH,
        )

    def relay_filter(slot):
        for turn in turns:
            zfil_copy(turn, slot).wait_recv()
            yfil_copy(turn, slot).start()

    def send_up(turn, slot):
        @pl.when(zpos + turn < zsize)
        def _():
            zfil_copy(turn, slot).start()

    def send_down(turn, slot):
        @pl.when(zpos + turn >= zsize)
        def _():
            zfil_copy(turn, slot).start()

    def wait_up(turn):
        @pl.when(zpos + turn < zsize)
        def _():
            pl.semaphore_wait(ready_sem.at[turn], 1)

    def send_near_filter():
        for chunk in range(chunks):
            own_filter_copy(chunk).wait()
        for slot in slots:
            for turn in turns:
                send_down(turn, slot)
            yfil_copy(0, slot).start()
        for slot in slots[:2]:
            send_up(1, slot)

    @pl.when(chip == 1)
    def _():
        enter()
        send_near_filter()

    halo_copy = pltpu.make_async_remote_copy(
        src_ref=halo_out,
        dst_ref=halo_in,
        send_sem=halo_send,
        recv_sem=halo_recv,
        device_id={"ctx": lax.rem(me + 1, ctx_size)},
        device_id_type=MESH,
    )
    has_following, has_previous = me < ctx_size - 1, me > 0
    tail_copy.wait()

    @pl.when(has_following)
    def _():
        halo_out[...] = tail_ref[:, tail_rows - (kernel_size - 1) :, :]

    own_taps_copy.wait()
    gate_rows[...] = jnp.zeros_like(gate_rows)
    query_rows[...] = jnp.zeros_like(query_rows)
    for tap in range(kernel_size):
        query_rows[tap : tap + 1, :] = own_taps[tap, 0:1, :]
        for gate in range(2):
            row = gate * kernel_size + tap
            gate_rows[row : row + 1, :] = own_taps[tap, 1 + gate : 2 + gate, :]
    gate_taps[me] = gate_rows[...].astype(jnp.bfloat16)
    query_taps[me] = query_rows[...].astype(jnp.bfloat16)

    def short_filter(stream, owner, chunk, values, edged=True):
        columns = pl.ds(pl.multiple_of(owner * channels + chunk * CHUNK, CHUNK), CHUNK)
        taps_columns = pl.ds(pl.multiple_of(chunk * CHUNK, CHUNK), CHUNK)
        values = values.astype(jnp.float32)
        if stream == 0:
            weights = query_taps[owner, :, taps_columns].astype(jnp.float32)
        else:
            weights = gate_taps[owner, :, taps_columns].astype(jnp.float32)
            weights = weights[(stream - 1) * kernel_size : stream * kernel_size]
        if edged:
            edge = halo_in[stream, :, columns].astype(jnp.float32)
            edge = jnp.where(has_previous, edge, jnp.zeros_like(edge))
            row_index = lax.broadcasted_iota(jnp.int32, (8, CHUNK), 0)
        total = weights[0:1] * values
        for tap in range(1, kernel_size):
            moved = pltpu.roll(values, tap, 0)
            if edged:
                top = moved[:8]
                for row in range(tap):
                    at = kernel_size - 1 + row - tap
                    top = jnp.where(row_index == row, edge[at : at + 1], top)
                moved = jnp.concatenate([top, moved[8:]], axis=0)
            total = total + weights[tap : tap + 1] * moved
        return total

    def x_columns(stream, owner, chunk):
        columns = pl.ds(pl.multiple_of(owner * channels + chunk * CHUNK, CHUNK), CHUNK)
        return x_ref[stream, :, columns]

    def gated_rows(owner, chunk):
        keys, values = (
            short_filter(stream, owner, chunk, x_columns(stream, owner, chunk)) for stream in (1, 2)
        )
        return (keys * values).astype(jnp.bfloat16)

    def shared_gated_rows(side, count=rows, edged=True):
        owner = lax.rem(core + side, 2)
        keys, values = (
            short_filter(1 + gate, owner, 0, shared_x[side, gate, :count, :], edged)
            for gate in range(2)
        )
        return (keys * values).astype(jnp.bfloat16)

    def position_rows(owner):
        return pl.ds(pl.multiple_of(owner * rows, rows), rows)

    body_rows = pl.ds(pl.multiple_of(me * rows + TOP, TOP), rows - TOP)
    top_rows = pl.ds(pl.multiple_of(me * rows, rows), TOP)

    for copy in shared_copies:
        copy.wait()

    @pl.when(chip == 0)
    def _():
        gated_slab[shared, body_rows, :] = shared_gated_rows(0, edged=False)[TOP:]

    def shared_part_copy(part, part_rows):
        return pltpu.make_async_remote_copy(
            src_ref=gated_slab.at[shared, part_rows, :],
            dst_ref=gated_slab.at[shared, part_rows, :],
            send_sem=shared_send.at[part],
            recv_sem=shared_recv.at[part],
            device_id={"ctx": dests[ACROSS]},
            device_id_type=MESH,
        )

    def shared_body_copy():
        return shared_part_copy(2, body_rows)

    def shared_top_copy():
        return shared_part_copy(3, top_rows)

    @pl.when(chip == 0)
    def _():
        enter()

    @pl.when(has_following)
    def _():
        halo_copy.start()

    def taps_copy(i, slot, kind=0):
        taps = (gate_taps, query_taps)[kind]
        return pltpu.make_async_remote_copy(
            src_ref=taps.at[slot],
            dst_ref=taps.at[slot],
            send_sem=taps_send.at[kind, i],
            recv_sem=taps_recv.at[kind, i],
            device_id={"ctx": dests[ACROSS] if i == ACROSS else dests[SIBLING]},
            device_id_type=MESH,
        )

    for i in (ACROSS, SIBLING):
        taps_copy(i, me).start()

    def send_query_taps():
        for i in (ACROSS, SIBLING):
            taps_copy(i, me, 1).start()

    @pl.when(chip == 1)
    def _():
        send_query_taps()

    @pl.when(chip == 0)
    def _():
        shared_body_copy().start()
        send_near_filter()

    def gated_copy(i, slot, owner, source=None):
        return pltpu.make_async_remote_copy(
            src_ref=gated_out.at[i, slot] if source is None else source,
            dst_ref=gated_slab.at[slot, position_rows(owner), :],
            send_sem=gated_send.at[i, slot],
            recv_sem=gated_recv.at[i, slot],
            device_id={"ctx": dests[i]},
            device_id_type=MESH,
        )

    def response_copy(i, slot):
        return pltpu.make_async_remote_copy(
            src_ref=response_slab.at[slot, position_rows(dests[i]), :],
            dst_ref=response_in.at[i, slot],
            send_sem=resp_send.at[i, slot],
            recv_sem=resp_recv.at[i, slot],
            device_id={"ctx": dests[i]},
            device_id_type=MESH,
        )

    def push_gated(i, chunk):
        gated_out[i, chunk] = gated_rows(dests[i], chunk)
        gated_copy(i, chunk, me).start()

    def push_near(chunk):
        push_gated(SIBLING, chunk)
        gated_slab[chunk, position_rows(me), :] = gated_rows(me, chunk)

    def shared_own():
        gated_slab[shared, position_rows(me), :] = shared_gated_rows(0)

    def shared_other():
        gated_out[SIBLING, shared] = shared_gated_rows(1)
        gated_copy(SIBLING, shared, me).start()

    taps_copy(SIBLING, sources[SIBLING]).wait_recv()

    @pl.when(jnp.logical_and(chip == 0, has_previous))
    def _():
        halo_copy.wait_recv()

    @pl.when(chip == 0)
    def _():
        gated_slab[shared, top_rows, :] = shared_gated_rows(0, TOP)
        shared_top_copy().start()
        shared_other()
        gated_copy(DIAGONAL, shared, me, gated_out.at[SIBLING, shared]).start()
        send_query_taps()
        shared_filter_copy().start()
        shared_skip_copy.wait()
        shared_skip_send().start()
        half = length // 2
        gated_slab[shared, half:] = jnp.zeros((length - half, CHUNK), jnp.bfloat16)

    late_copies = [
        local_copy(x_hbm.at[0], x_ref.at[0], 2),
        local_copy(forward_hbm, forward_ref, 6),
        local_copy(backward_hbm, backward_ref, 7),
        skip_copy,
    ]

    def send_far_up():
        for turn in turns[1:]:
            wait_up(turn)
        for k, slot in enumerate(slots):
            for turn in reversed(turns):
                if turn > 1 or k > 1:
                    send_up(turn, slot)

    @pl.when(chip == 1)
    def _():
        send_far_up()

    for copy in gate_copies:
        copy.wait()
    taps_copy(ACROSS, sources[ACROSS]).wait_recv()
    taps_copy(DIAGONAL, sources[ACROSS]).start()

    @pl.when(chip == 1)
    def _():
        halo_copy.wait_recv()

    push_gated(ACROSS, chip)
    taps_copy(DIAGONAL, sources[DIAGONAL]).wait_recv()
    push_gated(DIAGONAL, chip)

    @pl.when(chip == 0)
    def _():
        send_far_up()

    push_near(first)
    def push_chunk(step, carry):
        @pl.when(chip + step < chunks)
        def _():
            push_gated(ACROSS, chip + step)
            push_gated(DIAGONAL, chip + step)

        @pl.when(first + step < chunks)
        def _():
            push_near(first + step)

        return carry

    lax.fori_loop(1, 2, push_chunk, 0)
    taps_copy(ACROSS, sources[ACROSS], 1).wait_recv()
    taps_copy(DIAGONAL, sources[ACROSS], 1).start()
    lax.fori_loop(2, 3, push_chunk, 0)
    relay_filter(first)
    lax.fori_loop(3, chunks, push_chunk, 0)

    @pl.when(chip == 1)
    def _():
        shared_own()
        shared_other()

    for copy in late_copies:
        copy.wait()

    def fill_queries(chunk, carry):
        def one_owner(owner, inner):
            queries[owner, chunk] = short_filter(0, owner, chunk, x_columns(0, owner, chunk)).astype(
                jnp.bfloat16
            )
            return inner

        return lax.fori_loop(0, ctx_size, one_owner, carry)

    @pl.when(chip == 1)
    def _():
        shared_filter_copy().wait_recv()
        shared_skip_send().wait_recv()
        yfil_copy(0, shared).start()
        for turn in turns:
            zfil_copy(turn, shared).start()

    taps_copy(SIBLING, sources[SIBLING], 1).wait_recv()
    taps_copy(DIAGONAL, sources[DIAGONAL], 1).wait_recv()
    lax.fori_loop(0, chunks, fill_queries, 0)
    relay_filter(first + 1)

    def mix_into(owner, chunk, response):
        columns = pl.ds(pl.multiple_of(owner * channels + chunk * CHUNK, CHUNK), CHUNK)
        mixed = queries[owner, chunk].astype(jnp.float32) * response.astype(jnp.float32)
        out_ref[:, columns] = mixed.astype(jnp.bfloat16)

    def convolve(slot, carry):
        columns = pl.ds(pl.multiple_of(slot * CHUNK, CHUNK), CHUNK)

        @pl.when(slot < shared)
        def _():
            gated_copy(ACROSS, slot, sources[ACROSS]).wait_recv()

        @pl.when(jnp.logical_and(slot == shared, chip == 1))
        def _():
            shared_body_copy().wait_recv()
            shared_top_copy().wait_recv()

        @pl.when(jnp.logical_or(slot < shared, chip == 1))
        def _():
            gated_copy(DIAGONAL, slot, sources[DIAGONAL]).wait_recv()

        gated_copy(SIBLING, slot, sources[SIBLING]).wait_recv()
        gated = gated_slab[slot]
        spectrum[...] = jnp.dot(forward_ref[...], gated, preferred_element_type=jnp.float32)
        for turn in range(zsize):
            yfil_copy(turn, slot).wait_recv()
        taps = filter_slab[slot]
        ker_cos = jnp.dot(forward_ref[:length], taps, preferred_element_type=jnp.float32)
        ker_sin = jnp.dot(forward_ref[length:], taps, preferred_element_type=jnp.float32)
        sig_cos, sig_sin = spectrum[:length], spectrum[length:]
        prod_ref[:length] = (sig_cos * ker_cos - sig_sin * ker_sin).astype(jnp.bfloat16)
        prod_ref[length:] = (sig_cos * ker_sin + sig_sin * ker_cos).astype(jnp.bfloat16)
        long_part = jnp.dot(backward_ref[...], prod_ref[...], preferred_element_type=jnp.float32)
        direct_part = skip_ref[:, columns] * gated.astype(jnp.float32)
        response_slab[slot] = (long_part + direct_part).astype(jnp.bfloat16)

        @pl.when(slot < shared)
        def _():
            for i in CROSS:
                response_copy(i, slot).start()

        response_copy(SIBLING, slot).start()

        @pl.when(slot + 2 <= shared)
        def _():
            relay_filter(slot + 2)

        response = response_slab[slot, position_rows(me), :]

        @pl.when(slot < shared)
        def _():
            mix_into(me, slot, response)

        @pl.when(slot == shared)
        def _():
            mix_into(core, 0, response)

        return carry

    lax.fori_loop(first, shared + 1, convolve, 0)

    def finish_near(chunk, carry):
        response_copy(SIBLING, chunk).wait_recv()
        mix_into(sources[SIBLING], chunk, response_in[SIBLING, chunk])
        return carry

    def finish_cross(chunk, carry):
        for i in CROSS:
            response_copy(i, chunk).wait_recv()
            mix_into(sources[i], chunk, response_in[i, chunk])
        return carry

    lax.fori_loop(first, chunks, finish_near, 0)
    response_copy(SIBLING, shared).wait_recv()
    mix_into(1 - core, 0, response_in[SIBLING, shared])
    lax.fori_loop(chip, chunks, finish_cross, 0)

    def drain_gated(chunk, carry):
        for i in CROSS:
            gated_copy(i, chunk, me).wait_send()
        return carry

    def drain_response(slot, carry):
        for i in CROSS:
            response_copy(i, slot).wait_send()
        return carry

    def drain_near(slot, carry):
        gated_copy(SIBLING, slot, me).wait_send()
        response_copy(SIBLING, slot).wait_send()
        for turn in turns:
            zfil_copy(turn, slot).wait_send()
        for turn in range(zsize):
            yfil_copy(turn, slot).wait_send()
        return carry

    lax.fori_loop(chip, chunks, drain_gated, 0)
    lax.fori_loop(first, chunks, drain_response, 0)
    lax.fori_loop(first, shared + 1, drain_near, 0)

    @pl.when(chip == 0)
    def _():
        shared_body_copy().wait_send()
        shared_top_copy().wait_send()
        gated_copy(DIAGONAL, shared, me, gated_out.at[SIBLING, shared]).wait_send()
        shared_filter_copy().wait_send()
        shared_skip_send().wait_send()

    for kind in range(2):
        for i in (ACROSS, SIBLING, DIAGONAL):
            taps_copy(i, me, kind).wait_send()

    @pl.when(has_following)
    def _():
        halo_copy.wait_send()


def write_kernel(mixed_ref, out_hbm, sem):
    copy = pltpu.make_async_copy(mixed_ref, out_hbm, sem)
    copy.start()
    copy.wait()


def write_out(mixed):
    return pl.pallas_call(
        write_kernel,
        out_shape=jax.ShapeDtypeStruct(mixed.shape, mixed.dtype),
        in_specs=[pl.BlockSpec(memory_space=pltpu.VMEM)],
        out_specs=pl.BlockSpec(memory_space=pltpu.HBM),
        scratch_shapes=[pltpu.SemaphoreType.DMA],
    )(pltpu.with_memory_space_constraint(mixed, pltpu.VMEM))


def on_device(projected, short_taps, long_filter, skip_gain):
    ctx_size, dp_size = lax.axis_size("ctx"), lax.axis_size("dp")
    kernel_size, streams, channels = short_taps.shape
    rows, width = projected.shape[1], projected.shape[3]
    length = rows * ctx_size
    regular = ctx_size == 4 and dp_size % 2 == 0 and dp_size >= 6
    regular = regular and channels % CHUNK == 0 and channels >= 2 * CHUNK and kernel_size <= 4
    if length > 1024 or not regular:
        return on_device_large(projected, short_taps, long_filter, skip_gain)
    forward, backward = quarter_tables(length)
    chunks = channels // CHUNK
    slots = chunks + 1
    peers = ctx_size - 1
    zsize = dp_size // 2
    hbm_spec = pl.BlockSpec(memory_space=pltpu.HBM)
    dma = pltpu.SemaphoreType.DMA
    operands = (
        projected[0].transpose(1, 0, 2),
        short_taps,
        long_filter,
        skip_gain[None],
        forward,
        backward,
    )
    mixed = pl.pallas_call(
        functools.partial(mixer_kernel, ctx_size, dp_size),
        out_shape=pltpu.VMEM((rows, width), jnp.bfloat16),
        in_specs=[hbm_spec] * len(operands),
        out_specs=pl.BlockSpec(memory_space=pltpu.VMEM),
        scratch_shapes=[
            pltpu.VMEM((streams, rows, width), jnp.bfloat16),
            pltpu.VMEM((2, 2, rows, CHUNK), jnp.bfloat16),
            pltpu.VMEM((streams, 16, width), jnp.bfloat16),
            pltpu.VMEM((1, channels + CHUNK), jnp.float32),
            pltpu.VMEM(forward.shape, jnp.bfloat16),
            pltpu.VMEM(backward.shape, jnp.bfloat16),
            pltpu.VMEM((kernel_size, streams, channels), jnp.float32),
            pltpu.VMEM((8, channels), jnp.float32),
            pltpu.VMEM((4, channels), jnp.float32),
            pltpu.VMEM((ctx_size, 8, channels), jnp.bfloat16),
            pltpu.VMEM((ctx_size, 4, channels), jnp.bfloat16),
            pltpu.VMEM((streams, kernel_size - 1, width), jnp.bfloat16),
            pltpu.VMEM((streams, kernel_size - 1, width), jnp.bfloat16),
            pltpu.VMEM((peers, slots, rows, CHUNK), jnp.bfloat16),
            pltpu.VMEM((slots, length, CHUNK), jnp.bfloat16),
            pltpu.VMEM((slots, length, CHUNK), jnp.bfloat16),
            pltpu.VMEM((2 * length, CHUNK), jnp.float32),
            pltpu.VMEM((2 * length, CHUNK), jnp.bfloat16),
            pltpu.VMEM((slots, length, CHUNK), jnp.bfloat16),
            pltpu.VMEM((peers, slots, rows, CHUNK), jnp.bfloat16),
            pltpu.VMEM((ctx_size, chunks, rows, CHUNK), jnp.bfloat16),
            dma((13,)),
            dma((2, peers)),
            dma((2, peers)),
            dma,
            dma,
            dma((zsize - 1, slots)),
            dma((zsize - 1, slots)),
            dma((zsize, slots)),
            dma((zsize, slots)),
            dma((peers, slots)),
            dma((peers, slots)),
            dma((peers, slots)),
            dma((peers, slots)),
            dma((chunks,)),
            pltpu.SemaphoreType.REGULAR((zsize,)),
            dma((4,)),
            dma((4,)),
        ],
        compiler_params=pltpu.CompilerParams(
            collective_id=0, has_side_effects=True, vmem_limit_bytes=40 * 2**20
        ),
    )(*(pltpu.with_memory_space_constraint(array, pltpu.HBM) for array in operands))
    return write_out(mixed)[None]


def solution(mesh):
    return jax.shard_map(
        on_device,
        mesh=mesh,
        in_specs=(P("dp", "ctx", None, None), P(None, None, "ctx"), P("dp", "ctx"), P("ctx")),
        out_specs=P("dp", "ctx", None),
        check_vma=False,
    )
```

```python
import functools
import math

import jax
import jax.numpy as jnp
import numpy as np
from jax import lax
from jax.experimental import pallas as pl
from jax.experimental.pallas import tpu as pltpu
from jax.sharding import PartitionSpec as P

RADIX = 64


HIGH = lax.Precision.HIGHEST


def causal_short(extended, taps, kernel_size):
    row_count = extended.shape[0] - (kernel_size - 1)
    widened = extended.astype(jnp.float32)
    summed = jnp.zeros((row_count,) + widened.shape[1:], jnp.float32)
    for tap_index in range(kernel_size):
        offset = kernel_size - 1 - tap_index
        summed = summed + taps[tap_index] * widened[offset : offset + row_count]
    return (summed[:, 0].astype(jnp.bfloat16), (summed[:, 1] * summed[:, 2]).astype(jnp.bfloat16))


def dft_tables(length, radix_size):
    outer_size = 2 * length // radix_size
    total_size = outer_size * radix_size
    outer_range = jnp.arange(outer_size, dtype=jnp.int32)
    inner_range = jnp.arange(radix_size, dtype=jnp.int32)
    angle_one = (
        2.0
        * math.pi
        / outer_size
        * (outer_range[:, None] * outer_range[None, :] % outer_size).astype(jnp.float32)
    )
    angle_twist = (
        2.0
        * math.pi
        / total_size
        * (outer_range[:, None] * inner_range[None, :] % total_size).astype(jnp.float32)
    )
    angle_two = (
        2.0
        * math.pi
        / radix_size
        * (inner_range[:, None] * inner_range[None, :] % radix_size).astype(jnp.float32)
    )
    twist_cos = jnp.cos(angle_twist)[:, :, None]
    twist_sin = jnp.sin(angle_twist)[:, :, None]
    return (
        jnp.cos(angle_one),
        jnp.sin(angle_one),
        twist_cos,
        twist_sin,
        jnp.cos(angle_two),
        jnp.sin(angle_two),
    )


def forward_dft(signal, tables, radix_size):
    cos_one, sin_one, twist_cos, twist_sin, cos_two, sin_two = tables
    outer_size = cos_one.shape[0]
    half_size = outer_size // 2
    block_width = signal.shape[1]
    shaped = signal.reshape(half_size, radix_size * block_width)
    first_re = jnp.dot(cos_one[:, :half_size], shaped, precision=HIGH).reshape(
        outer_size, radix_size, block_width
    )
    first_im = -jnp.dot(sin_one[:, :half_size], shaped, precision=HIGH).reshape(
        outer_size, radix_size, block_width
    )
    second_re = first_re * twist_cos + first_im * twist_sin
    second_im = first_im * twist_cos - first_re * twist_sin
    spec_re = jnp.einsum("amc,mb->abc", second_re, cos_two, precision=HIGH) + jnp.einsum(
        "amc,mb->abc", second_im, sin_two, precision=HIGH
    )
    spec_im = jnp.einsum("amc,mb->abc", second_im, cos_two, precision=HIGH) - jnp.einsum(
        "amc,mb->abc", second_re, sin_two, precision=HIGH
    )
    return (spec_re, spec_im)


def inverse_dft(spec_re, spec_im, tables, radix_size):
    cos_one, sin_one, twist_cos, twist_sin, cos_two, sin_two = tables
    outer_size = cos_one.shape[0]
    half_size = outer_size // 2
    block_width = spec_re.shape[2]
    back_re = jnp.einsum("abc,mb->amc", spec_re, cos_two, precision=HIGH) - jnp.einsum(
        "abc,mb->amc", spec_im, sin_two, precision=HIGH
    )
    back_im = jnp.einsum("abc,mb->amc", spec_re, sin_two, precision=HIGH) + jnp.einsum(
        "abc,mb->amc", spec_im, cos_two, precision=HIGH
    )
    turned_re = (back_re * twist_cos - back_im * twist_sin).reshape(
        outer_size, radix_size * block_width
    )
    turned_im = (back_re * twist_sin + back_im * twist_cos).reshape(
        outer_size, radix_size * block_width
    )
    result = jnp.dot(cos_one[:half_size], turned_re, precision=HIGH) - jnp.dot(
        sin_one[:half_size], turned_im, precision=HIGH
    )
    return result.reshape(half_size * radix_size, block_width) / (outer_size * radix_size)


def long_convolve_blocked(gated_slab, filter_slab):
    length, channels = gated_slab.shape
    block_width = min(128, channels)
    tables = dft_tables(length, RADIX)

    def one_block(block_index, output):
        offset = block_index * block_width
        signal = lax.dynamic_slice_in_dim(gated_slab, offset, block_width, 1).astype(jnp.float32)
        kernel_block = lax.dynamic_slice_in_dim(filter_slab, offset, block_width, 1).astype(
            jnp.float32
        )
        sig_re, sig_im = forward_dft(signal, tables, RADIX)
        ker_re, ker_im = forward_dft(kernel_block, tables, RADIX)
        prod_re = sig_re * ker_re - sig_im * ker_im
        prod_im = sig_re * ker_im + sig_im * ker_re
        result = inverse_dft(prod_re, prod_im, tables, RADIX)
        return lax.dynamic_update_slice_in_dim(output, result, offset, 1)

    return lax.fori_loop(
        0, channels // block_width, one_block, jnp.zeros((length, channels), jnp.float32)
    )


def long_convolve(gated_slab, filter_slab):
    length = gated_slab.shape[0]
    if length > 1024:
        return long_convolve_blocked(gated_slab, filter_slab)
    forward, backward = quarter_tables(length)
    sig = jnp.dot(forward, gated_slab, preferred_element_type=jnp.float32)
    ker = jnp.dot(forward, filter_slab, preferred_element_type=jnp.float32)
    sig_cos, sig_sin, ker_cos, ker_sin = sig[:length], sig[length:], ker[:length], ker[length:]
    prod = jnp.concatenate(
        [sig_cos * ker_cos - sig_sin * ker_sin, sig_cos * ker_sin + sig_sin * ker_cos]
    ).astype(jnp.bfloat16)
    return jnp.dot(backward, prod, preferred_element_type=jnp.float32)


def quarter_tables(length):
    steps = (4 * np.arange(length)[:, None] + 1) * np.arange(length)[None, :] % (4 * length)
    angles = steps * (2.0 * math.pi / (4 * length))
    table = np.concatenate([np.cos(angles), np.sin(angles)])
    return (jnp.asarray(table, jnp.bfloat16), jnp.asarray(table.T / length, jnp.bfloat16))


def make_response(gated_slab, filter_slab, skip_gain):
    long_part = long_convolve(gated_slab, filter_slab)
    return (long_part + skip_gain * gated_slab.astype(jnp.float32)).astype(jnp.bfloat16)


def combine_rows(query_part, response_part):
    return (query_part.astype(jnp.float32) * response_part.astype(jnp.float32)).astype(jnp.bfloat16)


def on_device_large(projected, short_taps, long_filter, skip_gain):
    kernel_size = short_taps.shape[0]
    ctx_size = lax.axis_size("ctx")
    rows = projected[0]
    filter_slab = lax.all_gather(long_filter, "dp", axis=0, tiled=True)
    all_taps = lax.all_gather(short_taps, "ctx", axis=2, tiled=True)
    halo = lax.ppermute(
        rows[-(kernel_size - 1) :], "ctx", [(i, i + 1) for i in range(ctx_size - 1)]
    )
    queries, gated = causal_short(jnp.concatenate([halo, rows]), all_taps, kernel_size)
    gated_slab = lax.all_to_all(gated, "ctx", split_axis=1, concat_axis=0, tiled=True)
    response_slab = make_response(gated_slab, filter_slab, skip_gain)
    response = lax.all_to_all(response_slab, "ctx", split_axis=0, concat_axis=1, tiled=True)
    return combine_rows(queries, response)[None]


CHUNK = 256
MESH = pl.DeviceIdType.MESH
ACROSS, DIAGONAL, SIBLING = 0, 1, 2
CROSS = (ACROSS, DIAGONAL)
TOP = 16


def ctx_offsets(ctx_size):
    pairs = [(a, b) for a in range(1, ctx_size // 2) for b in range(2)]
    return pairs + [(0, 1)]


def ctx_peer(me, offset, ctx_size, sign):
    half = ctx_size // 2
    chip = lax.rem(me // 2 + (half + sign * offset[0]) % half, half)
    core = lax.rem(lax.rem(me, 2) + offset[1], 2)
    return chip * 2 + core


def mixer_kernel(
    ctx_size,
    dp_size,
    x_hbm,
    taps_hbm,
    filter_hbm,
    skip_hbm,
    forward_hbm,
    backward_hbm,
    out_ref,
    x_ref,
    shared_x,
    tail_ref,
    skip_ref,
    forward_ref,
    backward_ref,
    own_taps,
    gate_rows,
    query_rows,
    gate_taps,
    query_taps,
    halo_out,
    halo_in,
    gated_out,
    gated_slab,
    filter_slab,
    spectrum,
    prod_ref,
    response_slab,
    response_in,
    queries,
    local_sem,
    taps_send,
    taps_recv,
    halo_send,
    halo_recv,
    zfil_send,
    zfil_recv,
    yfil_send,
    yfil_recv,
    gated_send,
    gated_recv,
    resp_send,
    resp_recv,
    ready_sem,
    shared_send,
    shared_recv,
):
    kernel_size = taps_hbm.shape[0]
    channels = taps_hbm.shape[2]
    rows = x_ref.shape[1]
    length = rows * ctx_size
    chunks = channels // CHUNK
    fil_rows = filter_hbm.shape[0]
    zsize = dp_size // 2
    turns = list(range(1, zsize))
    me = lax.axis_index("ctx")
    dp = lax.axis_index("dp")
    zpos, ypos = dp // 2, lax.rem(dp, 2)
    chip, core = me // 2, lax.rem(me, 2)
    first = 1 - chip
    offsets = ctx_offsets(ctx_size)
    dests = [ctx_peer(me, o, ctx_size, 1) for o in offsets]
    sources = [ctx_peer(me, o, ctx_size, -1) for o in offsets]
    ypeer = zpos * 2 + (1 - ypos)

    def signal(semaphore, **where):
        pl.semaphore_signal(semaphore, inc=1, device_id=where, device_id_type=MESH)

    barrier = pltpu.get_barrier_semaphore()
    for dest in dests:
        signal(barrier, ctx=dest)
    above = (zpos < zsize - 1).astype(jnp.int32)
    greeted = len(dests) + 1 + above + zpos

    def wait_all(ref, semaphore):
        pltpu.make_async_copy(ref, ref, semaphore).wait()

    def wait_rows(ref, count, semaphore):
        wait_all(ref.at[pl.ds(0, 4), pl.ds(0, count // 4), :], semaphore)

    def by_chip(wait, on_first, on_second):
        for which, count in enumerate((on_first, on_second)):

            @pl.when(chip == which)
            def _(count=count):
                wait(count)

    def local_copy(source, target, index):
        copy = pltpu.make_async_copy(source, target, local_sem.at[index])
        copy.start()
        return copy

    own_taps_copy = local_copy(taps_hbm, own_taps, 0)
    for side in range(2):
        owner = lax.rem(core + side, 2)
        columns = pl.ds(pl.multiple_of(owner * channels, channels), CHUNK)
        local_copy(x_hbm.at[pl.ds(1, 2), :, columns], shared_x.at[side], 4)
    tail_rows = tail_ref.shape[1]
    tail_copy = local_copy(x_hbm.at[:, pl.ds(rows - tail_rows, tail_rows), :], tail_ref, 1)
    gate_copies = [local_copy(x_hbm.at[pl.ds(1, 2)], x_ref.at[pl.ds(1, 2)], 3)]
    signal(barrier, dp=ypeer)
    for turn in turns:

        @pl.when(zpos + turn < zsize)
        def _(turn=turn):
            signal(barrier, dp=dp + 2 * turn)

    @pl.when(zpos > 0)
    def _():
        signal(barrier, dp=dp - 2)


    shared = chunks
    slots = [first + k for k in range(chunks)]

    def filter_block(block, slot):
        return filter_slab.at[slot, pl.ds(pl.multiple_of(block * fil_rows, fil_rows), fil_rows), :]

    def own_filter(slot):
        chunk = lax.rem(slot, chunks)
        return filter_hbm.at[:, pl.ds(pl.multiple_of(chunk * CHUNK, CHUNK), CHUNK)]

    def own_filter_copy(k):
        return pltpu.make_async_copy(
            own_filter(slots[k]), filter_block(dp, slots[k]), local_sem.at[9]
        )

    shared_skip = skip_ref.at[:, pl.ds(channels, CHUNK)]
    first_skip = skip_hbm.at[:, pl.ds(0, CHUNK)]
    shared_skip_copy = pltpu.make_async_copy(first_skip, shared_skip, local_sem.at[8])

    def enter():
        pl.semaphore_wait(barrier, greeted)
        for turn in turns[1:]:

            @pl.when(zpos >= turn)
            def _(turn=turn):
                signal(ready_sem.at[turn - 2], dp=dp - 2 * turn)

    def zfil_copy(turn, slot, source=None):
        target = lax.rem(zpos + turn, zsize)
        return pltpu.make_async_remote_copy(
            src_ref=filter_block(dp, slot) if source is None else source,
            dst_ref=filter_block(dp, slot),
            send_sem=zfil_send,
            recv_sem=zfil_recv.at[slot],
            device_id={"dp": target * 2 + ypos},
            device_id_type=MESH,
        )

    def yfil_copy(turn, slot, source=None):
        origin = lax.rem(zpos + zsize - turn, zsize)
        block = origin * 2 + ypos
        return pltpu.make_async_remote_copy(
            src_ref=filter_block(block, slot) if source is None else source,
            dst_ref=filter_block(block, slot),
            send_sem=yfil_send,
            recv_sem=yfil_recv.at[slot],
            device_id={"dp": ypeer},
            device_id_type=MESH,
        )

    def shared_filter_copy():
        return pltpu.make_async_remote_copy(
            src_ref=own_filter(shared),
            dst_ref=filter_block(dp, shared),
            send_sem=shared_send.at[0],
            recv_sem=shared_recv.at[0],
            device_id={"ctx": dests[ACROSS]},
            device_id_type=MESH,
        )

    def shared_skip_send():
        return pltpu.make_async_remote_copy(
            src_ref=first_skip,
            dst_ref=shared_skip,
            send_sem=shared_send.at[1],
            recv_sem=shared_recv.at[1],
            device_id={"ctx": dests[ACROSS]},
            device_id_type=MESH,
        )

    def relay_filter(slot):
        wait_all(filter_slab.at[slot, pl.ds(0, len(turns) * fil_rows), :], zfil_recv.at[slot])
        for turn in turns:
            yfil_copy(turn, slot).start()

    def send_up(turn, slot):
        @pl.when(zpos + turn < zsize)
        def _():
            zfil_copy(turn, slot, own_filter(slot)).start()

    def send_down(turn, slot):
        @pl.when(zpos + turn >= zsize)
        def _():
            zfil_copy(turn, slot, own_filter(slot)).start()

    def wait_up(turn):
        @pl.when(zpos + turn < zsize)
        def _():
            pl.semaphore_wait(ready_sem.at[turn - 2], 1)

    def send_near_filter(steps):
        for k in steps:
            slot = slots[k]
            for turn in turns:
                send_down(turn, slot)
            yfil_copy(0, slot, own_filter(slot)).start()
            if k < 2:
                send_up(1, slot)

    @pl.when(chip == 1)
    def _():
        enter()
        send_near_filter(range(1))

    halo_copy = pltpu.make_async_remote_copy(
        src_ref=halo_out,
        dst_ref=halo_in,
        send_sem=halo_send,
        recv_sem=halo_recv,
        device_id={"ctx": lax.rem(me + 1, ctx_size)},
        device_id_type=MESH,
    )
    has_following, has_previous = me < ctx_size - 1, me > 0
    tail_copy.wait()

    @pl.when(has_following)
    def _():
        halo_out[...] = tail_ref[:, tail_rows - (kernel_size - 1) :, :]

    own_taps_copy.wait()
    gate_rows[...] = jnp.zeros_like(gate_rows)
    query_rows[...] = jnp.zeros_like(query_rows)
    for tap in range(kernel_size):
        query_rows[tap : tap + 1, :] = own_taps[tap, 0:1, :]
        for gate in range(2):
            row = gate * kernel_size + tap
            gate_rows[row : row + 1, :] = own_taps[tap, 1 + gate : 2 + gate, :]
    gate_taps[me] = gate_rows[...].astype(jnp.bfloat16)
    query_taps[me] = query_rows[...].astype(jnp.bfloat16)

    def short_filter(stream, owner, chunk, values, edged=True):
        columns = pl.ds(pl.multiple_of(owner * channels + chunk * CHUNK, CHUNK), CHUNK)
        taps_columns = pl.ds(pl.multiple_of(chunk * CHUNK, CHUNK), CHUNK)
        values = values.astype(jnp.float32)
        if stream == 0:
            weights = query_taps[owner, :, taps_columns].astype(jnp.float32)
        else:
            weights = gate_taps[owner, :, taps_columns].astype(jnp.float32)
            weights = weights[(stream - 1) * kernel_size : stream * kernel_size]
        if edged:
            edge = halo_in[stream, :, columns].astype(jnp.float32)
            edge = jnp.where(has_previous, edge, jnp.zeros_like(edge))
            row_index = lax.broadcasted_iota(jnp.int32, (8, CHUNK), 0)
        total = weights[0:1] * values
        for tap in range(1, kernel_size):
            moved = pltpu.roll(values, tap, 0)
            if edged:
                top = moved[:8]
                for row in range(tap):
                    at = kernel_size - 1 + row - tap
                    top = jnp.where(row_index == row, edge[at : at + 1], top)
                moved = jnp.concatenate([top, moved[8:]], axis=0)
            total = total + weights[tap : tap + 1] * moved
        return total

    def x_columns(stream, owner, chunk):
        columns = pl.ds(pl.multiple_of(owner * channels + chunk * CHUNK, CHUNK), CHUNK)
        return x_ref[stream, :, columns]

    def gated_rows(owner, chunk):
        keys, values = (
            short_filter(stream, owner, chunk, x_columns(stream, owner, chunk)) for stream in (1, 2)
        )
        return (keys * values).astype(jnp.bfloat16)

    def shared_gated_rows(side, count=rows, edged=True):
        owner = lax.rem(core + side, 2)
        keys, values = (
            short_filter(1 + gate, owner, 0, shared_x[side, gate, :count, :], edged)
            for gate in range(2)
        )
        return (keys * values).astype(jnp.bfloat16)

    def position_rows(owner):
        return pl.ds(pl.multiple_of(owner * rows, rows), rows)

    body_rows = pl.ds(pl.multiple_of(me * rows + TOP, TOP), rows - TOP)
    top_rows = pl.ds(pl.multiple_of(me * rows, rows), TOP)

    wait_all(shared_x, local_sem.at[4])

    @pl.when(chip == 0)
    def _():
        gated_slab[shared, body_rows, :] = shared_gated_rows(0, edged=False)[TOP:]

    def shared_part_copy(part_rows):
        return pltpu.make_async_remote_copy(
            src_ref=gated_slab.at[shared, part_rows, :],
            dst_ref=gated_slab.at[shared, part_rows, :],
            send_sem=gated_send,
            recv_sem=gated_recv.at[shared],
            device_id={"ctx": dests[ACROSS]},
            device_id_type=MESH,
        )

    def shared_body_copy():
        return shared_part_copy(body_rows)

    def shared_top_copy():
        return shared_part_copy(top_rows)

    @pl.when(chip == 0)
    def _():
        enter()

    @pl.when(has_following)
    def _():
        halo_copy.start()

    def taps_copy(i, slot, kind=0):
        taps = (gate_taps, query_taps)[kind]
        return pltpu.make_async_remote_copy(
            src_ref=taps.at[slot],
            dst_ref=taps.at[slot],
            send_sem=taps_send.at[kind],
            recv_sem=taps_recv.at[i if kind == 0 else 3 if i == ACROSS else 4],
            device_id={"ctx": dests[ACROSS] if i == ACROSS else dests[SIBLING]},
            device_id_type=MESH,
        )

    for i in (ACROSS, SIBLING):
        taps_copy(i, me).start()

    def send_query_taps():
        for i in (ACROSS, SIBLING):
            taps_copy(i, me, 1).start()

    @pl.when(chip == 1)
    def _():
        send_query_taps()

    @pl.when(chip == 0)
    def _():
        shared_body_copy().start()
        send_near_filter(range(chunks))

    @pl.when(chip == 1)
    def _():
        send_near_filter(range(1, chunks))

    def gated_copy(i, slot, owner, source=None):
        return pltpu.make_async_remote_copy(
            src_ref=gated_out.at[i, slot] if source is None else source,
            dst_ref=gated_slab.at[slot, position_rows(owner), :],
            send_sem=gated_send,
            recv_sem=gated_recv.at[slot],
            device_id={"ctx": dests[i]},
            device_id_type=MESH,
        )

    def response_copy(i, slot):
        return pltpu.make_async_remote_copy(
            src_ref=response_slab.at[slot, position_rows(dests[i]), :],
            dst_ref=response_in.at[i, slot],
            send_sem=resp_send,
            recv_sem=resp_recv.at[slot if i in CROSS else shared],
            device_id={"ctx": dests[i]},
            device_id_type=MESH,
        )

    def push_gated(i, chunk):
        gated_out[i, chunk] = gated_rows(dests[i], chunk)
        gated_copy(i, chunk, me).start()

    def push_near(chunk):
        push_gated(SIBLING, chunk)
        gated_slab[chunk, position_rows(me), :] = gated_rows(me, chunk)

    def shared_own():
        gated_slab[shared, position_rows(me), :] = shared_gated_rows(0)

    def shared_other():
        gated_out[SIBLING, shared] = shared_gated_rows(1)
        gated_copy(SIBLING, shared, me).start()

    taps_copy(SIBLING, sources[SIBLING]).wait_recv()

    @pl.when(jnp.logical_and(chip == 0, has_previous))
    def _():
        halo_copy.wait_recv()

    @pl.when(chip == 0)
    def _():
        gated_slab[shared, top_rows, :] = shared_gated_rows(0, TOP)
        shared_top_copy().start()
        shared_other()
        gated_copy(DIAGONAL, shared, me, gated_out.at[SIBLING, shared]).start()
        send_query_taps()
        shared_filter_copy().start()
        shared_skip_send().start()
        shared_skip_copy.start()
        half = length // 2
        gated_slab[shared, half:] = jnp.zeros((length - half, CHUNK), jnp.bfloat16)

    for k in range(chunks):
        own_filter_copy(k).start()
    late_copies = [
        local_copy(x_hbm.at[0], x_ref.at[0], 2),
        local_copy(forward_hbm, forward_ref, 6),
        local_copy(backward_hbm, backward_ref, 7),
        local_copy(skip_hbm, skip_ref.at[:, pl.ds(0, channels)], 5),
    ]

    def send_far_up():
        for turn in turns[1:]:
            wait_up(turn)
        for k, slot in enumerate(slots):
            for turn in reversed(turns):
                if turn > 1 or k > 1:
                    send_up(turn, slot)

    @pl.when(chip == 1)
    def _():
        send_far_up()

    for copy in gate_copies:
        copy.wait()
    taps_copy(ACROSS, sources[ACROSS]).wait_recv()
    taps_copy(DIAGONAL, sources[ACROSS]).start()

    @pl.when(chip == 1)
    def _():
        halo_copy.wait_recv()

    push_gated(ACROSS, chip)
    taps_copy(DIAGONAL, sources[DIAGONAL]).wait_recv()
    push_gated(DIAGONAL, chip)

    @pl.when(chip == 0)
    def _():
        send_far_up()

    push_near(first)
    def push_chunk(step, carry):
        @pl.when(chip + step < chunks)
        def _():
            push_gated(ACROSS, chip + step)
            push_gated(DIAGONAL, chip + step)

        @pl.when(first + step < chunks)
        def _():
            push_near(first + step)

        return carry

    lax.fori_loop(1, 2, push_chunk, 0)
    taps_copy(ACROSS, sources[ACROSS], 1).wait_recv()
    taps_copy(DIAGONAL, sources[ACROSS], 1).start()
    lax.fori_loop(2, 3, push_chunk, 0)
    relay_filter(first)
    lax.fori_loop(3, chunks, push_chunk, 0)

    @pl.when(chip == 1)
    def _():
        shared_own()
        shared_other()

    for copy in late_copies:
        copy.wait()
    wait_all(filter_slab.at[shared, pl.ds(0, chunks * fil_rows), :], local_sem.at[9])

    @pl.when(chip == 0)
    def _():
        shared_skip_copy.wait()

    def fill_queries(chunk, carry):
        def one_owner(owner, inner):
            queries[owner, chunk] = short_filter(0, owner, chunk, x_columns(0, owner, chunk)).astype(
                jnp.bfloat16
            )
            return inner

        return lax.fori_loop(0, ctx_size, one_owner, carry)

    @pl.when(chip == 1)
    def _():
        shared_filter_copy().wait_recv()
        shared_skip_send().wait_recv()
        yfil_copy(0, shared).start()
        for turn in turns:
            zfil_copy(turn, shared).start()

    wait_all(query_taps.at[pl.ds(0, 2)], taps_recv.at[4])
    lax.fori_loop(0, chunks, fill_queries, 0)
    relay_filter(first + 1)

    def mix_into(owner, chunk, response):
        columns = pl.ds(pl.multiple_of(owner * channels + chunk * CHUNK, CHUNK), CHUNK)
        mixed = queries[owner, chunk].astype(jnp.float32) * response.astype(jnp.float32)
        out_ref[:, columns] = mixed.astype(jnp.bfloat16)

    def convolve(slot, carry):
        columns = pl.ds(pl.multiple_of(slot * CHUNK, CHUNK), CHUNK)

        from_all = jnp.logical_or(slot < shared, chip == 1)

        @pl.when(from_all)
        def _():
            wait_all(gated_slab.at[slot, pl.ds(0, 3 * rows), :], gated_recv.at[slot])

        @pl.when(jnp.logical_not(from_all))
        def _():
            wait_all(gated_slab.at[slot, pl.ds(0, rows), :], gated_recv.at[slot])

        gated = gated_slab[slot]
        spectrum[...] = jnp.dot(forward_ref[...], gated, preferred_element_type=jnp.float32)
        wait_all(filter_slab.at[slot, pl.ds(0, zsize * fil_rows), :], yfil_recv.at[slot])
        taps = filter_slab[slot]
        ker_cos = jnp.dot(forward_ref[:length], taps, preferred_element_type=jnp.float32)
        ker_sin = jnp.dot(forward_ref[length:], taps, preferred_element_type=jnp.float32)
        sig_cos, sig_sin = spectrum[:length], spectrum[length:]
        prod_ref[:length] = (sig_cos * ker_cos - sig_sin * ker_sin).astype(jnp.bfloat16)
        prod_ref[length:] = (sig_cos * ker_sin + sig_sin * ker_cos).astype(jnp.bfloat16)
        long_part = jnp.dot(backward_ref[...], prod_ref[...], preferred_element_type=jnp.float32)
        direct_part = skip_ref[:, columns] * gated.astype(jnp.float32)
        response_slab[slot] = (long_part + direct_part).astype(jnp.bfloat16)

        @pl.when(slot < shared)
        def _():
            for i in CROSS:
                response_copy(i, slot).start()

        response_copy(SIBLING, slot).start()

        @pl.when(slot + 2 <= shared)
        def _():
            relay_filter(slot + 2)

        response = response_slab[slot, position_rows(me), :]

        @pl.when(slot < shared)
        def _():
            mix_into(me, slot, response)

        @pl.when(slot == shared)
        def _():
            mix_into(core, 0, response)

        return carry

    lax.fori_loop(first, shared + 1, convolve, 0)

    def wait_near(count):
        wait_rows(gated_slab, count * rows, resp_recv.at[shared])

    def finish_near(chunk, carry):
        mix_into(sources[SIBLING], chunk, response_in[SIBLING, chunk])
        return carry

    def finish_cross(chunk, carry):
        wait_all(response_in.at[pl.ds(0, len(CROSS)), chunk], resp_recv.at[chunk])
        for i in CROSS:
            mix_into(sources[i], chunk, response_in[i, chunk])
        return carry

    by_chip(wait_near, chunks, chunks + 1)
    lax.fori_loop(first, chunks, finish_near, 0)
    mix_into(1 - core, 0, response_in[SIBLING, shared])
    lax.fori_loop(chip, chunks, finish_cross, 0)

    def drain_gated(count):
        wait_rows(gated_slab, count * rows, gated_send)

    def drain_response(count):
        wait_rows(gated_slab, count * rows, resp_send)

    def drain_filter(count):
        wait_rows(filter_slab, count * len(turns) * fil_rows, zfil_send)
        wait_rows(filter_slab, count * zsize * fil_rows, yfil_send)

    by_chip(drain_gated, 3 * chunks + 2, 3 * chunks - 1)
    by_chip(drain_filter, chunks, chunks + 1)
    by_chip(drain_response, 3 * chunks - 2, 3 * chunks + 1)

    @pl.when(chip == 0)
    def _():
        shared_filter_copy().wait_send()
        shared_skip_send().wait_send()

    wait_all(gate_taps.at[pl.ds(0, 3)], taps_send.at[0])
    wait_all(query_taps.at[pl.ds(0, 3)], taps_send.at[1])

    @pl.when(has_following)
    def _():
        halo_copy.wait_send()


def write_kernel(mixed_ref, out_hbm, sem):
    copy = pltpu.make_async_copy(mixed_ref, out_hbm, sem)
    copy.start()
    copy.wait()


def write_out(mixed):
    return pl.pallas_call(
        write_kernel,
        out_shape=jax.ShapeDtypeStruct(mixed.shape, mixed.dtype),
        in_specs=[pl.BlockSpec(memory_space=pltpu.VMEM)],
        out_specs=pl.BlockSpec(memory_space=pltpu.HBM),
        scratch_shapes=[pltpu.SemaphoreType.DMA],
    )(pltpu.with_memory_space_constraint(mixed, pltpu.VMEM))


def on_device(projected, short_taps, long_filter, skip_gain):
    ctx_size, dp_size = lax.axis_size("ctx"), lax.axis_size("dp")
    kernel_size, streams, channels = short_taps.shape
    rows, width = projected.shape[1], projected.shape[3]
    length = rows * ctx_size
    regular = ctx_size == 4 and dp_size % 2 == 0 and dp_size >= 6
    regular = regular and channels % CHUNK == 0 and channels >= 2 * CHUNK and kernel_size <= 4
    regular = regular and channels == 4 * CHUNK
    if length > 1024 or not regular:
        return on_device_large(projected, short_taps, long_filter, skip_gain)
    forward, backward = quarter_tables(length)
    chunks = channels // CHUNK
    slots = chunks + 1
    peers = ctx_size - 1
    zsize = dp_size // 2
    hbm_spec = pl.BlockSpec(memory_space=pltpu.HBM)
    dma = pltpu.SemaphoreType.DMA
    operands = (
        projected[0].transpose(1, 0, 2),
        short_taps,
        long_filter,
        skip_gain[None],
        forward,
        backward,
    )
    mixed = pl.pallas_call(
        functools.partial(mixer_kernel, ctx_size, dp_size),
        out_shape=pltpu.VMEM((rows, width), jnp.bfloat16),
        in_specs=[hbm_spec] * len(operands),
        out_specs=pl.BlockSpec(memory_space=pltpu.VMEM),
        scratch_shapes=[
            pltpu.VMEM((streams, rows, width), jnp.bfloat16),
            pltpu.VMEM((2, 2, rows, CHUNK), jnp.bfloat16),
            pltpu.VMEM((streams, 16, width), jnp.bfloat16),
            pltpu.VMEM((1, channels + CHUNK), jnp.float32),
            pltpu.VMEM(forward.shape, jnp.bfloat16),
            pltpu.VMEM(backward.shape, jnp.bfloat16),
            pltpu.VMEM((kernel_size, streams, channels), jnp.float32),
            pltpu.VMEM((8, channels), jnp.float32),
            pltpu.VMEM((4, channels), jnp.float32),
            pltpu.VMEM((ctx_size, 8, channels), jnp.bfloat16),
            pltpu.VMEM((ctx_size, 4, channels), jnp.bfloat16),
            pltpu.VMEM((streams, kernel_size - 1, width), jnp.bfloat16),
            pltpu.VMEM((streams, kernel_size - 1, width), jnp.bfloat16),
            pltpu.VMEM((peers, slots, rows, CHUNK), jnp.bfloat16),
            pltpu.VMEM((slots, length, CHUNK), jnp.bfloat16),
            pltpu.VMEM((slots, length, CHUNK), jnp.bfloat16),
            pltpu.VMEM((2 * length, CHUNK), jnp.float32),
            pltpu.VMEM((2 * length, CHUNK), jnp.bfloat16),
            pltpu.VMEM((slots, length, CHUNK), jnp.bfloat16),
            pltpu.VMEM((peers, slots, rows, CHUNK), jnp.bfloat16),
            pltpu.VMEM((ctx_size, chunks, rows, CHUNK), jnp.bfloat16),
            dma((10,)),
            dma((2,)),
            dma((5,)),
            dma,
            dma,
            dma,
            dma((slots,)),
            dma,
            dma((slots,)),
            dma,
            dma((slots,)),
            dma,
            dma((slots,)),
            pltpu.SemaphoreType.REGULAR((zsize - 2,)),
            dma((2,)),
            dma((2,)),
        ],
        compiler_params=pltpu.CompilerParams(
            collective_id=0, has_side_effects=True, vmem_limit_bytes=40 * 2**20
        ),
    )(*(pltpu.with_memory_space_constraint(array, pltpu.HBM) for array in operands))
    return write_out(mixed)[None]


def solution(mesh):
    return jax.shard_map(
        on_device,
        mesh=mesh,
        in_specs=(P("dp", "ctx", None, None), P(None, None, "ctx"), P("dp", "ctx"), P("ctx")),
        out_specs=P("dp", "ctx", None),
        check_vma=False,
    )
```

```python
import functools
import math

import jax
import jax.numpy as jnp
import numpy as np
from jax import lax
from jax.experimental import pallas as pl
from jax.experimental.pallas import tpu as pltpu
from jax.sharding import PartitionSpec as P

RADIX = 64


HIGH = lax.Precision.HIGHEST


def causal_short(extended, taps, kernel_size):
    row_count = extended.shape[0] - (kernel_size - 1)
    widened = extended.astype(jnp.float32)
    summed = jnp.zeros((row_count,) + widened.shape[1:], jnp.float32)
    for tap_index in range(kernel_size):
        offset = kernel_size - 1 - tap_index
        summed = summed + taps[tap_index] * widened[offset : offset + row_count]
    return (summed[:, 0].astype(jnp.bfloat16), (summed[:, 1] * summed[:, 2]).astype(jnp.bfloat16))


def dft_tables(length, radix_size):
    outer_size = 2 * length // radix_size
    total_size = outer_size * radix_size
    outer_range = jnp.arange(outer_size, dtype=jnp.int32)
    inner_range = jnp.arange(radix_size, dtype=jnp.int32)
    angle_one = (
        2.0
        * math.pi
        / outer_size
        * (outer_range[:, None] * outer_range[None, :] % outer_size).astype(jnp.float32)
    )
    angle_twist = (
        2.0
        * math.pi
        / total_size
        * (outer_range[:, None] * inner_range[None, :] % total_size).astype(jnp.float32)
    )
    angle_two = (
        2.0
        * math.pi
        / radix_size
        * (inner_range[:, None] * inner_range[None, :] % radix_size).astype(jnp.float32)
    )
    twist_cos = jnp.cos(angle_twist)[:, :, None]
    twist_sin = jnp.sin(angle_twist)[:, :, None]
    return (
        jnp.cos(angle_one),
        jnp.sin(angle_one),
        twist_cos,
        twist_sin,
        jnp.cos(angle_two),
        jnp.sin(angle_two),
    )


def forward_dft(signal, tables, radix_size):
    cos_one, sin_one, twist_cos, twist_sin, cos_two, sin_two = tables
    outer_size = cos_one.shape[0]
    half_size = outer_size // 2
    block_width = signal.shape[1]
    shaped = signal.reshape(half_size, radix_size * block_width)
    first_re = jnp.dot(cos_one[:, :half_size], shaped, precision=HIGH).reshape(
        outer_size, radix_size, block_width
    )
    first_im = -jnp.dot(sin_one[:, :half_size], shaped, precision=HIGH).reshape(
        outer_size, radix_size, block_width
    )
    second_re = first_re * twist_cos + first_im * twist_sin
    second_im = first_im * twist_cos - first_re * twist_sin
    spec_re = jnp.einsum("amc,mb->abc", second_re, cos_two, precision=HIGH) + jnp.einsum(
        "amc,mb->abc", second_im, sin_two, precision=HIGH
    )
    spec_im = jnp.einsum("amc,mb->abc", second_im, cos_two, precision=HIGH) - jnp.einsum(
        "amc,mb->abc", second_re, sin_two, precision=HIGH
    )
    return (spec_re, spec_im)


def inverse_dft(spec_re, spec_im, tables, radix_size):
    cos_one, sin_one, twist_cos, twist_sin, cos_two, sin_two = tables
    outer_size = cos_one.shape[0]
    half_size = outer_size // 2
    block_width = spec_re.shape[2]
    back_re = jnp.einsum("abc,mb->amc", spec_re, cos_two, precision=HIGH) - jnp.einsum(
        "abc,mb->amc", spec_im, sin_two, precision=HIGH
    )
    back_im = jnp.einsum("abc,mb->amc", spec_re, sin_two, precision=HIGH) + jnp.einsum(
        "abc,mb->amc", spec_im, cos_two, precision=HIGH
    )
    turned_re = (back_re * twist_cos - back_im * twist_sin).reshape(
        outer_size, radix_size * block_width
    )
    turned_im = (back_re * twist_sin + back_im * twist_cos).reshape(
        outer_size, radix_size * block_width
    )
    result = jnp.dot(cos_one[:half_size], turned_re, precision=HIGH) - jnp.dot(
        sin_one[:half_size], turned_im, precision=HIGH
    )
    return result.reshape(half_size * radix_size, block_width) / (outer_size * radix_size)


def long_convolve_blocked(gated_slab, filter_slab):
    length, channels = gated_slab.shape
    block_width = min(128, channels)
    tables = dft_tables(length, RADIX)

    def one_block(block_index, output):
        offset = block_index * block_width
        signal = lax.dynamic_slice_in_dim(gated_slab, offset, block_width, 1).astype(jnp.float32)
        kernel_block = lax.dynamic_slice_in_dim(filter_slab, offset, block_width, 1).astype(
            jnp.float32
        )
        sig_re, sig_im = forward_dft(signal, tables, RADIX)
        ker_re, ker_im = forward_dft(kernel_block, tables, RADIX)
        prod_re = sig_re * ker_re - sig_im * ker_im
        prod_im = sig_re * ker_im + sig_im * ker_re
        result = inverse_dft(prod_re, prod_im, tables, RADIX)
        return lax.dynamic_update_slice_in_dim(output, result, offset, 1)

    return lax.fori_loop(
        0, channels // block_width, one_block, jnp.zeros((length, channels), jnp.float32)
    )


def long_convolve(gated_slab, filter_slab):
    length = gated_slab.shape[0]
    if length > 1024:
        return long_convolve_blocked(gated_slab, filter_slab)
    forward, backward = quarter_tables(length)
    sig = jnp.dot(forward, gated_slab, preferred_element_type=jnp.float32)
    ker = jnp.dot(forward, filter_slab, preferred_element_type=jnp.float32)
    sig_cos, sig_sin, ker_cos, ker_sin = sig[:length], sig[length:], ker[:length], ker[length:]
    prod = jnp.concatenate(
        [sig_cos * ker_cos - sig_sin * ker_sin, sig_cos * ker_sin + sig_sin * ker_cos]
    ).astype(jnp.bfloat16)
    return jnp.dot(backward, prod, preferred_element_type=jnp.float32)


def quarter_tables(length):
    steps = (4 * np.arange(length)[:, None] + 1) * np.arange(length)[None, :] % (4 * length)
    angles = steps * (2.0 * math.pi / (4 * length))
    table = np.concatenate([np.cos(angles), np.sin(angles)])
    return (jnp.asarray(table, jnp.bfloat16), jnp.asarray(table.T / length, jnp.bfloat16))


def make_response(gated_slab, filter_slab, skip_gain):
    long_part = long_convolve(gated_slab, filter_slab)
    return (long_part + skip_gain * gated_slab.astype(jnp.float32)).astype(jnp.bfloat16)


def combine_rows(query_part, response_part):
    return (query_part.astype(jnp.float32) * response_part.astype(jnp.float32)).astype(jnp.bfloat16)


def on_device_large(projected, short_taps, long_filter, skip_gain):
    kernel_size = short_taps.shape[0]
    ctx_size = lax.axis_size("ctx")
    rows = projected[0]
    filter_slab = lax.all_gather(long_filter, "dp", axis=0, tiled=True)
    all_taps = lax.all_gather(short_taps, "ctx", axis=2, tiled=True)
    halo = lax.ppermute(
        rows[-(kernel_size - 1) :], "ctx", [(i, i + 1) for i in range(ctx_size - 1)]
    )
    queries, gated = causal_short(jnp.concatenate([halo, rows]), all_taps, kernel_size)
    gated_slab = lax.all_to_all(gated, "ctx", split_axis=1, concat_axis=0, tiled=True)
    response_slab = make_response(gated_slab, filter_slab, skip_gain)
    response = lax.all_to_all(response_slab, "ctx", split_axis=0, concat_axis=1, tiled=True)
    return combine_rows(queries, response)[None]


CHUNK = 256
MESH = pl.DeviceIdType.MESH
ACROSS, DIAGONAL, SIBLING = 0, 1, 2
CROSS = (ACROSS, DIAGONAL)
TOP = 16


def ctx_offsets(ctx_size):
    pairs = [(a, b) for a in range(1, ctx_size // 2) for b in range(2)]
    return pairs + [(0, 1)]


def ctx_peer(me, offset, ctx_size, sign):
    half = ctx_size // 2
    chip = lax.rem(me // 2 + (half + sign * offset[0]) % half, half)
    core = lax.rem(lax.rem(me, 2) + offset[1], 2)
    return chip * 2 + core


def mixer_kernel(
    ctx_size,
    dp_size,
    x_hbm,
    taps_hbm,
    filter_hbm,
    skip_hbm,
    forward_hbm,
    backward_hbm,
    out_ref,
    x_ref,
    shared_x,
    tail_ref,
    skip_ref,
    forward_ref,
    backward_ref,
    own_taps,
    gate_rows,
    query_rows,
    gate_taps,
    query_taps,
    halo_out,
    halo_in,
    gated_out,
    gated_slab,
    filter_slab,
    spectrum,
    prod_ref,
    response_slab,
    response_in,
    queries,
    local_sem,
    taps_send,
    taps_recv,
    halo_send,
    halo_recv,
    zfil_send,
    zfil_recv,
    yfil_send,
    yfil_recv,
    gated_send,
    gated_recv,
    resp_send,
    resp_recv,
    ready_sem,
    shared_send,
    shared_recv,
):
    kernel_size = taps_hbm.shape[0]
    channels = taps_hbm.shape[2]
    rows = x_ref.shape[1]
    length = rows * ctx_size
    chunks = channels // CHUNK
    fil_rows = filter_hbm.shape[0]
    zsize = dp_size // 2
    turns = list(range(1, zsize))
    me = lax.axis_index("ctx")
    dp = lax.axis_index("dp")
    zpos, ypos = dp // 2, lax.rem(dp, 2)
    chip, core = me // 2, lax.rem(me, 2)
    first = 1 - chip
    offsets = ctx_offsets(ctx_size)
    dests = [ctx_peer(me, o, ctx_size, 1) for o in offsets]
    sources = [ctx_peer(me, o, ctx_size, -1) for o in offsets]
    ypeer = zpos * 2 + (1 - ypos)

    def signal(semaphore, **where):
        pl.semaphore_signal(semaphore, inc=1, device_id=where, device_id_type=MESH)

    barrier = pltpu.get_barrier_semaphore()
    for dest in dests:
        signal(barrier, ctx=dest)
    above = (zpos < zsize - 1).astype(jnp.int32)
    greeted = len(dests) + 1 + above + zpos

    def wait_all(ref, semaphore):
        pltpu.make_async_copy(ref, ref, semaphore).wait()

    def wait_rows(ref, count, semaphore):
        wait_all(ref.at[pl.ds(0, 4), pl.ds(0, count // 4), :], semaphore)

    def by_chip(wait, on_first, on_second):
        for which, count in enumerate((on_first, on_second)):

            @pl.when(chip == which)
            def _(count=count):
                wait(count)

    def local_copy(source, target, index):
        copy = pltpu.make_async_copy(source, target, local_sem.at[index])
        copy.start()
        return copy

    own_taps_copy = local_copy(taps_hbm, own_taps, 0)
    for side in range(2):
        owner = lax.rem(core + side, 2)
        columns = pl.ds(pl.multiple_of(owner * channels, channels), CHUNK)
        local_copy(x_hbm.at[pl.ds(1, 2), :, columns], shared_x.at[side], 4)
    tail_rows = tail_ref.shape[1]
    tail_copy = local_copy(x_hbm.at[:, pl.ds(rows - tail_rows, tail_rows), :], tail_ref, 1)
    gate_copies = [local_copy(x_hbm.at[pl.ds(1, 2)], x_ref.at[pl.ds(1, 2)], 3)]
    signal(barrier, dp=ypeer)
    for turn in turns:

        @pl.when(zpos + turn < zsize)
        def _(turn=turn):
            signal(barrier, dp=dp + 2 * turn)

    @pl.when(zpos > 0)
    def _():
        signal(barrier, dp=dp - 2)


    shared = chunks
    slots = [first + k for k in range(chunks)]

    def filter_block(block, slot):
        return filter_slab.at[slot, pl.ds(pl.multiple_of(block * fil_rows, fil_rows), fil_rows), :]

    def own_filter(slot):
        chunk = lax.rem(slot, chunks)
        return filter_hbm.at[:, pl.ds(pl.multiple_of(chunk * CHUNK, CHUNK), CHUNK)]

    def own_filter_copy(k):
        return pltpu.make_async_copy(
            own_filter(slots[k]), filter_block(dp, slots[k]), local_sem.at[9]
        )

    shared_skip = skip_ref.at[:, pl.ds(channels, CHUNK)]
    first_skip = skip_hbm.at[:, pl.ds(0, CHUNK)]
    shared_skip_copy = pltpu.make_async_copy(first_skip, shared_skip, local_sem.at[8])

    def enter():
        pl.semaphore_wait(barrier, greeted)
        for turn in turns[1:]:

            @pl.when(zpos >= turn)
            def _(turn=turn):
                signal(ready_sem.at[turn - 2], dp=dp - 2 * turn)

    def zfil_copy(turn, slot, source=None):
        target = lax.rem(zpos + turn, zsize)
        return pltpu.make_async_remote_copy(
            src_ref=filter_block(dp, slot) if source is None else source,
            dst_ref=filter_block(dp, slot),
            send_sem=zfil_send,
            recv_sem=zfil_recv.at[turn - 1, slot],
            device_id={"dp": target * 2 + ypos},
            device_id_type=MESH,
        )

    def yfil_copy(turn, slot, source=None):
        origin = lax.rem(zpos + zsize - turn, zsize)
        block = origin * 2 + ypos
        return pltpu.make_async_remote_copy(
            src_ref=filter_block(block, slot) if source is None else source,
            dst_ref=filter_block(block, slot),
            send_sem=yfil_send,
            recv_sem=yfil_recv.at[slot],
            device_id={"dp": ypeer},
            device_id_type=MESH,
        )

    def shared_filter_copy():
        return pltpu.make_async_remote_copy(
            src_ref=own_filter(shared),
            dst_ref=filter_block(dp, shared),
            send_sem=shared_send.at[0],
            recv_sem=shared_recv.at[0],
            device_id={"ctx": dests[ACROSS]},
            device_id_type=MESH,
        )

    def shared_skip_send():
        return pltpu.make_async_remote_copy(
            src_ref=first_skip,
            dst_ref=shared_skip,
            send_sem=shared_send.at[1],
            recv_sem=shared_recv.at[1],
            device_id={"ctx": dests[ACROSS]},
            device_id_type=MESH,
        )

    def relay_filter(slot):
        for turn in turns:
            zfil_copy(turn, slot).wait_recv()
            yfil_copy(turn, slot).start()

    def send_up(turn, slot):
        @pl.when(zpos + turn < zsize)
        def _():
            zfil_copy(turn, slot, own_filter(slot)).start()

    def send_down(turn, slot):
        @pl.when(zpos + turn >= zsize)
        def _():
            zfil_copy(turn, slot, own_filter(slot)).start()

    def wait_up(turn):
        @pl.when(zpos + turn < zsize)
        def _():
            pl.semaphore_wait(ready_sem.at[turn - 2], 1)

    def send_near_filter(steps):
        for k in steps:
            slot = slots[k]
            for turn in turns:
                send_down(turn, slot)
            yfil_copy(0, slot, own_filter(slot)).start()
            if k < 2:
                send_up(1, slot)

    @pl.when(chip == 1)
    def _():
        enter()
        send_near_filter(range(1))

    halo_copy = pltpu.make_async_remote_copy(
        src_ref=halo_out,
        dst_ref=halo_in,
        send_sem=halo_send,
        recv_sem=halo_recv,
        device_id={"ctx": lax.rem(me + 1, ctx_size)},
        device_id_type=MESH,
    )
    has_following, has_previous = me < ctx_size - 1, me > 0
    tail_copy.wait()

    @pl.when(has_following)
    def _():
        halo_out[...] = tail_ref[:, tail_rows - (kernel_size - 1) :, :]

    own_taps_copy.wait()
    gate_rows[...] = jnp.zeros_like(gate_rows)
    query_rows[...] = jnp.zeros_like(query_rows)
    for tap in range(kernel_size):
        query_rows[tap : tap + 1, :] = own_taps[tap, 0:1, :]
        for gate in range(2):
            row = gate * kernel_size + tap
            gate_rows[row : row + 1, :] = own_taps[tap, 1 + gate : 2 + gate, :]
    gate_taps[me] = gate_rows[...].astype(jnp.bfloat16)
    query_taps[me] = query_rows[...].astype(jnp.bfloat16)

    def short_filter(stream, owner, chunk, values, edged=True):
        columns = pl.ds(pl.multiple_of(owner * channels + chunk * CHUNK, CHUNK), CHUNK)
        taps_columns = pl.ds(pl.multiple_of(chunk * CHUNK, CHUNK), CHUNK)
        values = values.astype(jnp.float32)
        if stream == 0:
            weights = query_taps[owner, :, taps_columns].astype(jnp.float32)
        else:
            weights = gate_taps[owner, :, taps_columns].astype(jnp.float32)
            weights = weights[(stream - 1) * kernel_size : stream * kernel_size]
        if edged:
            edge = halo_in[stream, :, columns].astype(jnp.float32)
            edge = jnp.where(has_previous, edge, jnp.zeros_like(edge))
            row_index = lax.broadcasted_iota(jnp.int32, (8, CHUNK), 0)
        total = weights[0:1] * values
        for tap in range(1, kernel_size):
            moved = pltpu.roll(values, tap, 0)
            if edged:
                top = moved[:8]
                for row in range(tap):
                    at = kernel_size - 1 + row - tap
                    top = jnp.where(row_index == row, edge[at : at + 1], top)
                moved = jnp.concatenate([top, moved[8:]], axis=0)
            total = total + weights[tap : tap + 1] * moved
        return total

    def x_columns(stream, owner, chunk):
        columns = pl.ds(pl.multiple_of(owner * channels + chunk * CHUNK, CHUNK), CHUNK)
        return x_ref[stream, :, columns]

    def gated_rows(owner, chunk):
        keys, values = (
            short_filter(stream, owner, chunk, x_columns(stream, owner, chunk)) for stream in (1, 2)
        )
        return (keys * values).astype(jnp.bfloat16)

    def shared_gated_rows(side, count=rows, edged=True):
        owner = lax.rem(core + side, 2)
        keys, values = (
            short_filter(1 + gate, owner, 0, shared_x[side, gate, :count, :], edged)
            for gate in range(2)
        )
        return (keys * values).astype(jnp.bfloat16)

    def position_rows(owner):
        return pl.ds(pl.multiple_of(owner * rows, rows), rows)

    body_rows = pl.ds(pl.multiple_of(me * rows + TOP, TOP), rows - TOP)
    top_rows = pl.ds(pl.multiple_of(me * rows, rows), TOP)

    wait_all(shared_x, local_sem.at[4])

    @pl.when(chip == 0)
    def _():
        gated_slab[shared, body_rows, :] = shared_gated_rows(0, edged=False)[TOP:]

    def shared_part_copy(part_rows):
        return pltpu.make_async_remote_copy(
            src_ref=gated_slab.at[shared, part_rows, :],
            dst_ref=gated_slab.at[shared, part_rows, :],
            send_sem=gated_send,
            recv_sem=gated_recv.at[shared],
            device_id={"ctx": dests[ACROSS]},
            device_id_type=MESH,
        )

    def shared_body_copy():
        return shared_part_copy(body_rows)

    def shared_top_copy():
        return shared_part_copy(top_rows)

    @pl.when(chip == 0)
    def _():
        enter()

    @pl.when(has_following)
    def _():
        halo_copy.start()

    def taps_copy(i, slot, kind=0):
        taps = (gate_taps, query_taps)[kind]
        return pltpu.make_async_remote_copy(
            src_ref=taps.at[slot],
            dst_ref=taps.at[slot],
            send_sem=taps_send.at[kind],
            recv_sem=taps_recv.at[i if kind == 0 else 3 if i == ACROSS else 4],
            device_id={"ctx": dests[ACROSS] if i == ACROSS else dests[SIBLING]},
            device_id_type=MESH,
        )

    for i in (ACROSS, SIBLING):
        taps_copy(i, me).start()

    def send_query_taps():
        for i in (ACROSS, SIBLING):
            taps_copy(i, me, 1).start()

    @pl.when(chip == 1)
    def _():
        send_query_taps()

    @pl.when(chip == 0)
    def _():
        shared_body_copy().start()
        send_near_filter(range(chunks))

    @pl.when(chip == 1)
    def _():
        send_near_filter(range(1, chunks))

    def gated_copy(i, slot, owner, source=None):
        return pltpu.make_async_remote_copy(
            src_ref=gated_out.at[i, slot] if source is None else source,
            dst_ref=gated_slab.at[slot, position_rows(owner), :],
            send_sem=gated_send,
            recv_sem=gated_recv.at[slot],
            device_id={"ctx": dests[i]},
            device_id_type=MESH,
        )

    def response_copy(i, slot):
        return pltpu.make_async_remote_copy(
            src_ref=response_slab.at[slot, position_rows(dests[i]), :],
            dst_ref=response_in.at[i, slot],
            send_sem=resp_send,
            recv_sem=resp_recv.at[slot if i in CROSS else shared],
            device_id={"ctx": dests[i]},
            device_id_type=MESH,
        )

    def push_gated(i, chunk):
        gated_out[i, chunk] = gated_rows(dests[i], chunk)
        gated_copy(i, chunk, me).start()

    def push_near(chunk):
        push_gated(SIBLING, chunk)
        gated_slab[chunk, position_rows(me), :] = gated_rows(me, chunk)

    def shared_own():
        gated_slab[shared, position_rows(me), :] = shared_gated_rows(0)

    def shared_other():
        gated_out[SIBLING, shared] = shared_gated_rows(1)
        gated_copy(SIBLING, shared, me).start()

    taps_copy(SIBLING, sources[SIBLING]).wait_recv()

    @pl.when(jnp.logical_and(chip == 0, has_previous))
    def _():
        halo_copy.wait_recv()

    @pl.when(chip == 0)
    def _():
        gated_slab[shared, top_rows, :] = shared_gated_rows(0, TOP)
        shared_top_copy().start()
        shared_other()
        gated_copy(DIAGONAL, shared, me, gated_out.at[SIBLING, shared]).start()
        send_query_taps()
        shared_filter_copy().start()
        shared_skip_send().start()
        shared_skip_copy.start()
        half = length // 2
        gated_slab[shared, half:] = jnp.zeros((length - half, CHUNK), jnp.bfloat16)

    for k in range(chunks):
        own_filter_copy(k).start()
    late_copies = [
        local_copy(x_hbm.at[0], x_ref.at[0], 2),
        local_copy(forward_hbm, forward_ref, 6),
        local_copy(backward_hbm, backward_ref, 7),
        local_copy(skip_hbm, skip_ref.at[:, pl.ds(0, channels)], 5),
    ]

    def send_far_up():
        for turn in turns[1:]:
            wait_up(turn)
        for k, slot in enumerate(slots):
            for turn in reversed(turns):
                if turn > 1 or k > 1:
                    send_up(turn, slot)

    @pl.when(chip == 1)
    def _():
        send_far_up()

    for copy in gate_copies:
        copy.wait()
    taps_copy(ACROSS, sources[ACROSS]).wait_recv()
    taps_copy(DIAGONAL, sources[ACROSS]).start()

    @pl.when(chip == 1)
    def _():
        halo_copy.wait_recv()

    push_gated(ACROSS, chip)
    taps_copy(DIAGONAL, sources[DIAGONAL]).wait_recv()
    push_gated(DIAGONAL, chip)

    @pl.when(jnp.logical_and(chip == 0, zpos > 0))
    def _():
        send_far_up()

    push_near(first)
    def push_chunk(step, carry):
        @pl.when(chip + step < chunks)
        def _():
            push_gated(ACROSS, chip + step)
            push_gated(DIAGONAL, chip + step)

        @pl.when(first + step < chunks)
        def _():
            push_near(first + step)

        return carry

    lax.fori_loop(1, 2, push_chunk, 0)

    @pl.when(jnp.logical_and(chip == 0, zpos == 0))
    def _():
        send_far_up()

    taps_copy(ACROSS, sources[ACROSS], 1).wait_recv()
    taps_copy(DIAGONAL, sources[ACROSS], 1).start()
    lax.fori_loop(2, 3, push_chunk, 0)
    relay_filter(first)
    lax.fori_loop(3, chunks, push_chunk, 0)

    @pl.when(chip == 1)
    def _():
        shared_own()
        shared_other()

    for copy in late_copies:
        copy.wait()
    wait_all(filter_slab.at[shared, pl.ds(0, chunks * fil_rows), :], local_sem.at[9])

    @pl.when(chip == 0)
    def _():
        shared_skip_copy.wait()

    def fill_queries(chunk, carry):
        def one_owner(owner, inner):
            queries[owner, chunk] = short_filter(0, owner, chunk, x_columns(0, owner, chunk)).astype(
                jnp.bfloat16
            )
            return inner

        return lax.fori_loop(0, ctx_size, one_owner, carry)

    @pl.when(chip == 1)
    def _():
        shared_filter_copy().wait_recv()
        shared_skip_send().wait_recv()
        yfil_copy(0, shared).start()
        for turn in turns:
            zfil_copy(turn, shared).start()

    wait_all(query_taps.at[pl.ds(0, 2)], taps_recv.at[4])
    lax.fori_loop(0, chunks, fill_queries, 0)
    relay_filter(first + 1)

    def mix_into(owner, chunk, response):
        columns = pl.ds(pl.multiple_of(owner * channels + chunk * CHUNK, CHUNK), CHUNK)
        mixed = queries[owner, chunk].astype(jnp.float32) * response.astype(jnp.float32)
        out_ref[:, columns] = mixed.astype(jnp.bfloat16)

    def convolve(slot, carry):
        columns = pl.ds(pl.multiple_of(slot * CHUNK, CHUNK), CHUNK)

        from_all = jnp.logical_or(slot < shared, chip == 1)

        @pl.when(from_all)
        def _():
            wait_all(gated_slab.at[slot, pl.ds(0, 3 * rows), :], gated_recv.at[slot])

        @pl.when(jnp.logical_not(from_all))
        def _():
            wait_all(gated_slab.at[slot, pl.ds(0, rows), :], gated_recv.at[slot])

        gated = gated_slab[slot]
        spectrum[...] = jnp.dot(forward_ref[...], gated, preferred_element_type=jnp.float32)
        wait_all(filter_slab.at[slot, pl.ds(0, zsize * fil_rows), :], yfil_recv.at[slot])
        taps = filter_slab[slot]
        ker_cos = jnp.dot(forward_ref[:length], taps, preferred_element_type=jnp.float32)
        ker_sin = jnp.dot(forward_ref[length:], taps, preferred_element_type=jnp.float32)
        sig_cos, sig_sin = spectrum[:length], spectrum[length:]
        prod_ref[:length] = (sig_cos * ker_cos - sig_sin * ker_sin).astype(jnp.bfloat16)
        prod_ref[length:] = (sig_cos * ker_sin + sig_sin * ker_cos).astype(jnp.bfloat16)
        long_part = jnp.dot(backward_ref[...], prod_ref[...], preferred_element_type=jnp.float32)
        direct_part = skip_ref[:, columns] * gated.astype(jnp.float32)
        response_slab[slot] = (long_part + direct_part).astype(jnp.bfloat16)

        @pl.when(slot < shared)
        def _():
            for i in CROSS:
                response_copy(i, slot).start()

        response_copy(SIBLING, slot).start()

        @pl.when(slot + 2 <= shared)
        def _():
            relay_filter(slot + 2)

        response = response_slab[slot, position_rows(me), :]

        @pl.when(slot < shared)
        def _():
            mix_into(me, slot, response)

        @pl.when(slot == shared)
        def _():
            mix_into(core, 0, response)

        return carry

    lax.fori_loop(first, shared + 1, convolve, 0)

    def wait_near(count):
        wait_rows(gated_slab, count * rows, resp_recv.at[shared])

    def finish_near(chunk, carry):
        mix_into(sources[SIBLING], chunk, response_in[SIBLING, chunk])
        return carry

    def finish_cross(chunk, carry):
        wait_all(response_in.at[pl.ds(0, len(CROSS)), chunk], resp_recv.at[chunk])
        for i in CROSS:
            mix_into(sources[i], chunk, response_in[i, chunk])
        return carry

    by_chip(wait_near, chunks, chunks + 1)
    lax.fori_loop(first, chunks, finish_near, 0)
    mix_into(1 - core, 0, response_in[SIBLING, shared])
    lax.fori_loop(chip, chunks, finish_cross, 0)

    def drain_gated(count):
        wait_rows(gated_slab, count * rows, gated_send)

    def drain_response(count):
        wait_rows(gated_slab, count * rows, resp_send)

    def drain_filter(count):
        wait_rows(filter_slab, count * len(turns) * fil_rows, zfil_send)
        wait_rows(filter_slab, count * zsize * fil_rows, yfil_send)

    by_chip(drain_gated, 3 * chunks + 2, 3 * chunks - 1)
    by_chip(drain_filter, chunks, chunks + 1)
    by_chip(drain_response, 3 * chunks - 2, 3 * chunks + 1)

    @pl.when(chip == 0)
    def _():
        shared_filter_copy().wait_send()
        shared_skip_send().wait_send()

    wait_all(gate_taps.at[pl.ds(0, 3)], taps_send.at[0])
    wait_all(query_taps.at[pl.ds(0, 3)], taps_send.at[1])

    @pl.when(has_following)
    def _():
        halo_copy.wait_send()


def write_kernel(mixed_ref, out_hbm, sem):
    copy = pltpu.make_async_copy(mixed_ref, out_hbm, sem)
    copy.start()
    copy.wait()


def write_out(mixed):
    return pl.pallas_call(
        write_kernel,
        out_shape=jax.ShapeDtypeStruct(mixed.shape, mixed.dtype),
        in_specs=[pl.BlockSpec(memory_space=pltpu.VMEM)],
        out_specs=pl.BlockSpec(memory_space=pltpu.HBM),
        scratch_shapes=[pltpu.SemaphoreType.DMA],
    )(pltpu.with_memory_space_constraint(mixed, pltpu.VMEM))


def on_device(projected, short_taps, long_filter, skip_gain):
    ctx_size, dp_size = lax.axis_size("ctx"), lax.axis_size("dp")
    kernel_size, streams, channels = short_taps.shape
    rows, width = projected.shape[1], projected.shape[3]
    length = rows * ctx_size
    regular = ctx_size == 4 and dp_size % 2 == 0 and dp_size >= 6
    regular = regular and channels % CHUNK == 0 and channels >= 2 * CHUNK and kernel_size <= 4
    regular = regular and channels == 4 * CHUNK
    if length > 1024 or not regular:
        return on_device_large(projected, short_taps, long_filter, skip_gain)
    forward, backward = quarter_tables(length)
    chunks = channels // CHUNK
    slots = chunks + 1
    peers = ctx_size - 1
    zsize = dp_size // 2
    hbm_spec = pl.BlockSpec(memory_space=pltpu.HBM)
    dma = pltpu.SemaphoreType.DMA
    operands = (
        projected[0].transpose(1, 0, 2),
        short_taps,
        long_filter,
        skip_gain[None],
        forward,
        backward,
    )
    mixed = pl.pallas_call(
        functools.partial(mixer_kernel, ctx_size, dp_size),
        out_shape=pltpu.VMEM((rows, width), jnp.bfloat16),
        in_specs=[hbm_spec] * len(operands),
        out_specs=pl.BlockSpec(memory_space=pltpu.VMEM),
        scratch_shapes=[
            pltpu.VMEM((streams, rows, width), jnp.bfloat16),
            pltpu.VMEM((2, 2, rows, CHUNK), jnp.bfloat16),
            pltpu.VMEM((streams, 16, width), jnp.bfloat16),
            pltpu.VMEM((1, channels + CHUNK), jnp.float32),
            pltpu.VMEM(forward.shape, jnp.bfloat16),
            pltpu.VMEM(backward.shape, jnp.bfloat16),
            pltpu.VMEM((kernel_size, streams, channels), jnp.float32),
            pltpu.VMEM((8, channels), jnp.float32),
            pltpu.VMEM((4, channels), jnp.float32),
            pltpu.VMEM((ctx_size, 8, channels), jnp.bfloat16),
            pltpu.VMEM((ctx_size, 4, channels), jnp.bfloat16),
            pltpu.VMEM((streams, kernel_size - 1, width), jnp.bfloat16),
            pltpu.VMEM((streams, kernel_size - 1, width), jnp.bfloat16),
            pltpu.VMEM((peers, slots, rows, CHUNK), jnp.bfloat16),
            pltpu.VMEM((slots, length, CHUNK), jnp.bfloat16),
            pltpu.VMEM((slots, length, CHUNK), jnp.bfloat16),
            pltpu.VMEM((2 * length, CHUNK), jnp.float32),
            pltpu.VMEM((2 * length, CHUNK), jnp.bfloat16),
            pltpu.VMEM((slots, length, CHUNK), jnp.bfloat16),
            pltpu.VMEM((peers, slots, rows, CHUNK), jnp.bfloat16),
            pltpu.VMEM((ctx_size, chunks, rows, CHUNK), jnp.bfloat16),
            dma((10,)),
            dma((2,)),
            dma((5,)),
            dma,
            dma,
            dma,
            dma((zsize - 1, slots)),
            dma,
            dma((slots,)),
            dma,
            dma((slots,)),
            dma,
            dma((slots,)),
            pltpu.SemaphoreType.REGULAR((zsize - 2,)),
            dma((2,)),
            dma((2,)),
        ],
        compiler_params=pltpu.CompilerParams(
            collective_id=0, has_side_effects=True, vmem_limit_bytes=40 * 2**20
        ),
    )(*(pltpu.with_memory_space_constraint(array, pltpu.HBM) for array in operands))
    return write_out(mixed)[None]


def solution(mesh):
    return jax.shard_map(
        on_device,
        mesh=mesh,
        in_specs=(P("dp", "ctx", None, None), P(None, None, "ctx"), P("dp", "ctx"), P("ctx")),
        out_specs=P("dp", "ctx", None),
        check_vma=False,
    )
```

```python
import functools
import math

import jax
import jax.numpy as jnp
import numpy as np
from jax import lax
from jax.experimental import pallas as pl
from jax.experimental.pallas import tpu as pltpu
from jax.sharding import PartitionSpec as P

RADIX = 64


HIGH = lax.Precision.HIGHEST


def causal_short(extended, taps, kernel_size):
    row_count = extended.shape[0] - (kernel_size - 1)
    widened = extended.astype(jnp.float32)
    summed = jnp.zeros((row_count,) + widened.shape[1:], jnp.float32)
    for tap_index in range(kernel_size):
        offset = kernel_size - 1 - tap_index
        summed = summed + taps[tap_index] * widened[offset : offset + row_count]
    return (summed[:, 0].astype(jnp.bfloat16), (summed[:, 1] * summed[:, 2]).astype(jnp.bfloat16))


def dft_tables(length, radix_size):
    outer_size = 2 * length // radix_size
    total_size = outer_size * radix_size
    outer_range = jnp.arange(outer_size, dtype=jnp.int32)
    inner_range = jnp.arange(radix_size, dtype=jnp.int32)
    angle_one = (
        2.0
        * math.pi
        / outer_size
        * (outer_range[:, None] * outer_range[None, :] % outer_size).astype(jnp.float32)
    )
    angle_twist = (
        2.0
        * math.pi
        / total_size
        * (outer_range[:, None] * inner_range[None, :] % total_size).astype(jnp.float32)
    )
    angle_two = (
        2.0
        * math.pi
        / radix_size
        * (inner_range[:, None] * inner_range[None, :] % radix_size).astype(jnp.float32)
    )
    twist_cos = jnp.cos(angle_twist)[:, :, None]
    twist_sin = jnp.sin(angle_twist)[:, :, None]
    return (
        jnp.cos(angle_one),
        jnp.sin(angle_one),
        twist_cos,
        twist_sin,
        jnp.cos(angle_two),
        jnp.sin(angle_two),
    )


def forward_dft(signal, tables, radix_size):
    cos_one, sin_one, twist_cos, twist_sin, cos_two, sin_two = tables
    outer_size = cos_one.shape[0]
    half_size = outer_size // 2
    block_width = signal.shape[1]
    shaped = signal.reshape(half_size, radix_size * block_width)
    first_re = jnp.dot(cos_one[:, :half_size], shaped, precision=HIGH).reshape(
        outer_size, radix_size, block_width
    )
    first_im = -jnp.dot(sin_one[:, :half_size], shaped, precision=HIGH).reshape(
        outer_size, radix_size, block_width
    )
    second_re = first_re * twist_cos + first_im * twist_sin
    second_im = first_im * twist_cos - first_re * twist_sin
    spec_re = jnp.einsum("amc,mb->abc", second_re, cos_two, precision=HIGH) + jnp.einsum(
        "amc,mb->abc", second_im, sin_two, precision=HIGH
    )
    spec_im = jnp.einsum("amc,mb->abc", second_im, cos_two, precision=HIGH) - jnp.einsum(
        "amc,mb->abc", second_re, sin_two, precision=HIGH
    )
    return (spec_re, spec_im)


def inverse_dft(spec_re, spec_im, tables, radix_size):
    cos_one, sin_one, twist_cos, twist_sin, cos_two, sin_two = tables
    outer_size = cos_one.shape[0]
    half_size = outer_size // 2
    block_width = spec_re.shape[2]
    back_re = jnp.einsum("abc,mb->amc", spec_re, cos_two, precision=HIGH) - jnp.einsum(
        "abc,mb->amc", spec_im, sin_two, precision=HIGH
    )
    back_im = jnp.einsum("abc,mb->amc", spec_re, sin_two, precision=HIGH) + jnp.einsum(
        "abc,mb->amc", spec_im, cos_two, precision=HIGH
    )
    turned_re = (back_re * twist_cos - back_im * twist_sin).reshape(
        outer_size, radix_size * block_width
    )
    turned_im = (back_re * twist_sin + back_im * twist_cos).reshape(
        outer_size, radix_size * block_width
    )
    result = jnp.dot(cos_one[:half_size], turned_re, precision=HIGH) - jnp.dot(
        sin_one[:half_size], turned_im, precision=HIGH
    )
    return result.reshape(half_size * radix_size, block_width) / (outer_size * radix_size)


def long_convolve_blocked(gated_slab, filter_slab):
    length, channels = gated_slab.shape
    block_width = min(128, channels)
    tables = dft_tables(length, RADIX)

    def one_block(block_index, output):
        offset = block_index * block_width
        signal = lax.dynamic_slice_in_dim(gated_slab, offset, block_width, 1).astype(jnp.float32)
        kernel_block = lax.dynamic_slice_in_dim(filter_slab, offset, block_width, 1).astype(
            jnp.float32
        )
        sig_re, sig_im = forward_dft(signal, tables, RADIX)
        ker_re, ker_im = forward_dft(kernel_block, tables, RADIX)
        prod_re = sig_re * ker_re - sig_im * ker_im
        prod_im = sig_re * ker_im + sig_im * ker_re
        result = inverse_dft(prod_re, prod_im, tables, RADIX)
        return lax.dynamic_update_slice_in_dim(output, result, offset, 1)

    return lax.fori_loop(
        0, channels // block_width, one_block, jnp.zeros((length, channels), jnp.float32)
    )


def long_convolve(gated_slab, filter_slab):
    length = gated_slab.shape[0]
    if length > 1024:
        return long_convolve_blocked(gated_slab, filter_slab)
    forward, backward = quarter_tables(length)
    sig = jnp.dot(forward, gated_slab, preferred_element_type=jnp.float32)
    ker = jnp.dot(forward, filter_slab, preferred_element_type=jnp.float32)
    sig_cos, sig_sin, ker_cos, ker_sin = sig[:length], sig[length:], ker[:length], ker[length:]
    prod = jnp.concatenate(
        [sig_cos * ker_cos - sig_sin * ker_sin, sig_cos * ker_sin + sig_sin * ker_cos]
    ).astype(jnp.bfloat16)
    return jnp.dot(backward, prod, preferred_element_type=jnp.float32)


def quarter_tables(length):
    steps = (4 * np.arange(length)[:, None] + 1) * np.arange(length)[None, :] % (4 * length)
    angles = steps * (2.0 * math.pi / (4 * length))
    table = np.concatenate([np.cos(angles), np.sin(angles)])
    return (jnp.asarray(table, jnp.bfloat16), jnp.asarray(table.T / length, jnp.bfloat16))


def make_response(gated_slab, filter_slab, skip_gain):
    long_part = long_convolve(gated_slab, filter_slab)
    return (long_part + skip_gain * gated_slab.astype(jnp.float32)).astype(jnp.bfloat16)


def combine_rows(query_part, response_part):
    return (query_part.astype(jnp.float32) * response_part.astype(jnp.float32)).astype(jnp.bfloat16)


def on_device_large(projected, short_taps, long_filter, skip_gain):
    kernel_size = short_taps.shape[0]
    ctx_size = lax.axis_size("ctx")
    rows = projected[0]
    filter_slab = lax.all_gather(long_filter, "dp", axis=0, tiled=True)
    all_taps = lax.all_gather(short_taps, "ctx", axis=2, tiled=True)
    halo = lax.ppermute(
        rows[-(kernel_size - 1) :], "ctx", [(i, i + 1) for i in range(ctx_size - 1)]
    )
    queries, gated = causal_short(jnp.concatenate([halo, rows]), all_taps, kernel_size)
    gated_slab = lax.all_to_all(gated, "ctx", split_axis=1, concat_axis=0, tiled=True)
    response_slab = make_response(gated_slab, filter_slab, skip_gain)
    response = lax.all_to_all(response_slab, "ctx", split_axis=0, concat_axis=1, tiled=True)
    return combine_rows(queries, response)[None]


CHUNK = 256
MESH = pl.DeviceIdType.MESH
ACROSS, DIAGONAL, SIBLING = 0, 1, 2
CROSS = (ACROSS, DIAGONAL)
TOP = 16


def ctx_offsets(ctx_size):
    pairs = [(a, b) for a in range(1, ctx_size // 2) for b in range(2)]
    return pairs + [(0, 1)]


def ctx_peer(me, offset, ctx_size, sign):
    half = ctx_size // 2
    chip = lax.rem(me // 2 + (half + sign * offset[0]) % half, half)
    core = lax.rem(lax.rem(me, 2) + offset[1], 2)
    return chip * 2 + core


def mixer_kernel(
    ctx_size,
    dp_size,
    x_hbm,
    taps_hbm,
    filter_hbm,
    skip_hbm,
    forward_hbm,
    backward_hbm,
    out_ref,
    x_ref,
    shared_x,
    tail_ref,
    skip_ref,
    forward_ref,
    backward_ref,
    own_taps,
    gate_rows,
    query_rows,
    gate_taps,
    query_taps,
    halo_out,
    halo_in,
    gated_out,
    gated_slab,
    filter_slab,
    spectrum,
    prod_ref,
    response_slab,
    response_in,
    queries,
    local_sem,
    taps_send,
    taps_recv,
    halo_send,
    halo_recv,
    zfil_send,
    zfil_recv,
    yfil_send,
    yfil_recv,
    gated_send,
    gated_recv,
    resp_send,
    resp_recv,
    ready_sem,
    shared_send,
    shared_recv,
):
    kernel_size = taps_hbm.shape[0]
    channels = taps_hbm.shape[2]
    rows = x_ref.shape[1]
    length = rows * ctx_size
    chunks = channels // CHUNK
    fil_rows = filter_hbm.shape[0]
    zsize = dp_size // 2
    turns = list(range(1, zsize))
    me = lax.axis_index("ctx")
    dp = lax.axis_index("dp")
    zpos, ypos = dp // 2, lax.rem(dp, 2)
    chip, core = me // 2, lax.rem(me, 2)
    first = 1 - chip
    offsets = ctx_offsets(ctx_size)
    dests = [ctx_peer(me, o, ctx_size, 1) for o in offsets]
    sources = [ctx_peer(me, o, ctx_size, -1) for o in offsets]
    ypeer = zpos * 2 + (1 - ypos)

    def signal(semaphore, **where):
        pl.semaphore_signal(semaphore, inc=1, device_id=where, device_id_type=MESH)

    barrier = pltpu.get_barrier_semaphore()
    for dest in dests:
        signal(barrier, ctx=dest)
    above = (zpos < zsize - 1).astype(jnp.int32)
    greeted = len(dests) + 1 + above + zpos

    def wait_all(ref, semaphore):
        pltpu.make_async_copy(ref, ref, semaphore).wait()

    def wait_rows(ref, count, semaphore):
        wait_all(ref.at[pl.ds(0, 4), pl.ds(0, count // 4), :], semaphore)

    def by_chip(wait, on_first, on_second):
        for which, count in enumerate((on_first, on_second)):

            @pl.when(chip == which)
            def _(count=count):
                wait(count)

    def local_copy(source, target, index):
        copy = pltpu.make_async_copy(source, target, local_sem.at[index])
        copy.start()
        return copy

    own_taps_copy = local_copy(taps_hbm, own_taps, 0)
    for side in range(2):
        owner = lax.rem(core + side, 2)
        columns = pl.ds(pl.multiple_of(owner * channels, channels), CHUNK)
        local_copy(x_hbm.at[pl.ds(1, 2), :, columns], shared_x.at[side], 4)
    tail_rows = tail_ref.shape[1]
    tail_copy = local_copy(x_hbm.at[:, pl.ds(rows - tail_rows, tail_rows), :], tail_ref, 1)
    gate_copies = [local_copy(x_hbm.at[pl.ds(1, 2)], x_ref.at[pl.ds(1, 2)], 3)]
    signal(barrier, dp=ypeer)
    for turn in turns:

        @pl.when(zpos + turn < zsize)
        def _(turn=turn):
            signal(barrier, dp=dp + 2 * turn)

    @pl.when(zpos > 0)
    def _():
        signal(barrier, dp=dp - 2)


    shared = chunks
    slots = [first + k for k in range(chunks)]

    def filter_block(block, slot):
        return filter_slab.at[slot, pl.ds(pl.multiple_of(block * fil_rows, fil_rows), fil_rows), :]

    def own_filter(slot):
        chunk = lax.rem(slot, chunks)
        return filter_hbm.at[:, pl.ds(pl.multiple_of(chunk * CHUNK, CHUNK), CHUNK)]

    def own_filter_copy(k):
        return pltpu.make_async_copy(
            own_filter(slots[k]), filter_block(dp, slots[k]), local_sem.at[9]
        )

    shared_skip = skip_ref.at[:, pl.ds(channels, CHUNK)]
    first_skip = skip_hbm.at[:, pl.ds(0, CHUNK)]
    shared_skip_copy = pltpu.make_async_copy(first_skip, shared_skip, local_sem.at[8])

    def enter():
        pl.semaphore_wait(barrier, greeted)
        for turn in turns[1:]:

            @pl.when(zpos >= turn)
            def _(turn=turn):
                signal(ready_sem.at[turn - 2], dp=dp - 2 * turn)

    def zfil_copy(turn, slot, source=None):
        target = lax.rem(zpos + turn, zsize)
        return pltpu.make_async_remote_copy(
            src_ref=filter_block(dp, slot) if source is None else source,
            dst_ref=filter_block(dp, slot),
            send_sem=zfil_send,
            recv_sem=zfil_recv.at[turn - 1, slot],
            device_id={"dp": target * 2 + ypos},
            device_id_type=MESH,
        )

    def yfil_copy(turn, slot, source=None):
        origin = lax.rem(zpos + zsize - turn, zsize)
        block = origin * 2 + ypos
        return pltpu.make_async_remote_copy(
            src_ref=filter_block(block, slot) if source is None else source,
            dst_ref=filter_block(block, slot),
            send_sem=yfil_send,
            recv_sem=yfil_recv.at[slot],
            device_id={"dp": ypeer},
            device_id_type=MESH,
        )

    def shared_filter_copy():
        return pltpu.make_async_remote_copy(
            src_ref=own_filter(shared),
            dst_ref=filter_block(dp, shared),
            send_sem=shared_send.at[0],
            recv_sem=shared_recv.at[0],
            device_id={"ctx": dests[ACROSS]},
            device_id_type=MESH,
        )

    def shared_skip_send():
        return pltpu.make_async_remote_copy(
            src_ref=first_skip,
            dst_ref=shared_skip,
            send_sem=shared_send.at[1],
            recv_sem=shared_recv.at[1],
            device_id={"ctx": dests[ACROSS]},
            device_id_type=MESH,
        )

    def relay_filter(slot):
        for order, here in ((turns, zpos > 0), (turns[::-1], zpos == 0)):

            @pl.when(here)
            def _(order=order):
                for turn in order:
                    zfil_copy(turn, slot).wait_recv()
                    yfil_copy(turn, slot).start()

    def send_up(turn, slot):
        @pl.when(zpos + turn < zsize)
        def _():
            zfil_copy(turn, slot, own_filter(slot)).start()

    def send_down(turn, slot):
        @pl.when(zpos + turn >= zsize)
        def _():
            zfil_copy(turn, slot, own_filter(slot)).start()

    def wait_up(turn):
        @pl.when(zpos + turn < zsize)
        def _():
            pl.semaphore_wait(ready_sem.at[turn - 2], 1)

    def send_near_filter(steps):
        for k in steps:
            slot = slots[k]
            for turn in turns:
                send_down(turn, slot)
            yfil_copy(0, slot, own_filter(slot)).start()
            if k < 2:
                send_up(1, slot)

    @pl.when(chip == 1)
    def _():
        enter()
        send_near_filter(range(1))

    halo_copy = pltpu.make_async_remote_copy(
        src_ref=halo_out,
        dst_ref=halo_in,
        send_sem=halo_send,
        recv_sem=halo_recv,
        device_id={"ctx": lax.rem(me + 1, ctx_size)},
        device_id_type=MESH,
    )
    has_following, has_previous = me < ctx_size - 1, me > 0
    tail_copy.wait()

    @pl.when(has_following)
    def _():
        halo_out[...] = tail_ref[:, tail_rows - (kernel_size - 1) :, :]

    own_taps_copy.wait()
    gate_rows[...] = jnp.zeros_like(gate_rows)
    query_rows[...] = jnp.zeros_like(query_rows)
    for tap in range(kernel_size):
        query_rows[tap : tap + 1, :] = own_taps[tap, 0:1, :]
        for gate in range(2):
            row = gate * kernel_size + tap
            gate_rows[row : row + 1, :] = own_taps[tap, 1 + gate : 2 + gate, :]
    gate_taps[me] = gate_rows[...].astype(jnp.bfloat16)
    query_taps[me] = query_rows[...].astype(jnp.bfloat16)

    def short_filter(stream, owner, chunk, values, edged=True):
        columns = pl.ds(pl.multiple_of(owner * channels + chunk * CHUNK, CHUNK), CHUNK)
        taps_columns = pl.ds(pl.multiple_of(chunk * CHUNK, CHUNK), CHUNK)
        values = values.astype(jnp.float32)
        if stream == 0:
            weights = query_taps[owner, :, taps_columns].astype(jnp.float32)
        else:
            weights = gate_taps[owner, :, taps_columns].astype(jnp.float32)
            weights = weights[(stream - 1) * kernel_size : stream * kernel_size]
        if edged:
            edge = halo_in[stream, :, columns].astype(jnp.float32)
            edge = jnp.where(has_previous, edge, jnp.zeros_like(edge))
            row_index = lax.broadcasted_iota(jnp.int32, (8, CHUNK), 0)
        total = weights[0:1] * values
        for tap in range(1, kernel_size):
            moved = pltpu.roll(values, tap, 0)
            if edged:
                top = moved[:8]
                for row in range(tap):
                    at = kernel_size - 1 + row - tap
                    top = jnp.where(row_index == row, edge[at : at + 1], top)
                moved = jnp.concatenate([top, moved[8:]], axis=0)
            total = total + weights[tap : tap + 1] * moved
        return total

    def x_columns(stream, owner, chunk):
        columns = pl.ds(pl.multiple_of(owner * channels + chunk * CHUNK, CHUNK), CHUNK)
        return x_ref[stream, :, columns]

    def gated_rows(owner, chunk):
        keys, values = (
            short_filter(stream, owner, chunk, x_columns(stream, owner, chunk)) for stream in (1, 2)
        )
        return (keys * values).astype(jnp.bfloat16)

    def shared_gated_rows(side, count=rows, edged=True):
        owner = lax.rem(core + side, 2)
        keys, values = (
            short_filter(1 + gate, owner, 0, shared_x[side, gate, :count, :], edged)
            for gate in range(2)
        )
        return (keys * values).astype(jnp.bfloat16)

    def position_rows(owner):
        return pl.ds(pl.multiple_of(owner * rows, rows), rows)

    body_rows = pl.ds(pl.multiple_of(me * rows + TOP, TOP), rows - TOP)
    top_rows = pl.ds(pl.multiple_of(me * rows, rows), TOP)

    wait_all(shared_x, local_sem.at[4])

    @pl.when(chip == 0)
    def _():
        gated_slab[shared, body_rows, :] = shared_gated_rows(0, edged=False)[TOP:]

    def shared_part_copy(part_rows):
        return pltpu.make_async_remote_copy(
            src_ref=gated_slab.at[shared, part_rows, :],
            dst_ref=gated_slab.at[shared, part_rows, :],
            send_sem=gated_send,
            recv_sem=gated_recv.at[shared],
            device_id={"ctx": dests[ACROSS]},
            device_id_type=MESH,
        )

    def shared_body_copy():
        return shared_part_copy(body_rows)

    def shared_top_copy():
        return shared_part_copy(top_rows)

    @pl.when(chip == 0)
    def _():
        enter()

    @pl.when(has_following)
    def _():
        halo_copy.start()

    def taps_copy(i, slot, kind=0):
        taps = (gate_taps, query_taps)[kind]
        return pltpu.make_async_remote_copy(
            src_ref=taps.at[slot],
            dst_ref=taps.at[slot],
            send_sem=taps_send.at[kind],
            recv_sem=taps_recv.at[i if kind == 0 else 3 if i == ACROSS else 4],
            device_id={"ctx": dests[ACROSS] if i == ACROSS else dests[SIBLING]},
            device_id_type=MESH,
        )

    for i in (ACROSS, SIBLING):
        taps_copy(i, me).start()

    def send_query_taps():
        for i in (ACROSS, SIBLING):
            taps_copy(i, me, 1).start()

    @pl.when(chip == 1)
    def _():
        send_query_taps()

    @pl.when(chip == 0)
    def _():
        shared_body_copy().start()
        send_near_filter(range(chunks))

    @pl.when(chip == 1)
    def _():
        send_near_filter(range(1, chunks))

    def gated_copy(i, slot, owner, source=None):
        return pltpu.make_async_remote_copy(
            src_ref=gated_out.at[i, slot] if source is None else source,
            dst_ref=gated_slab.at[slot, position_rows(owner), :],
            send_sem=gated_send,
            recv_sem=gated_recv.at[slot],
            device_id={"ctx": dests[i]},
            device_id_type=MESH,
        )

    def response_copy(i, slot):
        return pltpu.make_async_remote_copy(
            src_ref=response_slab.at[slot, position_rows(dests[i]), :],
            dst_ref=response_in.at[i, slot],
            send_sem=resp_send,
            recv_sem=resp_recv.at[slot if i in CROSS else shared],
            device_id={"ctx": dests[i]},
            device_id_type=MESH,
        )

    def push_gated(i, chunk):
        gated_out[i, chunk] = gated_rows(dests[i], chunk)
        gated_copy(i, chunk, me).start()

    def push_near(chunk):
        push_gated(SIBLING, chunk)
        gated_slab[chunk, position_rows(me), :] = gated_rows(me, chunk)

    def shared_own():
        gated_slab[shared, position_rows(me), :] = shared_gated_rows(0)

    def shared_other():
        gated_out[SIBLING, shared] = shared_gated_rows(1)
        gated_copy(SIBLING, shared, me).start()

    taps_copy(SIBLING, sources[SIBLING]).wait_recv()

    @pl.when(jnp.logical_and(chip == 0, has_previous))
    def _():
        halo_copy.wait_recv()

    @pl.when(chip == 0)
    def _():
        gated_slab[shared, top_rows, :] = shared_gated_rows(0, TOP)
        shared_top_copy().start()
        shared_other()
        gated_copy(DIAGONAL, shared, me, gated_out.at[SIBLING, shared]).start()
        send_query_taps()
        shared_filter_copy().start()
        shared_skip_send().start()
        shared_skip_copy.start()
        half = length // 2
        gated_slab[shared, half:] = jnp.zeros((length - half, CHUNK), jnp.bfloat16)

    for k in range(chunks):
        own_filter_copy(k).start()
    late_copies = [
        local_copy(x_hbm.at[0], x_ref.at[0], 2),
        local_copy(forward_hbm, forward_ref, 6),
        local_copy(backward_hbm, backward_ref, 7),
        local_copy(skip_hbm, skip_ref.at[:, pl.ds(0, channels)], 5),
    ]

    def send_far_up():
        for turn in turns[1:]:
            wait_up(turn)
        for k, slot in enumerate(slots):
            for turn in reversed(turns):
                if turn > 1 or k > 1:
                    send_up(turn, slot)

    @pl.when(chip == 1)
    def _():
        send_far_up()

    for copy in gate_copies:
        copy.wait()
    taps_copy(ACROSS, sources[ACROSS]).wait_recv()
    taps_copy(DIAGONAL, sources[ACROSS]).start()

    @pl.when(chip == 1)
    def _():
        halo_copy.wait_recv()

    push_gated(ACROSS, chip)
    taps_copy(DIAGONAL, sources[DIAGONAL]).wait_recv()
    push_gated(DIAGONAL, chip)

    @pl.when(jnp.logical_and(chip == 0, zpos > 0))
    def _():
        send_far_up()

    push_near(first)
    def push_chunk(step, carry):
        @pl.when(chip + step < chunks)
        def _():
            push_gated(ACROSS, chip + step)
            push_gated(DIAGONAL, chip + step)

        @pl.when(first + step < chunks)
        def _():
            push_near(first + step)

        return carry

    lax.fori_loop(1, 2, push_chunk, 0)

    @pl.when(jnp.logical_and(chip == 0, zpos == 0))
    def _():
        send_far_up()

    taps_copy(ACROSS, sources[ACROSS], 1).wait_recv()
    taps_copy(DIAGONAL, sources[ACROSS], 1).start()
    lax.fori_loop(2, 3, push_chunk, 0)
    relay_filter(first)
    lax.fori_loop(3, chunks, push_chunk, 0)

    @pl.when(chip == 1)
    def _():
        shared_own()
        shared_other()

    for copy in late_copies:
        copy.wait()
    wait_all(filter_slab.at[shared, pl.ds(0, chunks * fil_rows), :], local_sem.at[9])

    @pl.when(chip == 0)
    def _():
        shared_skip_copy.wait()

    def fill_queries(chunk, carry):
        def one_owner(owner, inner):
            queries[owner, chunk] = short_filter(0, owner, chunk, x_columns(0, owner, chunk)).astype(
                jnp.bfloat16
            )
            return inner

        return lax.fori_loop(0, ctx_size, one_owner, carry)

    @pl.when(chip == 1)
    def _():
        shared_filter_copy().wait_recv()
        shared_skip_send().wait_recv()
        yfil_copy(0, shared).start()
        for turn in turns:
            zfil_copy(turn, shared).start()

    wait_all(query_taps.at[pl.ds(0, 2)], taps_recv.at[4])
    lax.fori_loop(0, chunks, fill_queries, 0)
    relay_filter(first + 1)

    def mix_into(owner, chunk, response):
        columns = pl.ds(pl.multiple_of(owner * channels + chunk * CHUNK, CHUNK), CHUNK)
        mixed = queries[owner, chunk].astype(jnp.float32) * response.astype(jnp.float32)
        out_ref[:, columns] = mixed.astype(jnp.bfloat16)

    def convolve(slot, carry):
        columns = pl.ds(pl.multiple_of(slot * CHUNK, CHUNK), CHUNK)

        from_all = jnp.logical_or(slot < shared, chip == 1)

        @pl.when(from_all)
        def _():
            wait_all(gated_slab.at[slot, pl.ds(0, 3 * rows), :], gated_recv.at[slot])

        @pl.when(jnp.logical_not(from_all))
        def _():
            wait_all(gated_slab.at[slot, pl.ds(0, rows), :], gated_recv.at[slot])

        gated = gated_slab[slot]
        spectrum[...] = jnp.dot(forward_ref[...], gated, preferred_element_type=jnp.float32)
        wait_all(filter_slab.at[slot, pl.ds(0, zsize * fil_rows), :], yfil_recv.at[slot])
        taps = filter_slab[slot]
        ker_cos = jnp.dot(forward_ref[:length], taps, preferred_element_type=jnp.float32)
        ker_sin = jnp.dot(forward_ref[length:], taps, preferred_element_type=jnp.float32)
        sig_cos, sig_sin = spectrum[:length], spectrum[length:]
        prod_ref[:length] = (sig_cos * ker_cos - sig_sin * ker_sin).astype(jnp.bfloat16)
        prod_ref[length:] = (sig_cos * ker_sin + sig_sin * ker_cos).astype(jnp.bfloat16)
        long_part = jnp.dot(backward_ref[...], prod_ref[...], preferred_element_type=jnp.float32)
        direct_part = skip_ref[:, columns] * gated.astype(jnp.float32)
        response_slab[slot] = (long_part + direct_part).astype(jnp.bfloat16)

        @pl.when(slot < shared)
        def _():
            for i in CROSS:
                response_copy(i, slot).start()

        response_copy(SIBLING, slot).start()

        @pl.when(slot + 2 <= shared)
        def _():
            relay_filter(slot + 2)

        response = response_slab[slot, position_rows(me), :]

        @pl.when(slot < shared)
        def _():
            mix_into(me, slot, response)

        @pl.when(slot == shared)
        def _():
            mix_into(core, 0, response)

        return carry

    lax.fori_loop(first, shared + 1, convolve, 0)

    def wait_near(count):
        wait_rows(gated_slab, count * rows, resp_recv.at[shared])

    def finish_near(chunk, carry):
        mix_into(sources[SIBLING], chunk, response_in[SIBLING, chunk])
        return carry

    def finish_cross(chunk, carry):
        wait_all(response_in.at[pl.ds(0, len(CROSS)), chunk], resp_recv.at[chunk])
        for i in CROSS:
            mix_into(sources[i], chunk, response_in[i, chunk])
        return carry

    by_chip(wait_near, chunks, chunks + 1)
    lax.fori_loop(first, chunks, finish_near, 0)
    mix_into(1 - core, 0, response_in[SIBLING, shared])
    lax.fori_loop(chip, chunks, finish_cross, 0)

    def drain_gated(count):
        wait_rows(gated_slab, count * rows, gated_send)

    def drain_response(count):
        wait_rows(gated_slab, count * rows, resp_send)

    def drain_filter(count):
        wait_rows(filter_slab, count * len(turns) * fil_rows, zfil_send)
        wait_rows(filter_slab, count * zsize * fil_rows, yfil_send)

    by_chip(drain_gated, 3 * chunks + 2, 3 * chunks - 1)
    by_chip(drain_filter, chunks, chunks + 1)
    by_chip(drain_response, 3 * chunks - 2, 3 * chunks + 1)

    @pl.when(chip == 0)
    def _():
        shared_filter_copy().wait_send()
        shared_skip_send().wait_send()

    wait_all(gate_taps.at[pl.ds(0, 3)], taps_send.at[0])
    wait_all(query_taps.at[pl.ds(0, 3)], taps_send.at[1])

    @pl.when(has_following)
    def _():
        halo_copy.wait_send()


def write_kernel(mixed_ref, out_hbm, sem):
    copy = pltpu.make_async_copy(mixed_ref, out_hbm, sem)
    copy.start()
    copy.wait()


def write_out(mixed):
    return pl.pallas_call(
        write_kernel,
        out_shape=jax.ShapeDtypeStruct(mixed.shape, mixed.dtype),
        in_specs=[pl.BlockSpec(memory_space=pltpu.VMEM)],
        out_specs=pl.BlockSpec(memory_space=pltpu.HBM),
        scratch_shapes=[pltpu.SemaphoreType.DMA],
    )(pltpu.with_memory_space_constraint(mixed, pltpu.VMEM))


def on_device(projected, short_taps, long_filter, skip_gain):
    ctx_size, dp_size = lax.axis_size("ctx"), lax.axis_size("dp")
    kernel_size, streams, channels = short_taps.shape
    rows, width = projected.shape[1], projected.shape[3]
    length = rows * ctx_size
    regular = ctx_size == 4 and dp_size % 2 == 0 and dp_size >= 6
    regular = regular and channels % CHUNK == 0 and channels >= 2 * CHUNK and kernel_size <= 4
    regular = regular and channels == 4 * CHUNK
    if length > 1024 or not regular:
        return on_device_large(projected, short_taps, long_filter, skip_gain)
    forward, backward = quarter_tables(length)
    chunks = channels // CHUNK
    slots = chunks + 1
    peers = ctx_size - 1
    zsize = dp_size // 2
    hbm_spec = pl.BlockSpec(memory_space=pltpu.HBM)
    dma = pltpu.SemaphoreType.DMA
    operands = (
        projected[0].transpose(1, 0, 2),
        short_taps,
        long_filter,
        skip_gain[None],
        forward,
        backward,
    )
    mixed = pl.pallas_call(
        functools.partial(mixer_kernel, ctx_size, dp_size),
        out_shape=pltpu.VMEM((rows, width), jnp.bfloat16),
        in_specs=[hbm_spec] * len(operands),
        out_specs=pl.BlockSpec(memory_space=pltpu.VMEM),
        scratch_shapes=[
            pltpu.VMEM((streams, rows, width), jnp.bfloat16),
            pltpu.VMEM((2, 2, rows, CHUNK), jnp.bfloat16),
            pltpu.VMEM((streams, 16, width), jnp.bfloat16),
            pltpu.VMEM((1, channels + CHUNK), jnp.float32),
            pltpu.VMEM(forward.shape, jnp.bfloat16),
            pltpu.VMEM(backward.shape, jnp.bfloat16),
            pltpu.VMEM((kernel_size, streams, channels), jnp.float32),
            pltpu.VMEM((8, channels), jnp.float32),
            pltpu.VMEM((4, channels), jnp.float32),
            pltpu.VMEM((ctx_size, 8, channels), jnp.bfloat16),
            pltpu.VMEM((ctx_size, 4, channels), jnp.bfloat16),
            pltpu.VMEM((streams, kernel_size - 1, width), jnp.bfloat16),
            pltpu.VMEM((streams, kernel_size - 1, width), jnp.bfloat16),
            pltpu.VMEM((peers, slots, rows, CHUNK), jnp.bfloat16),
            pltpu.VMEM((slots, length, CHUNK), jnp.bfloat16),
            pltpu.VMEM((slots, length, CHUNK), jnp.bfloat16),
            pltpu.VMEM((2 * length, CHUNK), jnp.float32),
            pltpu.VMEM((2 * length, CHUNK), jnp.bfloat16),
            pltpu.VMEM((slots, length, CHUNK), jnp.bfloat16),
            pltpu.VMEM((peers, slots, rows, CHUNK), jnp.bfloat16),
            pltpu.VMEM((ctx_size, chunks, rows, CHUNK), jnp.bfloat16),
            dma((10,)),
            dma((2,)),
            dma((5,)),
            dma,
            dma,
            dma,
            dma((zsize - 1, slots)),
            dma,
            dma((slots,)),
            dma,
            dma((slots,)),
            dma,
            dma((slots,)),
            pltpu.SemaphoreType.REGULAR((zsize - 2,)),
            dma((2,)),
            dma((2,)),
        ],
        compiler_params=pltpu.CompilerParams(
            collective_id=0, has_side_effects=True, vmem_limit_bytes=40 * 2**20
        ),
    )(*(pltpu.with_memory_space_constraint(array, pltpu.HBM) for array in operands))
    return write_out(mixed)[None]


def solution(mesh):
    return jax.shard_map(
        on_device,
        mesh=mesh,
        in_specs=(P("dp", "ctx", None, None), P(None, None, "ctx"), P("dp", "ctx"), P("ctx")),
        out_specs=P("dp", "ctx", None),
        check_vma=False,
    )
```
